128 devices in a mesh: xd: 8 (over z, y_lo), ta: 16 (over x, y_hi, core).
Axes of the slice: x: 4, y: 4 (y_hi: 2, y_lo: 2; y = y_hi * 2 + y_lo), z: 4, core: 2. Of those that a mesh axis runs over, the one named last changes fastest.
Arguments:
- gauge_links: float32 [4, 2, 3, 3, 32, 16, 4, 128], P(None, None, None, None, 'xd', 'ta'), may hold values from -1 to 1, as said below
- momenta: float32 [4, 2, 3, 3, 32, 16, 4, 128], P(None, None, None, None, 'xd', 'ta'), as said below
- noise_table: float32 [2, 4, 3, 4096], replicated, may hold values from -6 to 6
- noise_index: int32 [32, 16, 4, 128], P('xd', 'ta'), may hold values from 0 to 4095
- partner: int32 [32], P('xd'), may hold values from 0 to 31, as said below
Outputs:
- new_links: float32 [4, 2, 3, 3, 32, 16, 4, 128], P(None, None, None, None, 'xd', 'ta')
- new_momenta: float32 [4, 2, 3, 3, 32, 16, 4, 128], P(None, None, None, None, 'xd', 'ta')
The draws below stay inside these ranges and needn't reach their ends.
Inputs may be any that keep to these rules, and one draw needn't show every extreme that they name: partner is an involution without fixed points: each row x1 is paired with a row of the aligned block of 4 rows that lies 32 / 2 rows away, and partner[partner[x1]] = x1. Every gauge_links[mu] at every site is a special unitary 3 x 3 matrix. Every momenta[mu] at every site is a Hermitian traceless 3 x 3 matrix.
All inputs are finite; a program needn't handle non-finite values.
Results may differ from the reference program's by a relative error of at most 0.0001.
Values sent between devices are 32-bit elements; how exact they have to be, the bound alone decides.
No kernel may reach another device: no remote copies, remote signals or barrier semaphores. Data moves between devices by JAX's collectives and lax.ppermute only.
A program may use at most 128 MiB of HBM per device.

```python
import jax
import jax.numpy as jnp

X1L = 4
N2 = 4
N3 = 128
MD_STEPS = 2
DEGREE = 6
NOISE = 4096
NX1 = 32
NT = 16


def complex_times(left_real, left_imag, right_real, right_imag):
    return (left_real * right_real - left_imag * right_imag, left_real * right_imag + left_imag * right_real)


def draw_gauge_links(key, part):
    key_real, key_imag = jax.random.split(key, 2)
    full_shape = (4, 3, 3, NX1, NT, N2, N3)
    base_real = jax.random.normal(key_real, full_shape, jnp.float32)
    base_imag = jax.random.normal(key_imag, full_shape, jnp.float32)
    first_real = base_real[:, 0]
    first_imag = base_imag[:, 0]
    length_first = jnp.sqrt(jnp.sum(first_real * first_real + first_imag * first_imag, axis=1, keepdims=True)) + 1e-06
    first_real = first_real / length_first
    first_imag = first_imag / length_first
    second_real = base_real[:, 1]
    second_imag = base_imag[:, 1]
    inner_real = jnp.sum(first_real * second_real + first_imag * second_imag, axis=1, keepdims=True)
    inner_imag = jnp.sum(first_real * second_imag - first_imag * second_real, axis=1, keepdims=True)
    proj_real, proj_imag = complex_times(inner_real, inner_imag, first_real, first_imag)
    second_real = second_real - proj_real
    second_imag = second_imag - proj_imag
    length_second = jnp.sqrt(jnp.sum(second_real * second_real + second_imag * second_imag, axis=1, keepdims=True)) + 1e-06
    second_real = second_real / length_second
    second_imag = second_imag / length_second
    third_real = []
    third_imag = []
    for colour in range(3):
        next_one = (colour + 1) % 3
        next_two = (colour + 2) % 3
        prod_real, prod_imag = complex_times(first_real[:, next_one], first_imag[:, next_one], second_real[:, next_two], second_imag[:, next_two])
        back_real, back_imag = complex_times(first_real[:, next_two], first_imag[:, next_two], second_real[:, next_one], second_imag[:, next_one])
        third_real.append(prod_real - back_real)
        third_imag.append(-(prod_imag - back_imag))
    whole_real = jnp.stack([first_real, second_real, jnp.stack(third_real, axis=1)], axis=1)
    whole_imag = jnp.stack([first_imag, second_imag, jnp.stack(third_imag, axis=1)], axis=1)
    return jnp.stack([whole_real, whole_imag], axis=1)


def draw_momenta(key, part):
    key_real, key_imag = jax.random.split(jax.random.fold_in(key, 7), 2)
    full_shape = (4, 3, 3, NX1, NT, N2, N3)
    base_real = jax.random.normal(key_real, full_shape, jnp.float32)
    base_imag = jax.random.normal(key_imag, full_shape, jnp.float32)
    herm_real = (base_real + jnp.swapaxes(base_real, 1, 2)) * 0.5
    herm_imag = (base_imag - jnp.swapaxes(base_imag, 1, 2)) * 0.5
    trace_third = (herm_real[:, 0, 0] + herm_real[:, 1, 1] + herm_real[:, 2, 2]) / 3.0
    identity = jnp.eye(3, dtype=jnp.float32)[None, :, :, None, None, None, None]
    herm_real = herm_real - identity * trace_third[:, None, None]
    return jnp.stack([herm_real, herm_imag], axis=1)


def one_shuffle(one_key):
    return jax.random.permutation(one_key, X1L)


def draw_partner(key, part):
    block_count = NX1 // X1L
    half_count = block_count // 2
    keys_list = jax.random.split(jax.random.fold_in(key, 11), half_count)
    shuffles = jax.vmap(one_shuffle)(keys_list).astype(jnp.int32)
    inverse = jnp.argsort(shuffles, axis=1, stable=True).astype(jnp.int32)
    block_start = jnp.arange(half_count, dtype=jnp.int32)[:, None] * X1L
    lower_half = block_start + half_count * X1L + shuffles
    upper_half = block_start + inverse
    return jnp.concatenate([lower_half.reshape(-1), upper_half.reshape(-1)]).astype(jnp.int32)


def with_ends(drawn, rng, smallest, largest):
    dims = drawn.shape
    index_at = [jax.random.randint(jax.random.fold_in(rng, axis), (), 0, dims[axis]) for axis in range(len(dims))]
    drawn = drawn.at[tuple(index_at)].set(smallest)
    longest = dims.index(max(dims))
    index_at[longest] = (index_at[longest] + 1) % dims[longest]
    return drawn.at[tuple(index_at)].set(largest)


def noise(key, extent, spread, bound, kind=jnp.bfloat16):
    values = jax.random.normal(key, extent, jnp.float32) * spread
    return jnp.minimum(jnp.maximum(values, -bound), bound).astype(kind)


def setup_inputs(seed: int = 0) -> dict:
    streams_of = jax.random.split(jax.random.key(seed), 6)
    gauge_links = draw_gauge_links(jax.random.fold_in(streams_of[5], 71), 0)
    momenta = draw_momenta(jax.random.fold_in(streams_of[5], 71), 0)
    noise_table = noise(streams_of[2], (2, 4, 3, NOISE), 1.0, 6.0, jnp.float32)
    noise_index = with_ends(jax.random.randint(streams_of[3], (NX1, NT, N2, N3), 0, NOISE), jax.random.fold_in(streams_of[3], 1), 0, NOISE - 1).astype(jnp.int32)
    partner = draw_partner(jax.random.fold_in(streams_of[5], 71), 0)
    return {"gauge_links": gauge_links, "momenta": momenta, "noise_table": noise_table, "noise_index": noise_index, "partner": partner}


hopping = 0.13
step_size = 0.25

gamma_table = (
    ((3, 2, 1, 0), (0, 0, 0, 0), (1, 1, -1, -1)),
    ((2, 3, 0, 1), (1, 1, 1, 1), (0, 0, 0, 0)),
    ((3, 2, 1, 0), (-1, 1, 1, -1), (0, 0, 0, 0)),
    ((2, 3, 0, 1), (0, 0, 0, 0), (1, -1, -1, 1)),
)


def spin_apply(spinor, direction, sign_factor):
    source_order, real_part, imag_part = gamma_table[direction]
    rows_real = []
    rows_imag = []
    for spin_row in range(4):
        source = source_order[spin_row]
        add_real = spinor[0, source] * (sign_factor * real_part[spin_row]) - spinor[1, source] * (sign_factor * imag_part[spin_row])
        add_imag = spinor[1, source] * (sign_factor * real_part[spin_row]) + spinor[0, source] * (sign_factor * imag_part[spin_row])
        rows_real.append(spinor[0, spin_row] + add_real)
        rows_imag.append(spinor[1, spin_row] + add_imag)
    return jnp.stack([jnp.stack(rows_real), jnp.stack(rows_imag)])


def mat_vec(matrix, spinor):
    mat_real = matrix[0][None]
    mat_imag = matrix[1][None]
    vec_real = spinor[0][:, None]
    vec_imag = spinor[1][:, None]
    out_real = jnp.sum(mat_real * vec_real - mat_imag * vec_imag, axis=2)
    out_imag = jnp.sum(mat_real * vec_imag + mat_imag * vec_real, axis=2)
    return jnp.stack([out_real, out_imag])


def dagger(matrix):
    return jnp.stack([jnp.swapaxes(matrix[0], 0, 1), -jnp.swapaxes(matrix[1], 0, 1)])


def mat_mat(left_mat, right_mat):
    left_real = left_mat[0][:, :, None]
    left_imag = left_mat[1][:, :, None]
    right_real = right_mat[0][None]
    right_imag = right_mat[1][None]
    return jnp.stack([jnp.sum(left_real * right_real - left_imag * right_imag, axis=1),
                      jnp.sum(left_real * right_imag + left_imag * right_real, axis=1)])


def outer_sum(first_spin, second_spin):
    first_real = first_spin[0][:, :, None]
    first_imag = first_spin[1][:, :, None]
    second_real = second_spin[0][:, None]
    second_imag = second_spin[1][:, None]
    return jnp.stack([jnp.sum(first_real * second_real + first_imag * second_imag, axis=0),
                      jnp.sum(first_imag * second_real - first_real * second_imag, axis=0)])


def hermitian_part(matrix):
    swap_real = jnp.swapaxes(matrix[0], 0, 1)
    swap_imag = jnp.swapaxes(matrix[1], 0, 1)
    part_real = (matrix[1] + swap_imag) * 0.5
    part_imag = (swap_real - matrix[0]) * 0.5
    trace_third = (matrix[1][0, 0] + matrix[1][1, 1] + matrix[1][2, 2]) / 3.0
    identity = jnp.eye(3, dtype=jnp.float32).reshape((3, 3) + (1,) * (matrix.ndim - 3))
    return jnp.stack([part_real - identity * trace_third, part_imag])


def step_up(spinor, direction, partner):
    if direction == 0:
        return jnp.roll(spinor, -1, axis=-4)
    if direction == 1:
        time_index = jnp.arange(spinor.shape[-3])
        flip_sign = jnp.where(time_index == spinor.shape[-3] - 1, -1.0, 1.0).astype(jnp.float32)
        return jnp.roll(spinor, -1, axis=-3) * flip_sign[:, None, None]
    if direction == 2:
        wrapped = jnp.take(spinor[..., :1, :], partner, axis=-4)
        return jnp.concatenate([spinor[..., 1:, :], wrapped], axis=-2)
    return jnp.roll(spinor, -1, axis=-1)


def step_down(spinor, direction, partner):
    if direction == 0:
        return jnp.roll(spinor, 1, axis=-4)
    if direction == 1:
        time_index = jnp.arange(spinor.shape[-3])
        flip_sign = jnp.where(time_index == 0, -1.0, 1.0).astype(jnp.float32)
        return jnp.roll(spinor, 1, axis=-3) * flip_sign[:, None, None]
    if direction == 2:
        wrapped = jnp.take(spinor[..., -1:, :], partner, axis=-4)
        return jnp.concatenate([wrapped, spinor[..., :-1, :]], axis=-2)
    return jnp.roll(spinor, 1, axis=-1)


def dirac_dag(gauge_links, spinor, partner):
    hop_sum = None
    for direction in range(4):
        ahead = mat_vec(gauge_links[direction], step_up(spinor, direction, partner))
        behind = step_down(mat_vec(dagger(gauge_links[direction]), spinor), direction, partner)
        hop_term = spin_apply(ahead, direction, 1) + spin_apply(behind, direction, -1)
        hop_sum = hop_term if direction == 0 else hop_sum + hop_term
    return spinor - hopping * hop_sum


def force_term(gauge_links, phi, response, partner):
    forces = []
    for direction in range(4):
        ahead_field = spin_apply(step_up(response, direction, partner), direction, -1)
        local_field = spin_apply(response, direction, 1)
        bracket = outer_sum(ahead_field, phi) + outer_sum(step_up(phi, direction, partner), local_field)
        forces.append(hermitian_part(mat_mat(gauge_links[direction], bracket)) * (-2.0 * hopping))
    return jnp.stack(forces)


def link_update(momenta, gauge_links):
    identity = jnp.stack([jnp.eye(3, dtype=jnp.float32), jnp.zeros((3, 3), jnp.float32)]).reshape(2, 3, 3, 1, 1, 1, 1)
    updated = []
    for direction in range(4):
        generator = jnp.stack([-step_size * momenta[direction, 1], step_size * momenta[direction, 0]])
        series = identity
        for term_index in range(DEGREE, 0, -1):
            series = identity + mat_mat(generator, series) / float(term_index)
        updated.append(mat_mat(series, gauge_links[direction]))
    return jnp.stack(updated)


def reference(gauge_links, momenta, noise_table, noise_index, partner):
    noise_field = jnp.take(noise_table, noise_index, axis=3)
    phi = dirac_dag(gauge_links, noise_field, partner)
    for step_number in range(MD_STEPS):
        response = dirac_dag(gauge_links, phi, partner)
        forces = force_term(gauge_links, phi, response, partner)
        mirrored = jnp.take(forces, partner, axis=-4)
        total_force = jnp.stack([forces[:, 0] - mirrored[:, 0], forces[:, 1] + mirrored[:, 1]], axis=1)
        momenta = momenta + step_size * total_force
        gauge_links = link_update(momenta, gauge_links)
    return gauge_links, momenta
```

```python
import jax
import jax.numpy as jnp
from jax import lax
from jax.experimental import pallas as pl
from jax.experimental.pallas import tpu as pltpu
from jax.sharding import PartitionSpec as P

HOPPING = 0.13
STEP = 0.25
DEGREE = 6
F32 = jnp.float32
GAMMA = (
    ((3, 2, 1, 0), ((0, 1), (0, 1), (0, -1), (0, -1))),
    ((2, 3, 0, 1), ((1, 0), (1, 0), (1, 0), (1, 0))),
    ((3, 2, 1, 0), ((-1, 0), (1, 0), (1, 0), (-1, 0))),
    ((2, 3, 0, 1), ((0, 1), (0, -1), (0, -1), (0, 1))),
)
ROWS = 16
HALO = 24


def ld(ref, k, h):
    return ref[k * ROWS + 8 * h : k * ROWS + 8 * h + 8, :]


def st(ref, k, h, value):
    ref[k * ROWS + 8 * h : k * ROWS + 8 * h + 8, :] = value


def cadd(a, b):
    return (a[0] + b[0], a[1] + b[1])


def csub(a, b):
    return (a[0] - b[0], a[1] - b[1])


def cmul(a, b):
    return (a[0] * b[0] - a[1] * b[1], a[0] * b[1] + a[1] * b[0])


def cmul_conj(a, b):
    return (a[0] * b[0] + a[1] * b[1], a[1] * b[0] - a[0] * b[1])


def add_unit(x, y, coef, sign):
    re, im = coef
    if re:
        if re * sign > 0:
            return cadd(x, y)
        return csub(x, y)
    if im * sign > 0:
        return (x[0] - y[1], x[1] + y[0])
    return (x[0] + y[1], x[1] - y[0])


def spinor(ref, h):
    return [[(ld(ref, c * 4 + s, h), ld(ref, 12 + c * 4 + s, h)) for c in range(3)] for s in range(4)]


def project(psi, mu, sign):
    source, coef = GAMMA[mu]
    return [[add_unit(psi[t][c], psi[source[t]][c], coef[t], sign) for c in range(3)] for t in range(2)]


def matrix(ref, mu, h):
    return [[(ld(ref, mu * 18 + i * 3 + j, h), ld(ref, mu * 18 + 9 + i * 3 + j, h)) for j in range(3)] for i in range(3)]


def mat_half(u, v):
    out = []
    for t in range(2):
        row = []
        for i in range(3):
            acc = cmul(u[i][0], v[t][0])
            for j in (1, 2):
                acc = cadd(acc, cmul(u[i][j], v[t][j]))
            row.append(acc)
        out.append(row)
    return out


def mat_dag_half(u, v):
    out = []
    for t in range(2):
        row = []
        for i in range(3):
            acc = cmul_conj(v[t][0], u[0][i])
            for j in (1, 2):
                acc = cadd(acc, cmul_conj(v[t][j], u[j][i]))
            row.append(acc)
        out.append(row)
    return out


def half_index(part, t, c):
    return part * 6 + t * 3 + c


def put_half(ref, h, v, base=0):
    for t in range(2):
        for c in range(3):
            for part in range(2):
                st(ref, base + half_index(part, t, c), h, v[t][c][part])


def get_half(fn):
    return [[tuple(fn(half_index(part, t, c)) for part in range(2)) for c in range(3)] for t in range(2)]


def map_half(fn, *vs):
    return [[tuple(fn(*(v[t][c][part] for v in vs)) for part in range(2)) for c in range(3)] for t in range(2)]


class Info:
    def __init__(self, table, partner):
        self.even_t = table[0] == 0
        self.even_x = table[1] == 0
        self.sign_ahead = table[2].astype(F32)
        self.sign_behind = table[3].astype(F32)
        self.partner = [partner[j] & 3 for j in range(4)]


def row_in_pair():
    return lax.broadcasted_iota(jnp.int32, (8, 128), 0) & 3


def send_rows(dst, base, src, k, info, row):
    for j in range(4):
        dst[pl.ds(base * 4 + info.partner[j], 1), :] = src[k * ROWS + 4 * j + row : k * ROWS + 4 * j + row + 1, :]


def send_both(psi_ref, u_ref, info, t_a, t_b, x_a, x_b, mirror, q0, q2, q3, h0, h2):
    for h in range(2):
        psi = spinor(psi_ref, h)
        front = map_half(lambda a: a * info.sign_ahead, project(psi, 1, 1))
        back = map_half(
            lambda a: a * info.sign_behind, mat_dag_half(matrix(u_ref, 1, h), project(psi, 1, -1))
        )
        put_half(t_a, h, map_half(lambda a, b: jnp.where(info.even_t, b, a), front, back))
        put_half(t_b, h, map_half(lambda a, b: jnp.where(info.even_t, a, b), front, back))
        put_half(h0, h, project(psi, 0, 1))
        put_half(h2, h, project(psi, 2, 1))
        for mu, ref in ((0, q0), (2, q2), (3, q3)):
            put_half(ref, h, mat_dag_half(matrix(u_ref, mu, h), project(psi, mu, -1)))
    for k in range(12):
        front = h0[k * ROWS : k * ROWS + 4, :]
        back = q0[k * ROWS + 12 : k * ROWS + 16, :]
        x_a[k * 4 : k * 4 + 4, :] = jnp.where(info.even_x, back, front)
        x_b[k * 4 : k * 4 + 4, :] = jnp.where(info.even_x, front, back)
        send_rows(mirror, k, h2, k, info, 0)
        send_rows(mirror, 12 + k, q2, k, info, 3)


def dirac(psi_ref, u_ref, arrived, q0, q2, q3, scratch, out_ref, w_ref):
    ahead_t, behind_t, ahead_x, behind_x, ahead_m, behind_m = arrived
    a0, b0, fa, fb = scratch
    for k in range(12):
        a0[k * HALO + 16 : k * HALO + 20, :] = ahead_x(k)
        b0[k * HALO : k * HALO + 4, :] = behind_x(k)
        b0[k * HALO + 4 : k * HALO + 20, :] = q0[k * ROWS : k * ROWS + 16, :]
        fa[pl.ds(k * ROWS + 3, 4, stride=4), :] = ahead_m(k)
        fb[pl.ds(k * ROWS, 4, stride=4), :] = behind_m(k)
    for h in range(2):
        v = project(spinor(psi_ref, h), 0, 1)
        for t in range(2):
            for c in range(3):
                for part in range(2):
                    k = half_index(part, t, c)
                    a0[k * HALO + 8 * h : k * HALO + 8 * h + 8, :] = v[t][c][part]
    x2 = row_in_pair()
    for h in range(2):
        psi = spinor(psi_ref, h)
        acc = None
        for mu in range(4):
            if mu == 0:
                ahead = get_half(lambda k: a0[k * HALO + 8 * h + 4 : k * HALO + 8 * h + 12, :])
                behind = get_half(lambda k: b0[k * HALO + 8 * h : k * HALO + 8 * h + 8, :])
            elif mu == 1:
                ahead = get_half(lambda k: ahead_t(k, h))
                behind = get_half(lambda k: behind_t(k, h))
            elif mu == 2:
                raw = project(psi, 2, 1)
                face = get_half(lambda k: ld(fa, k, h))
                ahead = map_half(lambda r, f: jnp.where(x2 == 3, f, pltpu.roll(r, 7, 0)), raw, face)
                behind = get_half(lambda k: jnp.where(x2 == 0, ld(fb, k, h), pltpu.roll(ld(q2, k, h), 1, 0)))
            else:
                ahead = map_half(lambda r: pltpu.roll(r, 127, 1), project(psi, 3, 1))
                behind = get_half(lambda k: pltpu.roll(ld(q3, k, h), 1, 1))
            w = mat_half(matrix(u_ref, mu, h), ahead)
            if w_ref is not None:
                put_half(w_ref, h, w, mu * 12)
            total = map_half(lambda a, b: a + b, w, behind)
            delta = map_half(lambda a, b: a - b, w, behind)
            source, coef = GAMMA[mu]
            if acc is None:
                zero = jnp.zeros((8, 128), F32)
                acc = [total[0], total[1]] + [
                    [add_unit((zero, zero), delta[source[s]][c], coef[s], 1) for c in range(3)] for s in (2, 3)
                ]
            else:
                for s in range(2):
                    acc[s] = [cadd(acc[s][c], total[s][c]) for c in range(3)]
                for s in (2, 3):
                    acc[s] = [add_unit(acc[s][c], delta[source[s]][c], coef[s], 1) for c in range(3)]
        for s in range(4):
            for c in range(3):
                for part in range(2):
                    st(out_ref, part * 12 + c * 4 + s, h, psi[s][c][part] - HOPPING * acc[s][c][part])


def arrived_swap(info, t_a, t_b, x_a, x_b, mirror):
    def rows(ref, k):
        return ref[k * 4 : k * 4 + 4, :]

    return (
        lambda k, h: jnp.where(info.even_t, ld(t_a, k, h), ld(t_b, k, h)),
        lambda k, h: jnp.where(info.even_t, ld(t_b, k, h), ld(t_a, k, h)),
        lambda k: jnp.where(info.even_x, rows(x_a, k), rows(x_b, k)),
        lambda k: jnp.where(info.even_x, rows(x_b, k), rows(x_a, k)),
        lambda k: rows(mirror, k),
        lambda k: rows(mirror, 12 + k),
    )


def noise_kernel(table_i, partner, index, table, u, *rest):
    psi, t_a, t_b, x_a, x_b, mirror, q0, q2, q3, flat, parts, h0, h2 = rest
    info = Info(table_i, partner)
    for part in range(2):
        for c in range(3):
            flat[(part * 3 + c) * 4 : (part * 3 + c) * 4 + 4, :] = table[part, c]
    for hi in range(16):
        block = flat[:, hi * 256 : hi * 256 + 256]
        first = block.astype(jnp.bfloat16)
        left = block - first.astype(F32)
        second = left.astype(jnp.bfloat16)
        third = (left - second.astype(F32)).astype(jnp.bfloat16)
        for n, value in enumerate((first, second, third)):
            parts[hi * 24 : hi * 24 + 24, n * 256 : n * 256 + 256] = value
    low_iota = lax.broadcasted_iota(jnp.int32, (256, 128), 0)
    table_parts = parts[...]
    for r in range(16):
        wanted = index[r : r + 1, :]
        hot = jnp.where(low_iota == (wanted & 255), 1.0, 0.0).astype(jnp.bfloat16)
        found = jnp.dot(table_parts, jnp.concatenate([hot, hot, hot], axis=0), preferred_element_type=F32)
        high = jnp.broadcast_to(wanted >> 8, (24, 128))
        value = found[0:24]
        for hi in range(1, 16):
            value = jnp.where(high == hi, found[hi * 24 : hi * 24 + 24], value)
        psi[pl.ds(r, 24, stride=16), :] = value
    send_both(psi, u, info, t_a, t_b, x_a, x_b, mirror, q0, q2, q3, h0, h2)


def phi_kernel(table_i, partner, psi, u, q0, q2, q3, t_a, t_b, x_a, x_b, mirror, *rest):
    phi, o_ta, o_tb, o_xa, o_xb, o_m, o_q0, o_q2, o_q3, a0, b0, fa, fb, h0, h2 = rest
    info = Info(table_i, partner)
    arrived = arrived_swap(info, t_a, t_b, x_a, x_b, mirror)
    dirac(psi, u, arrived, q0, q2, q3, (a0, b0, fa, fb), phi, None)
    send_both(phi, u, info, o_ta, o_tb, o_xa, o_xb, o_m, o_q0, o_q2, o_q3, h0, h2)


def send_response(y, info, o_t, o_x, o_m, h2):
    for h in range(2):
        v = spinor(y, h)
        put_half(o_t, h, map_half(lambda a: a * info.sign_ahead, project(v, 1, -1)))
        put_half(h2, h, project(v, 2, -1))
        if h == 0:
            face = project(v, 0, -1)
            for t in range(2):
                for c in range(3):
                    for part in range(2):
                        k = half_index(part, t, c)
                        o_x[k * 4 : k * 4 + 4, :] = face[t][c][part][0:4]
    for k in range(12):
        send_rows(o_m, k, h2, k, info, 0)


def response_kernel(table_i, partner, phi, u, q0, q2, q3, t_a, t_b, x_a, x_b, mirror, *rest):
    y, w, o_t, o_x, o_m, a0, b0, fa, fb, h2 = rest
    info = Info(table_i, partner)
    arrived = arrived_swap(info, t_a, t_b, x_a, x_b, mirror)
    dirac(phi, u, arrived, q0, q2, q3, (a0, b0, fa, fb), y, w)
    send_response(y, info, o_t, o_x, o_m, h2)


def response2_kernel(table_i, partner, phi, u, q0, q2, q3, t_a, t_b, x_a, x_b, mirror, b_t, b_x, b_m, *rest):
    y, w, o_t, o_x, o_m, a0, b0, fa, fb, h2 = rest
    info = Info(table_i, partner)
    arrived = list(arrived_swap(info, t_a, t_b, x_a, x_b, mirror))
    arrived[1] = lambda k, h: ld(b_t, k, h)
    arrived[3] = lambda k: b_x[k * 4 : k * 4 + 4, :]
    arrived[5] = lambda k: b_m[k * 4 : k * 4 + 4, :]
    dirac(phi, u, arrived, q0, q2, q3, (a0, b0, fa, fb), y, w)
    send_response(y, info, o_t, o_x, o_m, h2)


def force_kernel(table_i, partner, phi, u, y, w, r_t, r_x, r_m, force, sent, a0, fa):
    info = Info(table_i, partner)
    for k in range(12):
        a0[k * HALO + 16 : k * HALO + 20, :] = r_x[k * 4 : k * 4 + 4, :]
        fa[pl.ds(k * ROWS + 3, 4, stride=4), :] = r_m[k * 4 : k * 4 + 4, :]
    for h in range(2):
        v = project(spinor(y, h), 0, -1)
        for t in range(2):
            for c in range(3):
                for part in range(2):
                    k = half_index(part, t, c)
                    a0[k * HALO + 8 * h : k * HALO + 8 * h + 8, :] = v[t][c][part]
    x2 = row_in_pair()
    for h in range(2):
        ysp = spinor(y, h)
        psp = spinor(phi, h)
        for mu in range(4):
            if mu == 0:
                x = get_half(lambda k: a0[k * HALO + 8 * h + 4 : k * HALO + 8 * h + 12, :])
            elif mu == 1:
                x = get_half(lambda k: ld(r_t, k, h))
            elif mu == 2:
                face = get_half(lambda k: ld(fa, k, h))
                x = map_half(
                    lambda r, f: jnp.where(x2 == 3, f, pltpu.roll(r, 7, 0)), project(ysp, 2, -1), face
                )
            else:
                x = map_half(lambda r: pltpu.roll(r, 127, 1), project(ysp, 3, -1))
            left = mat_half(matrix(u, mu, h), x) + get_half(lambda k: ld(w, mu * 12 + k, h))
            right = project(psp, mu, -1) + project(ysp, mu, 1)

            def g_im(i, j):
                return sum(left[n][i][1] * right[n][j][0] - left[n][i][0] * right[n][j][1] for n in range(4))

            def g_re(i, j):
                return sum(left[n][i][0] * right[n][j][0] + left[n][i][1] * right[n][j][1] for n in range(4))

            d = [g_im(i, i) for i in range(3)]
            third = (d[0] + d[1] + d[2]) * (1.0 / 3.0)
            scale = -2.0 * HOPPING
            values = [scale * (d[0] - third), scale * (d[1] - third)]
            for i, j in ((0, 1), (0, 2), (1, 2)):
                values.append((0.5 * scale) * (g_im(i, j) + g_im(j, i)))
                values.append((0.5 * scale) * (g_re(j, i) - g_re(i, j)))
            for n, value in enumerate(values):
                st(force, mu * 8 + n, h, value)
    for k in range(32):
        for j in range(4):
            at = pl.multiple_of(k * ROWS + 4 * info.partner[j], 4)
            sent[pl.ds(at, 4), :] = force[k * ROWS + 4 * j : k * ROWS + 4 * j + 4, :]


OFF = ((0, 1), (0, 2), (1, 2))


def updated_momenta(read, force, mirrored, mu, h):
    diag_force = [ld(force, mu * 8 + n, h) - ld(mirrored, mu * 8 + n, h) for n in range(2)]
    diag_force.append(-(diag_force[0] + diag_force[1]))
    diag = [read(n) + STEP * diag_force[n] for n in range(3)]
    upper = []
    for n in range(3):
        re = ld(force, mu * 8 + 2 + 2 * n, h) - ld(mirrored, mu * 8 + 2 + 2 * n, h)
        im = ld(force, mu * 8 + 3 + 2 * n, h) + ld(mirrored, mu * 8 + 3 + 2 * n, h)
        upper.append((read(3 + 2 * n) + STEP * re, read(4 + 2 * n) + STEP * im))
    return diag, upper


def link_step(diag, upper, u):
    b = [STEP * value for value in diag]
    b01, b02, b12 = ((STEP * value[0], STEP * value[1]) for value in upper)
    n01, n02, n12 = (v[0] * v[0] + v[1] * v[1] for v in (b01, b02, b12))
    square_diag = [b[0] * b[0] + n01 + n02, b[1] * b[1] + n01 + n12, b[2] * b[2] + n02 + n12]

    def scaled(v, by):
        return (v[0] * by, v[1] * by)

    square = [
        cadd(scaled(b01, b[0] + b[1]), cmul_conj(b02, b12)),
        cadd(scaled(b02, b[0] + b[2]), cmul(b01, b12)),
        cadd(scaled(b12, b[1] + b[2]), cmul_conj(b02, b01)),
    ]
    c1 = 0.5 * (square_diag[0] + square_diag[1] + square_diag[2])
    triple = cmul_conj(cmul(b01, b12), b02)[0]
    c0 = b[0] * (b[1] * b[2] - n12) - b[1] * n02 - b[2] * n01 + 2.0 * triple
    one = jnp.ones_like(c1)
    zero = jnp.zeros_like(c1)
    r0, r1, r2 = (one, zero), (zero, zero), (zero, zero)
    for k in range(DEGREE, 0, -1):
        inv = 1.0 / k
        new0 = (1.0 + (r2[1] * c0) * inv, -(r2[0] * c0) * inv)
        new1 = ((r0[0] - r2[0] * c1) * inv, (r0[1] - r2[1] * c1) * inv)
        new2 = (r1[0] * inv, r1[1] * inv)
        r0, r1, r2 = new0, new1, new2
    ir1 = (-r1[1], r1[0])
    e = [[None] * 3 for _ in range(3)]
    for i in range(3):
        e[i][i] = cadd(r0, csub(scaled(ir1, b[i]), scaled(r2, square_diag[i])))
    for (i, j), v, s in zip(OFF, (b01, b02, b12), square):
        e[i][j] = csub(cmul(ir1, v), cmul(r2, s))
        e[j][i] = csub(cmul_conj(ir1, v), cmul_conj(r2, s))
    return [[cadd(cadd(cmul(e[i][0], u[0][j]), cmul(e[i][1], u[1][j])), cmul(e[i][2], u[2][j])) for j in range(3)] for i in range(3)]


def input_momentum(ref, mu, h):
    def read(n):
        if n < 3:
            return ld(ref, mu * 18 + 4 * n, h)
        i, j = OFF[(n - 3) // 2]
        return ld(ref, mu * 18 + 9 * ((n - 3) % 2) + 3 * i + j, h)

    return read


def put_matrix(ref, mu, h, value):
    for i in range(3):
        for j in range(3):
            for part in range(2):
                st(ref, mu * 18 + part * 9 + i * 3 + j, h, value[i][j][part])


def update_kernel(table_i, partner, phi, u, p, force, mirrored, *rest):
    new_u, new_p, o_t, o_x, o_m, q0, q2, q3 = rest
    info = Info(table_i, partner)
    for h in range(2):
        psi = spinor(phi, h)
        for mu in range(4):
            diag, upper = updated_momenta(input_momentum(p, mu, h), force, mirrored, mu, h)
            for n in range(3):
                st(new_p, mu * 9 + n, h, diag[n])
                st(new_p, mu * 9 + 3 + 2 * n, h, upper[n][0])
                st(new_p, mu * 9 + 4 + 2 * n, h, upper[n][1])
            link = link_step(diag, upper, matrix(u, mu, h))
            put_matrix(new_u, mu, h, link)
            back = mat_dag_half(link, project(psi, mu, -1))
            if mu == 1:
                put_half(o_t, h, map_half(lambda a: a * info.sign_behind, back))
            else:
                put_half({0: q0, 2: q2, 3: q3}[mu], h, back)
    for k in range(12):
        o_x[k * 4 : k * 4 + 4, :] = q0[k * ROWS + 12 : k * ROWS + 16, :]
        send_rows(o_m, k, q2, k, info, 3)


def last_kernel(u, p, old_p, force, mirrored, new_u, new_p):
    for h in range(2):
        for mu in range(4):
            diag, upper = updated_momenta(lambda n: ld(p, mu * 9 + n, h), force, mirrored, mu, h)
            for i in range(3):
                st(new_p, mu * 18 + 4 * i, h, diag[i])
                st(new_p, mu * 18 + 9 + 4 * i, h, ld(old_p, mu * 18 + 9 + 4 * i, h))
            for (i, j), v in zip(OFF, upper):
                st(new_p, mu * 18 + 3 * i + j, h, v[0])
                st(new_p, mu * 18 + 3 * j + i, h, v[0])
                st(new_p, mu * 18 + 9 + 3 * i + j, h, v[1])
                st(new_p, mu * 18 + 9 + 3 * j + i, h, -v[1])
            put_matrix(new_u, mu, h, link_step(diag, upper, matrix(u, mu, h)))


VM = pl.BlockSpec(memory_space=pltpu.VMEM)
SM = pl.BlockSpec(memory_space=pltpu.SMEM)
FULL = ROWS * 12
FACE = 4 * 12


def call(kernel, name, n_scalar, args, outs, scratch, limit=4):
    return pl.pallas_call(
        kernel,
        name=name,
        out_shape=[jax.ShapeDtypeStruct((rows, 128), F32) for rows in outs],
        in_specs=[SM] * n_scalar + [VM] * (len(args) - n_scalar),
        out_specs=[VM] * len(outs),
        scratch_shapes=[s if not isinstance(s, int) else pltpu.VMEM((s, 128), F32) for s in scratch],
        compiler_params=pltpu.CompilerParams(vmem_limit_bytes=limit << 20),
    )(*args)


def swap(value, axis, far):
    n = lax.axis_size(axis)
    if far:
        pairs = [(i, (i + 1) % n if i % 2 else (i - 1) % n) for i in range(n)]
    else:
        pairs = [(i, i ^ 1) for i in range(n)]
    return lax.ppermute(value, axis, pairs)


def shift(value, axis, by):
    n = lax.axis_size(axis)
    return lax.ppermute(value, axis, [(i, (i + by) % n) for i in range(n)])


def mirror_swap(value):
    n = lax.axis_size("xd")
    return lax.ppermute(value, "xd", [(i, i ^ (n // 2)) for i in range(n)])


def exchange(t_a, t_b, x_a, x_b, m):
    far_t = swap(t_b, "ta", True)
    mirrored = mirror_swap(m)
    far_x = swap(x_b, "xd", True)
    near_x = swap(x_a, "xd", False)
    near_t = swap(t_a, "ta", False)
    return near_t, far_t, near_x, far_x, mirrored


def per_device(gauge_links, momenta, noise_table, noise_index, partner):
    ta = lax.axis_index("ta")
    xd = lax.axis_index("xd")
    lane = lax.iota(jnp.int32, 8)
    last = lax.axis_size("ta") - 1
    info = jnp.where(
        lane == 0,
        ta & 1,
        jnp.where(
            lane == 1,
            xd & 1,
            jnp.where(lane == 2, jnp.where(ta == 0, -1, 1), jnp.where(ta == last, -1, 1)),
        ),
    ).astype(jnp.int32)
    s = (info, partner)
    u = gauge_links.reshape(72 * ROWS, 128)
    p = momenta.reshape(72 * ROWS, 128)
    table = jnp.transpose(noise_table, (0, 2, 1, 3))
    index = noise_index.reshape(ROWS, 128)
    messages = [FULL, FULL, FACE, FACE, 2 * FACE]
    local = [FULL, FULL, FULL]
    halo = [12 * HALO, 12 * HALO, FULL, FULL]
    spin = 24 * ROWS

    psi, *rest = call(
        noise_kernel,
        "noise",
        2,
        (*s, index, table, u),
        [spin] + messages + local,
        [pltpu.VMEM((24, 4096), F32), pltpu.VMEM((384, 768), jnp.bfloat16), FULL, FULL],
        12,
    )
    arrived = exchange(*rest[:5])
    phi, *rest = call(
        phi_kernel, "phi", 2, (*s, psi, u, *rest[5:], *arrived), [spin] + messages + local, halo + [FULL, FULL]
    )
    arrived = exchange(*rest[:5])
    y, w, o_t, o_x, o_m = call(
        response_kernel,
        "response",
        2,
        (*s, phi, u, *rest[5:], *arrived),
        [spin, 4 * FULL, FULL, FACE, FACE],
        halo + [FULL],
    )
    force, sent = call(
        force_kernel,
        "force",
        2,
        (*s, phi, u, y, w, shift(o_t, "ta", -1), shift(o_x, "xd", -1), mirror_swap(o_m)),
        [32 * ROWS, 32 * ROWS],
        [12 * HALO, FULL],
    )
    u, p1, o_t, o_x, o_m, *q = call(
        update_kernel,
        "update",
        2,
        (*s, phi, u, p, force, mirror_swap(sent)),
        [72 * ROWS, 36 * ROWS, FULL, FACE, FACE] + local,
        [],
    )
    y, w, o_t, o_x, o_m = call(
        response2_kernel,
        "response2",
        2,
        (*s, phi, u, *q, *arrived, shift(o_t, "ta", 1), shift(o_x, "xd", 1), mirror_swap(o_m)),
        [spin, 4 * FULL, FULL, FACE, FACE],
        halo + [FULL],
    )
    force, sent = call(
        force_kernel,
        "force2",
        2,
        (*s, phi, u, y, w, shift(o_t, "ta", -1), shift(o_x, "xd", -1), mirror_swap(o_m)),
        [32 * ROWS, 32 * ROWS],
        [12 * HALO, FULL],
    )
    new_u, new_p = call(
        last_kernel, "last", 0, (u, p1, p, force, mirror_swap(sent)), [72 * ROWS, 72 * ROWS], []
    )
    return new_u.reshape(gauge_links.shape), new_p.reshape(momenta.shape)


def solution(mesh):
    sites = P(None, None, None, None, "xd", "ta", None, None)
    return jax.shard_map(
        per_device,
        mesh=mesh,
        in_specs=(sites, sites, P(), P("xd", "ta", None, None), P("xd")),
        out_specs=(sites, sites),
        check_vma=False,
    )
```

```python
import jax
import jax.numpy as jnp
from jax import lax
from jax.experimental import pallas as pl
from jax.experimental.pallas import tpu as pltpu
from jax.sharding import PartitionSpec as P


HOPPING = 0.13
STEP = 0.25
DEGREE = 6
F32 = jnp.float32
GAMMA = (
    ((3, 2, 1, 0), ((0, 1), (0, 1), (0, -1), (0, -1))),
    ((2, 3, 0, 1), ((1, 0), (1, 0), (1, 0), (1, 0))),
    ((3, 2, 1, 0), ((-1, 0), (1, 0), (1, 0), (-1, 0))),
    ((2, 3, 0, 1), ((0, 1), (0, -1), (0, -1), (0, 1))),
)
ROWS = 16
HALO = 24


def ld(ref, k, h):
    return ref[k * ROWS + 8 * h : k * ROWS + 8 * h + 8, :]


def st(ref, k, h, value):
    ref[k * ROWS + 8 * h : k * ROWS + 8 * h + 8, :] = value


def cadd(a, b):
    return (a[0] + b[0], a[1] + b[1])


def csub(a, b):
    return (a[0] - b[0], a[1] - b[1])


def cmul(a, b):
    return (a[0] * b[0] - a[1] * b[1], a[0] * b[1] + a[1] * b[0])


def cmul_conj(a, b):
    return (a[0] * b[0] + a[1] * b[1], a[1] * b[0] - a[0] * b[1])


def add_unit(x, y, coef, sign):
    re, im = coef
    if re:
        if re * sign > 0:
            return cadd(x, y)
        return csub(x, y)
    if im * sign > 0:
        return (x[0] - y[1], x[1] + y[0])
    return (x[0] + y[1], x[1] - y[0])


def spinor(ref, h):
    return [[(ld(ref, c * 4 + s, h), ld(ref, 12 + c * 4 + s, h)) for c in range(3)] for s in range(4)]


def project(psi, mu, sign):
    source, coef = GAMMA[mu]
    return [[add_unit(psi[t][c], psi[source[t]][c], coef[t], sign) for c in range(3)] for t in range(2)]


def matrix(ref, mu, h):
    return [[(ld(ref, mu * 18 + i * 3 + j, h), ld(ref, mu * 18 + 9 + i * 3 + j, h)) for j in range(3)] for i in range(3)]


def mat_half(u, v):
    out = []
    for t in range(2):
        row = []
        for i in range(3):
            acc = cmul(u[i][0], v[t][0])
            for j in (1, 2):
                acc = cadd(acc, cmul(u[i][j], v[t][j]))
            row.append(acc)
        out.append(row)
    return out


def mat_dag_half(u, v):
    out = []
    for t in range(2):
        row = []
        for i in range(3):
            acc = cmul_conj(v[t][0], u[0][i])
            for j in (1, 2):
                acc = cadd(acc, cmul_conj(v[t][j], u[j][i]))
            row.append(acc)
        out.append(row)
    return out


def half_index(part, t, c):
    return part * 6 + t * 3 + c


def put_half(ref, h, v, base=0):
    for t in range(2):
        for c in range(3):
            for part in range(2):
                st(ref, base + half_index(part, t, c), h, v[t][c][part])


def get_half(fn):
    return [[tuple(fn(half_index(part, t, c)) for part in range(2)) for c in range(3)] for t in range(2)]


def map_half(fn, *vs):
    return [[tuple(fn(*(v[t][c][part] for v in vs)) for part in range(2)) for c in range(3)] for t in range(2)]


class Info:
    def __init__(self, table, partner):
        self.even_t = table[0] == 0
        self.even_x = table[1] == 0
        self.sign_ahead = table[2].astype(F32)
        self.sign_behind = table[3].astype(F32)
        self.partner = [partner[j] & 3 for j in range(4)]


def row_in_pair():
    return lax.broadcasted_iota(jnp.int32, (8, 128), 0) & 3


def send_rows(dst, base, src, k, info, row):
    for j in range(4):
        dst[pl.ds(base * 4 + info.partner[j], 1), :] = src[k * ROWS + 4 * j + row : k * ROWS + 4 * j + row + 1, :]


def send_both(psi_ref, u_ref, info, t_a, t_b, x_a, x_b, mirror, q0, q2, q3, h0, h2):
    for h in range(2):
        psi = spinor(psi_ref, h)
        front = map_half(lambda a: a * info.sign_ahead, project(psi, 1, 1))
        back = map_half(
            lambda a: a * info.sign_behind, mat_dag_half(matrix(u_ref, 1, h), project(psi, 1, -1))
        )
        put_half(t_a, h, map_half(lambda a, b: jnp.where(info.even_t, b, a), front, back))
        put_half(t_b, h, map_half(lambda a, b: jnp.where(info.even_t, a, b), front, back))
        put_half(h0, h, project(psi, 0, 1))
        put_half(h2, h, project(psi, 2, 1))
        for mu, ref in ((0, q0), (2, q2), (3, q3)):
            put_half(ref, h, mat_dag_half(matrix(u_ref, mu, h), project(psi, mu, -1)))
    for k in range(12):
        front = h0[k * ROWS : k * ROWS + 4, :]
        back = q0[k * ROWS + 12 : k * ROWS + 16, :]
        x_a[k * 4 : k * 4 + 4, :] = jnp.where(info.even_x, back, front)
        x_b[k * 4 : k * 4 + 4, :] = jnp.where(info.even_x, front, back)
        send_rows(mirror, k, h2, k, info, 0)
        send_rows(mirror, 12 + k, q2, k, info, 3)


def dirac(psi_ref, u_ref, arrived, q0, q2, q3, scratch, out_ref, w_ref):
    ahead_t, behind_t, ahead_x, behind_x, ahead_m, behind_m = arrived
    a0, b0, fa, fb = scratch
    for k in range(12):
        a0[k * HALO + 16 : k * HALO + 20, :] = ahead_x(k)
        b0[k * HALO : k * HALO + 4, :] = behind_x(k)
        b0[k * HALO + 4 : k * HALO + 20, :] = q0[k * ROWS : k * ROWS + 16, :]
        fa[pl.ds(k * ROWS + 3, 4, stride=4), :] = ahead_m(k)
        fb[pl.ds(k * ROWS, 4, stride=4), :] = behind_m(k)
    for h in range(2):
        v = project(spinor(psi_ref, h), 0, 1)
        for t in range(2):
            for c in range(3):
                for part in range(2):
                    k = half_index(part, t, c)
                    a0[k * HALO + 8 * h : k * HALO + 8 * h + 8, :] = v[t][c][part]
    x2 = row_in_pair()
    for h in range(2):
        psi = spinor(psi_ref, h)
        acc = None
        for mu in range(4):
            if mu == 0:
                ahead = get_half(lambda k: a0[k * HALO + 8 * h + 4 : k * HALO + 8 * h + 12, :])
                behind = get_half(lambda k: b0[k * HALO + 8 * h : k * HALO + 8 * h + 8, :])
            elif mu == 1:
                ahead = get_half(lambda k: ahead_t(k, h))
                behind = get_half(lambda k: behind_t(k, h))
            elif mu == 2:
                raw = project(psi, 2, 1)
                face = get_half(lambda k: ld(fa, k, h))
                ahead = map_half(lambda r, f: jnp.where(x2 == 3, f, pltpu.roll(r, 7, 0)), raw, face)
                behind = get_half(lambda k: jnp.where(x2 == 0, ld(fb, k, h), pltpu.roll(ld(q2, k, h), 1, 0)))
            else:
                ahead = map_half(lambda r: pltpu.roll(r, 127, 1), project(psi, 3, 1))
                behind = get_half(lambda k: pltpu.roll(ld(q3, k, h), 1, 1))
            w = mat_half(matrix(u_ref, mu, h), ahead)
            if w_ref is not None:
                put_half(w_ref, h, w, mu * 12)
            total = map_half(lambda a, b: a + b, w, behind)
            delta = map_half(lambda a, b: a - b, w, behind)
            source, coef = GAMMA[mu]
            if acc is None:
                zero = jnp.zeros((8, 128), F32)
                acc = [total[0], total[1]] + [
                    [add_unit((zero, zero), delta[source[s]][c], coef[s], 1) for c in range(3)] for s in (2, 3)
                ]
            else:
                for s in range(2):
                    acc[s] = [cadd(acc[s][c], total[s][c]) for c in range(3)]
                for s in (2, 3):
                    acc[s] = [add_unit(acc[s][c], delta[source[s]][c], coef[s], 1) for c in range(3)]
        for s in range(4):
            for c in range(3):
                for part in range(2):
                    st(out_ref, part * 12 + c * 4 + s, h, psi[s][c][part] - HOPPING * acc[s][c][part])


def arrived_swap(info, t_a, t_b, x_a, x_b, mirror):
    def rows(ref, k):
        return ref[k * 4 : k * 4 + 4, :]

    return (
        lambda k, h: jnp.where(info.even_t, ld(t_a, k, h), ld(t_b, k, h)),
        lambda k, h: jnp.where(info.even_t, ld(t_b, k, h), ld(t_a, k, h)),
        lambda k: jnp.where(info.even_x, rows(x_a, k), rows(x_b, k)),
        lambda k: jnp.where(info.even_x, rows(x_b, k), rows(x_a, k)),
        lambda k: rows(mirror, k),
        lambda k: rows(mirror, 12 + k),
    )


def noise_kernel(table_i, partner, index, table, u, *rest):
    psi, t_a, t_b, x_a, x_b, mirror, q0, q2, q3, flat, parts, h0, h2 = rest
    info = Info(table_i, partner)
    for part in range(2):
        for c in range(3):
            flat[(part * 3 + c) * 4 : (part * 3 + c) * 4 + 4, :] = table[part, c]
    for hi in range(16):
        block = flat[:, hi * 256 : hi * 256 + 256]
        first = block.astype(jnp.bfloat16)
        left = block - first.astype(F32)
        second = left.astype(jnp.bfloat16)
        third = (left - second.astype(F32)).astype(jnp.bfloat16)
        for n, value in enumerate((first, second, third)):
            parts[hi * 24 : hi * 24 + 24, n * 256 : n * 256 + 256] = value
    low_iota = lax.broadcasted_iota(jnp.int32, (256, 128), 0)
    table_parts = parts[...]
    for r in range(16):
        wanted = index[r : r + 1, :]
        hot = jnp.where(low_iota == (wanted & 255), 1.0, 0.0).astype(jnp.bfloat16)
        found = jnp.dot(table_parts, jnp.concatenate([hot, hot, hot], axis=0), preferred_element_type=F32)
        high = jnp.broadcast_to(wanted >> 8, (24, 128))
        value = found[0:24]
        for hi in range(1, 16):
            value = jnp.where(high == hi, found[hi * 24 : hi * 24 + 24], value)
        psi[pl.ds(r, 24, stride=16), :] = value
    send_both(psi, u, info, t_a, t_b, x_a, x_b, mirror, q0, q2, q3, h0, h2)


def phi_kernel(table_i, partner, psi, u, q0, q2, q3, t_a, t_b, x_a, x_b, mirror, *rest):
    phi, o_ta, o_tb, o_xa, o_xb, o_m, o_q0, o_q2, o_q3, a0, b0, fa, fb, h0, h2 = rest
    info = Info(table_i, partner)
    arrived = arrived_swap(info, t_a, t_b, x_a, x_b, mirror)
    dirac(psi, u, arrived, q0, q2, q3, (a0, b0, fa, fb), phi, None)
    send_both(phi, u, info, o_ta, o_tb, o_xa, o_xb, o_m, o_q0, o_q2, o_q3, h0, h2)


def send_response(y, info, o_t, o_x, o_m, h2):
    for h in range(2):
        v = spinor(y, h)
        put_half(o_t, h, map_half(lambda a: a * info.sign_ahead, project(v, 1, -1)))
        put_half(h2, h, project(v, 2, -1))
        if h == 0:
            face = project(v, 0, -1)
            for t in range(2):
                for c in range(3):
                    for part in range(2):
                        k = half_index(part, t, c)
                        o_x[k * 4 : k * 4 + 4, :] = face[t][c][part][0:4]
    for k in range(12):
        send_rows(o_m, k, h2, k, info, 0)


def response_kernel(table_i, partner, phi, u, q0, q2, q3, t_a, t_b, x_a, x_b, mirror, *rest):
    y, w, o_t, o_x, o_m, a0, b0, fa, fb, h2 = rest
    info = Info(table_i, partner)
    arrived = arrived_swap(info, t_a, t_b, x_a, x_b, mirror)
    dirac(phi, u, arrived, q0, q2, q3, (a0, b0, fa, fb), y, w)
    send_response(y, info, o_t, o_x, o_m, h2)


def response2_kernel(table_i, partner, phi, u, q0, q2, q3, t_a, t_b, x_a, x_b, mirror, b_t, b_x, b_m, *rest):
    y, w, o_t, o_x, o_m, a0, b0, fa, fb, h2 = rest
    info = Info(table_i, partner)
    arrived = list(arrived_swap(info, t_a, t_b, x_a, x_b, mirror))
    arrived[1] = lambda k, h: ld(b_t, k, h)
    arrived[3] = lambda k: b_x[k * 4 : k * 4 + 4, :]
    arrived[5] = lambda k: b_m[k * 4 : k * 4 + 4, :]
    dirac(phi, u, arrived, q0, q2, q3, (a0, b0, fa, fb), y, w)
    send_response(y, info, o_t, o_x, o_m, h2)


def force_kernel(table_i, partner, phi, u, y, w, r_t, r_x, r_m, force, sent, a0, fa):
    info = Info(table_i, partner)
    for k in range(12):
        a0[k * HALO + 16 : k * HALO + 20, :] = r_x[k * 4 : k * 4 + 4, :]
        fa[pl.ds(k * ROWS + 3, 4, stride=4), :] = r_m[k * 4 : k * 4 + 4, :]
    for h in range(2):
        v = project(spinor(y, h), 0, -1)
        for t in range(2):
            for c in range(3):
                for part in range(2):
                    k = half_index(part, t, c)
                    a0[k * HALO + 8 * h : k * HALO + 8 * h + 8, :] = v[t][c][part]
    x2 = row_in_pair()
    for h in range(2):
        ysp = spinor(y, h)
        psp = spinor(phi, h)
        for mu in range(4):
            if mu == 0:
                x = get_half(lambda k: a0[k * HALO + 8 * h + 4 : k * HALO + 8 * h + 12, :])
            elif mu == 1:
                x = get_half(lambda k: ld(r_t, k, h))
            elif mu == 2:
                face = get_half(lambda k: ld(fa, k, h))
                x = map_half(
                    lambda r, f: jnp.where(x2 == 3, f, pltpu.roll(r, 7, 0)), project(ysp, 2, -1), face
                )
            else:
                x = map_half(lambda r: pltpu.roll(r, 127, 1), project(ysp, 3, -1))
            left = mat_half(matrix(u, mu, h), x) + get_half(lambda k: ld(w, mu * 12 + k, h))
            right = project(psp, mu, -1) + project(ysp, mu, 1)

            def g_im(i, j):
                return sum(left[n][i][1] * right[n][j][0] - left[n][i][0] * right[n][j][1] for n in range(4))

            def g_re(i, j):
                return sum(left[n][i][0] * right[n][j][0] + left[n][i][1] * right[n][j][1] for n in range(4))

            d = [g_im(i, i) for i in range(3)]
            third = (d[0] + d[1] + d[2]) * (1.0 / 3.0)
            scale = -2.0 * HOPPING
            values = [scale * (d[0] - third), scale * (d[1] - third)]
            for i, j in ((0, 1), (0, 2), (1, 2)):
                values.append((0.5 * scale) * (g_im(i, j) + g_im(j, i)))
                values.append((0.5 * scale) * (g_re(j, i) - g_re(i, j)))
            for n, value in enumerate(values):
                st(force, mu * 8 + n, h, value)
    for k in range(32):
        for j in range(4):
            at = pl.multiple_of(k * ROWS + 4 * info.partner[j], 4)
            sent[pl.ds(at, 4), :] = force[k * ROWS + 4 * j : k * ROWS + 4 * j + 4, :]


OFF = ((0, 1), (0, 2), (1, 2))


def updated_momenta(read, force, mirrored, mu, h):
    diag_force = [ld(force, mu * 8 + n, h) - ld(mirrored, mu * 8 + n, h) for n in range(2)]
    diag_force.append(-(diag_force[0] + diag_force[1]))
    diag = [read(n) + STEP * diag_force[n] for n in range(3)]
    upper = []
    for n in range(3):
        re = ld(force, mu * 8 + 2 + 2 * n, h) - ld(mirrored, mu * 8 + 2 + 2 * n, h)
        im = ld(force, mu * 8 + 3 + 2 * n, h) + ld(mirrored, mu * 8 + 3 + 2 * n, h)
        upper.append((read(3 + 2 * n) + STEP * re, read(4 + 2 * n) + STEP * im))
    return diag, upper


def link_step(diag, upper, u):
    b = [STEP * value for value in diag]
    b01, b02, b12 = ((STEP * value[0], STEP * value[1]) for value in upper)
    n01, n02, n12 = (v[0] * v[0] + v[1] * v[1] for v in (b01, b02, b12))
    square_diag = [b[0] * b[0] + n01 + n02, b[1] * b[1] + n01 + n12, b[2] * b[2] + n02 + n12]

    def scaled(v, by):
        return (v[0] * by, v[1] * by)

    square = [
        cadd(scaled(b01, b[0] + b[1]), cmul_conj(b02, b12)),
        cadd(scaled(b02, b[0] + b[2]), cmul(b01, b12)),
        cadd(scaled(b12, b[1] + b[2]), cmul_conj(b02, b01)),
    ]
    c1 = 0.5 * (square_diag[0] + square_diag[1] + square_diag[2])
    triple = cmul_conj(cmul(b01, b12), b02)[0]
    c0 = b[0] * (b[1] * b[2] - n12) - b[1] * n02 - b[2] * n01 + 2.0 * triple
    one = jnp.ones_like(c1)
    zero = jnp.zeros_like(c1)
    r0, r1, r2 = (one, zero), (zero, zero), (zero, zero)
    for k in range(DEGREE, 0, -1):
        inv = 1.0 / k
        new0 = (1.0 + (r2[1] * c0) * inv, -(r2[0] * c0) * inv)
        new1 = ((r0[0] - r2[0] * c1) * inv, (r0[1] - r2[1] * c1) * inv)
        new2 = (r1[0] * inv, r1[1] * inv)
        r0, r1, r2 = new0, new1, new2
    ir1 = (-r1[1], r1[0])
    e = [[None] * 3 for _ in range(3)]
    for i in range(3):
        e[i][i] = cadd(r0, csub(scaled(ir1, b[i]), scaled(r2, square_diag[i])))
    for (i, j), v, s in zip(OFF, (b01, b02, b12), square):
        e[i][j] = csub(cmul(ir1, v), cmul(r2, s))
        e[j][i] = csub(cmul_conj(ir1, v), cmul_conj(r2, s))
    return [[cadd(cadd(cmul(e[i][0], u[0][j]), cmul(e[i][1], u[1][j])), cmul(e[i][2], u[2][j])) for j in range(3)] for i in range(3)]


def input_momentum(ref, mu, h):
    def read(n):
        if n < 3:
            return ld(ref, mu * 18 + 4 * n, h)
        i, j = OFF[(n - 3) // 2]
        return ld(ref, mu * 18 + 9 * ((n - 3) % 2) + 3 * i + j, h)

    return read


def put_matrix(ref, mu, h, value):
    for i in range(3):
        for j in range(3):
            for part in range(2):
                st(ref, mu * 18 + part * 9 + i * 3 + j, h, value[i][j][part])


def update_kernel(table_i, partner, phi, u, p, force, mirrored, *rest):
    new_u, new_p, o_t, o_x, o_m, q0, q2, q3 = rest
    info = Info(table_i, partner)
    for h in range(2):
        psi = spinor(phi, h)
        for mu in range(4):
            diag, upper = updated_momenta(input_momentum(p, mu, h), force, mirrored, mu, h)
            for n in range(3):
                st(new_p, mu * 9 + n, h, diag[n])
                st(new_p, mu * 9 + 3 + 2 * n, h, upper[n][0])
                st(new_p, mu * 9 + 4 + 2 * n, h, upper[n][1])
            link = link_step(diag, upper, matrix(u, mu, h))
            put_matrix(new_u, mu, h, link)
            back = mat_dag_half(link, project(psi, mu, -1))
            if mu == 1:
                put_half(o_t, h, map_half(lambda a: a * info.sign_behind, back))
            else:
                put_half({0: q0, 2: q2, 3: q3}[mu], h, back)
    for k in range(12):
        o_x[k * 4 : k * 4 + 4, :] = q0[k * ROWS + 12 : k * ROWS + 16, :]
        send_rows(o_m, k, q2, k, info, 3)


def last_kernel(u, p, old_p, force, mirrored, new_u, new_p):
    for h in range(2):
        for mu in range(4):
            diag, upper = updated_momenta(lambda n: ld(p, mu * 9 + n, h), force, mirrored, mu, h)
            for i in range(3):
                st(new_p, mu * 18 + 4 * i, h, diag[i])
                st(new_p, mu * 18 + 9 + 4 * i, h, ld(old_p, mu * 18 + 9 + 4 * i, h))
            for (i, j), v in zip(OFF, upper):
                st(new_p, mu * 18 + 3 * i + j, h, v[0])
                st(new_p, mu * 18 + 3 * j + i, h, v[0])
                st(new_p, mu * 18 + 9 + 3 * i + j, h, v[1])
                st(new_p, mu * 18 + 9 + 3 * j + i, h, -v[1])
            put_matrix(new_u, mu, h, link_step(diag, upper, matrix(u, mu, h)))


VM = pl.BlockSpec(memory_space=pltpu.VMEM)
SM = pl.BlockSpec(memory_space=pltpu.SMEM)
FULL = ROWS * 12
FACE = 4 * 12


def call(kernel, n_scalar, args, outs, scratch, limit=4):
    return pl.pallas_call(
        kernel,
        out_shape=[jax.ShapeDtypeStruct((rows, 128), F32) for rows in outs],
        in_specs=[SM] * n_scalar + [VM] * (len(args) - n_scalar),
        out_specs=[VM] * len(outs),
        scratch_shapes=[s if not isinstance(s, int) else pltpu.VMEM((s, 128), F32) for s in scratch],
        compiler_params=pltpu.CompilerParams(vmem_limit_bytes=limit << 20),
    )(*args)


def swap(value, axis, far):
    n = lax.axis_size(axis)
    if far:
        pairs = [(i, (i + 1) % n if i % 2 else (i - 1) % n) for i in range(n)]
    else:
        pairs = [(i, i ^ 1) for i in range(n)]
    return lax.ppermute(value, axis, pairs)


def shift(value, axis, by):
    n = lax.axis_size(axis)
    return lax.ppermute(value, axis, [(i, (i + by) % n) for i in range(n)])


def mirror_swap(value):
    n = lax.axis_size("xd")
    return lax.ppermute(value, "xd", [(i, i ^ (n // 2)) for i in range(n)])


def moved(name, value):
    if name == "far_t":
        return swap(value, "ta", True)
    if name == "near_t":
        return swap(value, "ta", False)
    if name == "far_x":
        return swap(value, "xd", True)
    if name == "near_x":
        return swap(value, "xd", False)
    if name == "back_t":
        return shift(value, "ta", -1)
    if name == "back_x":
        return shift(value, "xd", -1)
    if name == "on_t":
        return shift(value, "ta", 1)
    if name == "on_x":
        return shift(value, "xd", 1)
    return mirror_swap(value)


SWAP_ORDER = ("far_t", "mirror", "far_x", "near_x", "near_t")
BACK_ORDER = ("back_t", "mirror", "back_x")
ON_ORDER = ("on_t", "mirror", "on_x")


def exchange(order, **values):
    return {name: moved(name, values[name]) for name in order}


def swap_exchange(t_a, t_b, x_a, x_b, m):
    got = exchange(SWAP_ORDER, near_t=t_a, far_t=t_b, near_x=x_a, far_x=x_b, mirror=m)
    return [got[name] for name in ("near_t", "far_t", "near_x", "far_x", "mirror")]


def back_exchange(t, x, m):
    got = exchange(BACK_ORDER, back_t=t, back_x=x, mirror=m)
    return [got[name] for name in ("back_t", "back_x", "mirror")]


def on_exchange(t, x, m):
    got = exchange(ON_ORDER, on_t=t, on_x=x, mirror=m)
    return [got[name] for name in ("on_t", "on_x", "mirror")]


def per_device(gauge_links, momenta, noise_table, noise_index, partner):
    ta = lax.axis_index("ta")
    xd = lax.axis_index("xd")
    lane = lax.iota(jnp.int32, 8)
    last = lax.axis_size("ta") - 1
    info = jnp.where(
        lane == 0,
        ta & 1,
        jnp.where(
            lane == 1,
            xd & 1,
            jnp.where(lane == 2, jnp.where(ta == 0, -1, 1), jnp.where(ta == last, -1, 1)),
        ),
    ).astype(jnp.int32)
    s = (info, partner)
    u = gauge_links.reshape(72 * ROWS, 128)
    p = momenta.reshape(72 * ROWS, 128)
    table = jnp.transpose(noise_table, (0, 2, 1, 3))
    index = noise_index.reshape(ROWS, 128)
    messages = [FULL, FULL, FACE, FACE, 2 * FACE]
    local = [FULL, FULL, FULL]
    halo = [12 * HALO, 12 * HALO, FULL, FULL]
    spin = 24 * ROWS

    psi, *rest = call(
        noise_kernel,
        2,
        (*s, index, table, u),
        [spin] + messages + local,
        [pltpu.VMEM((24, 4096), F32), pltpu.VMEM((384, 768), jnp.bfloat16), FULL, FULL],
        12,
    )
    arrived = swap_exchange(*rest[:5])
    phi, *rest = call(phi_kernel, 2, (*s, psi, u, *rest[5:], *arrived), [spin] + messages + local, halo + [FULL, FULL])
    arrived = swap_exchange(*rest[:5])
    y, w, o_t, o_x, o_m = call(
        response_kernel, 2, (*s, phi, u, *rest[5:], *arrived), [spin, 4 * FULL, FULL, FACE, FACE], halo + [FULL]
    )
    force, sent = call(
        force_kernel, 2, (*s, phi, u, y, w, *back_exchange(o_t, o_x, o_m)), [32 * ROWS, 32 * ROWS], [12 * HALO, FULL]
    )
    u, p1, o_t, o_x, o_m, *q = call(
        update_kernel,
        2,
        (*s, phi, u, p, force, mirror_swap(sent)),
        [72 * ROWS, 36 * ROWS, FULL, FACE, FACE] + local,
        [],
    )
    y, w, o_t, o_x, o_m = call(
        response2_kernel,
        2,
        (*s, phi, u, *q, *arrived, *on_exchange(o_t, o_x, o_m)),
        [spin, 4 * FULL, FULL, FACE, FACE],
        halo + [FULL],
    )
    force, sent = call(
        force_kernel, 2, (*s, phi, u, y, w, *back_exchange(o_t, o_x, o_m)), [32 * ROWS, 32 * ROWS], [12 * HALO, FULL]
    )
    new_u, new_p = call(last_kernel, 0, (u, p1, p, force, mirror_swap(sent)), [72 * ROWS, 72 * ROWS], [])
    return new_u.reshape(gauge_links.shape), new_p.reshape(momenta.shape)


def solution(mesh):
    sites = P(None, None, None, None, "xd", "ta", None, None)
    return jax.shard_map(
        per_device,
        mesh=mesh,
        in_specs=(sites, sites, P(), P("xd", "ta", None, None), P("xd")),
        out_specs=(sites, sites),
        check_vma=False,
    )
```

```python
import jax
import jax.numpy as jnp
from jax import lax
from jax.experimental import pallas as pl
from jax.experimental.pallas import tpu as pltpu
from jax.sharding import PartitionSpec as P


HOPPING = 0.13
STEP = 0.25
DEGREE = 6
F32 = jnp.float32
GAMMA = (
    ((3, 2, 1, 0), ((0, 1), (0, 1), (0, -1), (0, -1))),
    ((2, 3, 0, 1), ((1, 0), (1, 0), (1, 0), (1, 0))),
    ((3, 2, 1, 0), ((-1, 0), (1, 0), (1, 0), (-1, 0))),
    ((2, 3, 0, 1), ((0, 1), (0, -1), (0, -1), (0, 1))),
)
ROWS = 16
HALO = 24


def ld(ref, k, h):
    return ref[k * ROWS + 8 * h : k * ROWS + 8 * h + 8, :]


def st(ref, k, h, value):
    ref[k * ROWS + 8 * h : k * ROWS + 8 * h + 8, :] = value


def cadd(a, b):
    return (a[0] + b[0], a[1] + b[1])


def csub(a, b):
    return (a[0] - b[0], a[1] - b[1])


def cmul(a, b):
    return (a[0] * b[0] - a[1] * b[1], a[0] * b[1] + a[1] * b[0])


def cmul_conj(a, b):
    return (a[0] * b[0] + a[1] * b[1], a[1] * b[0] - a[0] * b[1])


def add_unit(x, y, coef, sign):
    re, im = coef
    if re:
        if re * sign > 0:
            return cadd(x, y)
        return csub(x, y)
    if im * sign > 0:
        return (x[0] - y[1], x[1] + y[0])
    return (x[0] + y[1], x[1] - y[0])


def spinor(ref, h):
    return [[(ld(ref, c * 4 + s, h), ld(ref, 12 + c * 4 + s, h)) for c in range(3)] for s in range(4)]


def project(psi, mu, sign):
    source, coef = GAMMA[mu]
    return [[add_unit(psi[t][c], psi[source[t]][c], coef[t], sign) for c in range(3)] for t in range(2)]


def matrix(ref, mu, h):
    return [[(ld(ref, mu * 18 + i * 3 + j, h), ld(ref, mu * 18 + 9 + i * 3 + j, h)) for j in range(3)] for i in range(3)]


def mat_half(u, v):
    out = []
    for t in range(2):
        row = []
        for i in range(3):
            acc = cmul(u[i][0], v[t][0])
            for j in (1, 2):
                acc = cadd(acc, cmul(u[i][j], v[t][j]))
            row.append(acc)
        out.append(row)
    return out


def mat_dag_half(u, v):
    out = []
    for t in range(2):
        row = []
        for i in range(3):
            acc = cmul_conj(v[t][0], u[0][i])
            for j in (1, 2):
                acc = cadd(acc, cmul_conj(v[t][j], u[j][i]))
            row.append(acc)
        out.append(row)
    return out


def half_index(part, t, c):
    return part * 6 + t * 3 + c


def put_half(ref, h, v, base=0):
    for t in range(2):
        for c in range(3):
            for part in range(2):
                st(ref, base + half_index(part, t, c), h, v[t][c][part])


def get_half(fn):
    return [[tuple(fn(half_index(part, t, c)) for part in range(2)) for c in range(3)] for t in range(2)]


def map_half(fn, *vs):
    return [[tuple(fn(*(v[t][c][part] for v in vs)) for part in range(2)) for c in range(3)] for t in range(2)]


class Info:
    def __init__(self, table, partner):
        self.even_t = table[0] == 0
        self.even_x = table[1] == 0
        self.sign_ahead = table[2].astype(F32)
        self.sign_behind = table[3].astype(F32)
        self.partner = [partner[j] & 3 for j in range(4)]


def row_in_pair():
    return lax.broadcasted_iota(jnp.int32, (8, 128), 0) & 3


def send_rows(dst, base, src, k, info, row):
    for j in range(4):
        dst[pl.ds(base * 4 + info.partner[j], 1), :] = src[k * ROWS + 4 * j + row : k * ROWS + 4 * j + row + 1, :]


def send_both(psi_ref, u_ref, info, t_a, t_b, x_a, x_b, mirror, q0, q2, q3, h0, h2):
    for h in range(2):
        psi = spinor(psi_ref, h)
        front = map_half(lambda a: a * info.sign_ahead, project(psi, 1, 1))
        back = map_half(
            lambda a: a * info.sign_behind, mat_dag_half(matrix(u_ref, 1, h), project(psi, 1, -1))
        )
        put_half(t_a, h, map_half(lambda a, b: jnp.where(info.even_t, b, a), front, back))
        put_half(t_b, h, map_half(lambda a, b: jnp.where(info.even_t, a, b), front, back))
        put_half(h0, h, project(psi, 0, 1))
        put_half(h2, h, project(psi, 2, 1))
        for mu, ref in ((0, q0), (2, q2), (3, q3)):
            put_half(ref, h, mat_dag_half(matrix(u_ref, mu, h), project(psi, mu, -1)))
    for k in range(12):
        front = h0[k * ROWS : k * ROWS + 4, :]
        back = q0[k * ROWS + 12 : k * ROWS + 16, :]
        x_a[k * 4 : k * 4 + 4, :] = jnp.where(info.even_x, back, front)
        x_b[k * 4 : k * 4 + 4, :] = jnp.where(info.even_x, front, back)
        send_rows(mirror, k, h2, k, info, 0)
        send_rows(mirror, 12 + k, q2, k, info, 3)


def dirac(psi_ref, u_ref, arrived, q0, q2, q3, scratch, out_ref, w_ref):
    ahead_t, behind_t, ahead_x, behind_x, ahead_m, behind_m = arrived
    a0, b0, fa, fb = scratch
    for k in range(12):
        a0[k * HALO + 16 : k * HALO + 20, :] = ahead_x(k)
        b0[k * HALO : k * HALO + 4, :] = behind_x(k)
        b0[k * HALO + 4 : k * HALO + 20, :] = q0[k * ROWS : k * ROWS + 16, :]
        fa[pl.ds(k * ROWS + 3, 4, stride=4), :] = ahead_m(k)
        fb[pl.ds(k * ROWS, 4, stride=4), :] = behind_m(k)
    for h in range(2):
        v = project(spinor(psi_ref, h), 0, 1)
        for t in range(2):
            for c in range(3):
                for part in range(2):
                    k = half_index(part, t, c)
                    a0[k * HALO + 8 * h : k * HALO + 8 * h + 8, :] = v[t][c][part]
    x2 = row_in_pair()
    for h in range(2):
        psi = spinor(psi_ref, h)
        acc = None
        for mu in range(4):
            if mu == 0:
                ahead = get_half(lambda k: a0[k * HALO + 8 * h + 4 : k * HALO + 8 * h + 12, :])
                behind = get_half(lambda k: b0[k * HALO + 8 * h : k * HALO + 8 * h + 8, :])
            elif mu == 1:
                ahead = get_half(lambda k: ahead_t(k, h))
                behind = get_half(lambda k: behind_t(k, h))
            elif mu == 2:
                raw = project(psi, 2, 1)
                face = get_half(lambda k: ld(fa, k, h))
                ahead = map_half(lambda r, f: jnp.where(x2 == 3, f, pltpu.roll(r, 7, 0)), raw, face)
                behind = get_half(lambda k: jnp.where(x2 == 0, ld(fb, k, h), pltpu.roll(ld(q2, k, h), 1, 0)))
            else:
                ahead = map_half(lambda r: pltpu.roll(r, 127, 1), project(psi, 3, 1))
                behind = get_half(lambda k: pltpu.roll(ld(q3, k, h), 1, 1))
            w = mat_half(matrix(u_ref, mu, h), ahead)
            if w_ref is not None:
                put_half(w_ref, h, w, mu * 12)
            total = map_half(lambda a, b: a + b, w, behind)
            delta = map_half(lambda a, b: a - b, w, behind)
            source, coef = GAMMA[mu]
            if acc is None:
                zero = jnp.zeros((8, 128), F32)
                acc = [total[0], total[1]] + [
                    [add_unit((zero, zero), delta[source[s]][c], coef[s], 1) for c in range(3)] for s in (2, 3)
                ]
            else:
                for s in range(2):
                    acc[s] = [cadd(acc[s][c], total[s][c]) for c in range(3)]
                for s in (2, 3):
                    acc[s] = [add_unit(acc[s][c], delta[source[s]][c], coef[s], 1) for c in range(3)]
        for s in range(4):
            for c in range(3):
                for part in range(2):
                    st(out_ref, part * 12 + c * 4 + s, h, psi[s][c][part] - HOPPING * acc[s][c][part])


def arrived_swap(info, t_a, t_b, x_a, x_b, mirror):
    def rows(ref, k):
        return ref[k * 4 : k * 4 + 4, :]

    return (
        lambda k, h: jnp.where(info.even_t, ld(t_a, k, h), ld(t_b, k, h)),
        lambda k, h: jnp.where(info.even_t, ld(t_b, k, h), ld(t_a, k, h)),
        lambda k: jnp.where(info.even_x, rows(x_a, k), rows(x_b, k)),
        lambda k: jnp.where(info.even_x, rows(x_b, k), rows(x_a, k)),
        lambda k: rows(mirror, k),
        lambda k: rows(mirror, 12 + k),
    )


def noise_kernel(table_i, partner, index, table, u, *rest):
    psi, t_a, t_b, x_a, x_b, mirror, q0, q2, q3, flat, parts, h0, h2 = rest
    info = Info(table_i, partner)
    for part in range(2):
        for c in range(3):
            flat[(part * 3 + c) * 4 : (part * 3 + c) * 4 + 4, :] = table[part, c]
    for hi in range(16):
        block = flat[:, hi * 256 : hi * 256 + 256]
        first = block.astype(jnp.bfloat16)
        left = block - first.astype(F32)
        second = left.astype(jnp.bfloat16)
        third = (left - second.astype(F32)).astype(jnp.bfloat16)
        for n, value in enumerate((first, second, third)):
            parts[hi * 24 : hi * 24 + 24, n * 256 : n * 256 + 256] = value
    low_iota = lax.broadcasted_iota(jnp.int32, (256, 128), 0)
    table_parts = parts[...]
    for r in range(16):
        wanted = index[r : r + 1, :]
        hot = jnp.where(low_iota == (wanted & 255), 1.0, 0.0).astype(jnp.bfloat16)
        found = jnp.dot(table_parts, jnp.concatenate([hot, hot, hot], axis=0), preferred_element_type=F32)
        high = jnp.broadcast_to(wanted >> 8, (24, 128))
        value = found[0:24]
        for hi in range(1, 16):
            value = jnp.where(high == hi, found[hi * 24 : hi * 24 + 24], value)
        psi[pl.ds(r, 24, stride=16), :] = value
    send_both(psi, u, info, t_a, t_b, x_a, x_b, mirror, q0, q2, q3, h0, h2)


def phi_kernel(table_i, partner, psi, u, q0, q2, q3, t_a, t_b, x_a, x_b, mirror, *rest):
    phi, o_ta, o_tb, o_xa, o_xb, o_m, o_q0, o_q2, o_q3, a0, b0, fa, fb, h0, h2 = rest
    info = Info(table_i, partner)
    arrived = arrived_swap(info, t_a, t_b, x_a, x_b, mirror)
    dirac(psi, u, arrived, q0, q2, q3, (a0, b0, fa, fb), phi, None)
    send_both(phi, u, info, o_ta, o_tb, o_xa, o_xb, o_m, o_q0, o_q2, o_q3, h0, h2)


def send_response(y, info, o_t, o_x, o_m, h2):
    for h in range(2):
        v = spinor(y, h)
        put_half(o_t, h, map_half(lambda a: a * info.sign_ahead, project(v, 1, -1)))
        put_half(h2, h, project(v, 2, -1))
        if h == 0:
            face = project(v, 0, -1)
            for t in range(2):
                for c in range(3):
                    for part in range(2):
                        k = half_index(part, t, c)
                        o_x[k * 4 : k * 4 + 4, :] = face[t][c][part][0:4]
    for k in range(12):
        send_rows(o_m, k, h2, k, info, 0)


def response_kernel(table_i, partner, phi, u, q0, q2, q3, t_a, t_b, x_a, x_b, mirror, *rest):
    y, w, o_t, o_x, o_m, a0, b0, fa, fb, h2 = rest
    info = Info(table_i, partner)
    arrived = arrived_swap(info, t_a, t_b, x_a, x_b, mirror)
    dirac(phi, u, arrived, q0, q2, q3, (a0, b0, fa, fb), y, w)
    send_response(y, info, o_t, o_x, o_m, h2)


def response2_kernel(table_i, partner, phi, u, q0, q2, q3, t_a, t_b, x_a, x_b, mirror, b_t, b_x, b_m, *rest):
    y, w, o_t, o_x, o_m, a0, b0, fa, fb, h2 = rest
    info = Info(table_i, partner)
    arrived = list(arrived_swap(info, t_a, t_b, x_a, x_b, mirror))
    arrived[1] = lambda k, h: ld(b_t, k, h)
    arrived[3] = lambda k: b_x[k * 4 : k * 4 + 4, :]
    arrived[5] = lambda k: b_m[k * 4 : k * 4 + 4, :]
    dirac(phi, u, arrived, q0, q2, q3, (a0, b0, fa, fb), y, w)
    send_response(y, info, o_t, o_x, o_m, h2)


OFF = ((0, 1), (0, 2), (1, 2))
EARLY = (0, 2, 3)


def force_values(left, right):
    def g_im(i, j):
        return sum(left[n][i][1] * right[n][j][0] - left[n][i][0] * right[n][j][1] for n in range(4))

    def g_re(i, j):
        return sum(left[n][i][0] * right[n][j][0] + left[n][i][1] * right[n][j][1] for n in range(4))

    d = [g_im(i, i) for i in range(3)]
    third = (d[0] + d[1] + d[2]) * (1.0 / 3.0)
    scale = -2.0 * HOPPING
    values = [scale * (d[0] - third), scale * (d[1] - third)]
    for i, j in OFF:
        values.append((0.5 * scale) * (g_im(i, j) + g_im(j, i)))
        values.append((0.5 * scale) * (g_re(j, i) - g_re(i, j)))
    return values


def force_at(at, phi, u, y, w, mu, x):
    ysp = [[(at(y, c * 4 + s), at(y, 12 + c * 4 + s)) for c in range(3)] for s in range(4)]
    psp = [[(at(phi, c * 4 + s), at(phi, 12 + c * 4 + s)) for c in range(3)] for s in range(4)]
    link = [[(at(u, mu * 18 + i * 3 + j), at(u, mu * 18 + 9 + i * 3 + j)) for j in range(3)] for i in range(3)]
    left = mat_half(link, x(ysp)) + get_half(lambda k: at(w, mu * 12 + k))
    right = project(psp, mu, -1) + project(ysp, mu, 1)
    return force_values(left, right)


def early_force_kernel(table_i, partner, phi, u, y, w, force, sent, a0):
    info = Info(table_i, partner)
    nothing = jnp.zeros((4, 128), F32)
    for k in range(12):
        a0[k * HALO + 16 : k * HALO + 20, :] = nothing
    for h in range(2):
        v = project(spinor(y, h), 0, -1)
        for t in range(2):
            for c in range(3):
                for part in range(2):
                    k = half_index(part, t, c)
                    a0[k * HALO + 8 * h : k * HALO + 8 * h + 8, :] = v[t][c][part]
    for h in range(2):
        for e, mu in enumerate(EARLY):
            if mu == 0:
                x = lambda ysp: get_half(lambda k: a0[k * HALO + 8 * h + 4 : k * HALO + 8 * h + 12, :])
            elif mu == 2:
                x = lambda ysp: map_half(lambda r: pltpu.roll(r, 7, 0), project(ysp, 2, -1))
            else:
                x = lambda ysp: map_half(lambda r: pltpu.roll(r, 127, 1), project(ysp, 3, -1))
            for n, value in enumerate(force_at(lambda ref, k: ld(ref, k, h), phi, u, y, w, mu, x)):
                st(force, e * 8 + n, h, value)
    for k in range(24):
        send_blocks(sent, k, force, k, info)


def send_blocks(dst, base, src, k, info):
    for j in range(4):
        at = pl.multiple_of(base * ROWS + 4 * info.partner[j], 4)
        dst[pl.ds(at, 4), :] = src[k * ROWS + 4 * j : k * ROWS + 4 * j + 4, :]


def late_force_kernel(table_i, partner, phi, u, y, w, r_t, r_x, r_m, f_t, f_x, f_m, sent):
    info = Info(table_i, partner)
    for h in range(2):
        arrived = get_half(lambda k: ld(r_t, k, h))
        for n, value in enumerate(force_at(lambda ref, k: ld(ref, k, h), phi, u, y, w, 1, lambda ysp: arrived)):
            st(f_t, n, h, value)
    for n in range(8):
        send_blocks(sent, n, f_t, n, info)
    face = lambda ref: get_half(lambda k: ref[k * 4 : k * 4 + 4, :])
    last_x = lambda ref, k: ref[k * ROWS + 12 : k * ROWS + 16, :]
    for n, value in enumerate(force_at(last_x, phi, u, y, w, 0, lambda ysp: face(r_x))):
        f_x[n * ROWS + 12 : n * ROWS + 16, :] = value
        sent[8 * ROWS + n * 4 : 8 * ROWS + n * 4 + 4, :] = value
    last_m = lambda ref, k: ref[pl.ds(k * ROWS + 3, 4, stride=4), :]
    for n, value in enumerate(force_at(last_m, phi, u, y, w, 2, lambda ysp: face(r_m))):
        f_m[pl.ds(n * ROWS + 3, 4, stride=4), :] = value
    for n in range(8):
        for j in range(4):
            row = 8 * ROWS + 32 + n * 4 + info.partner[j]
            sent[pl.ds(row, 1), :] = f_m[n * ROWS + 4 * j + 3 : n * ROWS + 4 * j + 4, :]


def place_faces(info, mirrored, m_x, m_m):
    block = jnp.int32(0)
    for j in range(4):
        block = block + jnp.where(info.partner[j] == 3, j, 0)
    for n in range(8):
        at = pl.multiple_of(n * ROWS + 4 * block, 4)
        m_x[pl.ds(at, 4), :] = mirrored[8 * ROWS + n * 4 : 8 * ROWS + n * 4 + 4, :]
        m_m[pl.ds(n * ROWS + 3, 4, stride=4), :] = mirrored[8 * ROWS + 32 + n * 4 : 8 * ROWS + 32 + n * 4 + 4, :]
    return block


def both_forces(mu, h, block, early, mirror_early, f_t, f_x, f_m, mirrored, m_x, m_m):
    row = lax.broadcasted_iota(jnp.int32, (8, 128), 0)
    if mu == 1:
        return (lambda n: ld(f_t, n, h)), (lambda n: ld(mirrored, n, h))
    if mu == 2:
        edge = (row & 3) == 3
        return (
            lambda n: jnp.where(edge, ld(f_m, n, h), ld(early, 8 + n, h)),
            lambda n: jnp.where(edge, ld(m_m, n, h), ld(mirror_early, 8 + n, h)),
        )
    edge = (row >> 2) + 2 * h == block
    if h == 0:
        here = lambda n: ld(early, n, h)
    else:
        here = lambda n: jnp.where(row >= 4, ld(f_x, n, h), ld(early, n, h))
    return here, (lambda n: jnp.where(edge, ld(m_x, n, h), ld(mirror_early, n, h)))


def updated_momenta(read, force, mirrored):
    diag_force = [force(n) - mirrored(n) for n in range(2)]
    diag_force.append(-(diag_force[0] + diag_force[1]))
    diag = [read(n) + STEP * diag_force[n] for n in range(3)]
    upper = []
    for n in range(3):
        re = force(2 + 2 * n) - mirrored(2 + 2 * n)
        im = force(3 + 2 * n) + mirrored(3 + 2 * n)
        upper.append((read(3 + 2 * n) + STEP * re, read(4 + 2 * n) + STEP * im))
    return diag, upper


def link_step(diag, upper, u):
    b = [STEP * value for value in diag]
    b01, b02, b12 = ((STEP * value[0], STEP * value[1]) for value in upper)
    n01, n02, n12 = (v[0] * v[0] + v[1] * v[1] for v in (b01, b02, b12))
    square_diag = [b[0] * b[0] + n01 + n02, b[1] * b[1] + n01 + n12, b[2] * b[2] + n02 + n12]

    def scaled(v, by):
        return (v[0] * by, v[1] * by)

    square = [
        cadd(scaled(b01, b[0] + b[1]), cmul_conj(b02, b12)),
        cadd(scaled(b02, b[0] + b[2]), cmul(b01, b12)),
        cadd(scaled(b12, b[1] + b[2]), cmul_conj(b02, b01)),
    ]
    c1 = 0.5 * (square_diag[0] + square_diag[1] + square_diag[2])
    triple = cmul_conj(cmul(b01, b12), b02)[0]
    c0 = b[0] * (b[1] * b[2] - n12) - b[1] * n02 - b[2] * n01 + 2.0 * triple
    one = jnp.ones_like(c1)
    zero = jnp.zeros_like(c1)
    r0, r1, r2 = (one, zero), (zero, zero), (zero, zero)
    for k in range(DEGREE, 0, -1):
        inv = 1.0 / k
        new0 = (1.0 + (r2[1] * c0) * inv, -(r2[0] * c0) * inv)
        new1 = ((r0[0] - r2[0] * c1) * inv, (r0[1] - r2[1] * c1) * inv)
        new2 = (r1[0] * inv, r1[1] * inv)
        r0, r1, r2 = new0, new1, new2
    ir1 = (-r1[1], r1[0])
    e = [[None] * 3 for _ in range(3)]
    for i in range(3):
        e[i][i] = cadd(r0, csub(scaled(ir1, b[i]), scaled(r2, square_diag[i])))
    for (i, j), v, s in zip(OFF, (b01, b02, b12), square):
        e[i][j] = csub(cmul(ir1, v), cmul(r2, s))
        e[j][i] = csub(cmul_conj(ir1, v), cmul_conj(r2, s))
    return [[cadd(cadd(cmul(e[i][0], u[0][j]), cmul(e[i][1], u[1][j])), cmul(e[i][2], u[2][j])) for j in range(3)] for i in range(3)]


def input_momentum(ref, mu, h):
    def read(n):
        if n < 3:
            return ld(ref, mu * 18 + 4 * n, h)
        i, j = OFF[(n - 3) // 2]
        return ld(ref, mu * 18 + 9 * ((n - 3) % 2) + 3 * i + j, h)

    return read


def put_matrix(ref, mu, h, value):
    for i in range(3):
        for j in range(3):
            for part in range(2):
                st(ref, mu * 18 + part * 9 + i * 3 + j, h, value[i][j][part])


def put_momenta(ref, base, h, diag, upper):
    for n in range(3):
        st(ref, base + n, h, diag[n])
        st(ref, base + 3 + 2 * n, h, upper[n][0])
        st(ref, base + 4 + 2 * n, h, upper[n][1])


def put_full_momenta(new_p, old_p, mu, h, diag, upper):
    for i in range(3):
        st(new_p, mu * 18 + 4 * i, h, diag[i])
        st(new_p, mu * 18 + 9 + 4 * i, h, ld(old_p, mu * 18 + 9 + 4 * i, h))
    for (i, j), v in zip(OFF, upper):
        st(new_p, mu * 18 + 3 * i + j, h, v[0])
        st(new_p, mu * 18 + 3 * j + i, h, v[0])
        st(new_p, mu * 18 + 9 + 3 * i + j, h, v[1])
        st(new_p, mu * 18 + 9 + 3 * j + i, h, -v[1])


def early_update_kernel(phi, u, p, early, mirror_early, new_u, new_p, q3):
    for h in range(2):
        force, mirrored = (lambda n: ld(early, 16 + n, h)), (lambda n: ld(mirror_early, 16 + n, h))
        diag, upper = updated_momenta(input_momentum(p, 3, h), force, mirrored)
        put_momenta(new_p, 0, h, diag, upper)
        link = link_step(diag, upper, matrix(u, 3, h))
        put_matrix(new_u, 0, h, link)
        put_half(q3, h, mat_dag_half(link, project(spinor(phi, h), 3, -1)))


def early_last_kernel(u, p, early, mirror_early, new_u, new_p):
    for h in range(2):
        force, mirrored = (lambda n: ld(early, 16 + n, h)), (lambda n: ld(mirror_early, 16 + n, h))
        diag, upper = updated_momenta(lambda n: ld(p, 27 + n, h), force, mirrored)
        put_momenta(new_p, 0, h, diag, upper)
        put_matrix(new_u, 0, h, link_step(diag, upper, matrix(u, 3, h)))


def update_kernel(table_i, partner, phi, u, p, u3, p3, *rest):
    forces = rest[:6]
    new_u, new_p, o_t, o_x, o_m, q0, q2, m_x, m_m = rest[6:]
    info = Info(table_i, partner)
    block = place_faces(info, forces[5], m_x, m_m)
    for h in range(2):
        psi = spinor(phi, h)
        for mu in range(3):
            diag, upper = updated_momenta(
                input_momentum(p, mu, h), *both_forces(mu, h, block, *forces, m_x, m_m)
            )
            put_momenta(new_p, mu * 9, h, diag, upper)
            link = link_step(diag, upper, matrix(u, mu, h))
            put_matrix(new_u, mu, h, link)
            back = mat_dag_half(link, project(psi, mu, -1))
            if mu == 1:
                put_half(o_t, h, map_half(lambda a: a * info.sign_behind, back))
            else:
                put_half({0: q0, 2: q2}[mu], h, back)
    new_u[54 * ROWS : 72 * ROWS, :] = u3[...]
    new_p[27 * ROWS : 36 * ROWS, :] = p3[...]
    for k in range(12):
        o_x[k * 4 : k * 4 + 4, :] = q0[k * ROWS + 12 : k * ROWS + 16, :]
        send_rows(o_m, k, q2, k, info, 3)


def last_kernel(table_i, partner, u, p, old_p, u3, p3, *rest):
    forces = rest[:6]
    new_u, new_p, m_x, m_m = rest[6:]
    info = Info(table_i, partner)
    block = place_faces(info, forces[5], m_x, m_m)
    for h in range(2):
        for mu in range(3):
            diag, upper = updated_momenta(
                lambda n: ld(p, mu * 9 + n, h), *both_forces(mu, h, block, *forces, m_x, m_m)
            )
            put_full_momenta(new_p, old_p, mu, h, diag, upper)
            put_matrix(new_u, mu, h, link_step(diag, upper, matrix(u, mu, h)))
        diag = [ld(p3, n, h) for n in range(3)]
        upper = [(ld(p3, 3 + 2 * n, h), ld(p3, 4 + 2 * n, h)) for n in range(3)]
        put_full_momenta(new_p, old_p, 3, h, diag, upper)
    new_u[54 * ROWS : 72 * ROWS, :] = u3[...]


VM = pl.BlockSpec(memory_space=pltpu.VMEM)
SM = pl.BlockSpec(memory_space=pltpu.SMEM)
FULL = ROWS * 12
FACE = 4 * 12


def call(kernel, n_scalar, args, outs, scratch, limit=4):
    return pl.pallas_call(
        kernel,
        out_shape=[jax.ShapeDtypeStruct((rows, 128), F32) for rows in outs],
        in_specs=[SM] * n_scalar + [VM] * (len(args) - n_scalar),
        out_specs=[VM] * len(outs),
        scratch_shapes=[s if not isinstance(s, int) else pltpu.VMEM((s, 128), F32) for s in scratch],
        compiler_params=pltpu.CompilerParams(vmem_limit_bytes=limit << 20),
    )(*args)


def swap(value, axis, far):
    n = lax.axis_size(axis)
    if far:
        pairs = [(i, (i + 1) % n if i % 2 else (i - 1) % n) for i in range(n)]
    else:
        pairs = [(i, i ^ 1) for i in range(n)]
    return lax.ppermute(value, axis, pairs)


def shift(value, axis, by):
    n = lax.axis_size(axis)
    return lax.ppermute(value, axis, [(i, (i + by) % n) for i in range(n)])


def mirror_swap(value):
    n = lax.axis_size("xd")
    return lax.ppermute(value, "xd", [(i, i ^ (n // 2)) for i in range(n)])


def moved(name, value):
    if name == "far_t":
        return swap(value, "ta", True)
    if name == "near_t":
        return swap(value, "ta", False)
    if name == "far_x":
        return swap(value, "xd", True)
    if name == "near_x":
        return swap(value, "xd", False)
    if name == "back_t":
        return shift(value, "ta", -1)
    if name == "back_x":
        return shift(value, "xd", -1)
    if name == "on_t":
        return shift(value, "ta", 1)
    if name == "on_x":
        return shift(value, "xd", 1)
    return mirror_swap(value)


SWAP_ORDER = ("far_t", "mirror", "far_x", "near_x", "near_t")
BACK_ORDER = ("back_t", "mirror", "back_x", "early")
ON_ORDER = ("on_t", "mirror", "on_x")


def exchange(order, **values):
    return {name: moved(name, values[name]) for name in order}


def swap_exchange(t_a, t_b, x_a, x_b, m):
    got = exchange(SWAP_ORDER, near_t=t_a, far_t=t_b, near_x=x_a, far_x=x_b, mirror=m)
    return [got[name] for name in ("near_t", "far_t", "near_x", "far_x", "mirror")]


def all_forces(s, phi, u, y, w, o_t, o_x, o_m):
    early, sent = call(early_force_kernel, 2, (*s, phi, u, y, w), [24 * ROWS, 24 * ROWS], [12 * HALO])
    got = exchange(BACK_ORDER, back_t=o_t, back_x=o_x, mirror=o_m, early=sent)
    f_t, f_x, f_m, sent = call(
        late_force_kernel,
        2,
        (*s, phi, u, y, w, got["back_t"], got["back_x"], got["mirror"]),
        [8 * ROWS, 8 * ROWS, 8 * ROWS, 12 * ROWS],
        [],
    )
    late = exchange(("mirror",), mirror=sent)["mirror"]
    return early, got["early"], f_t, f_x, f_m, late


def on_exchange(t, x, m):
    got = exchange(ON_ORDER, on_t=t, on_x=x, mirror=m)
    return [got[name] for name in ("on_t", "on_x", "mirror")]


def per_device(gauge_links, momenta, noise_table, noise_index, partner):
    ta = lax.axis_index("ta")
    xd = lax.axis_index("xd")
    lane = lax.iota(jnp.int32, 8)
    last = lax.axis_size("ta") - 1
    info = jnp.where(
        lane == 0,
        ta & 1,
        jnp.where(
            lane == 1,
            xd & 1,
            jnp.where(lane == 2, jnp.where(ta == 0, -1, 1), jnp.where(ta == last, -1, 1)),
        ),
    ).astype(jnp.int32)
    s = (info, partner)
    u = gauge_links.reshape(72 * ROWS, 128)
    p = momenta.reshape(72 * ROWS, 128)
    table = jnp.transpose(noise_table, (0, 2, 1, 3))
    index = noise_index.reshape(ROWS, 128)
    messages = [FULL, FULL, FACE, FACE, 2 * FACE]
    local = [FULL, FULL, FULL]
    halo = [12 * HALO, 12 * HALO, FULL, FULL]
    spin = 24 * ROWS

    psi, *rest = call(
        noise_kernel,
        2,
        (*s, index, table, u),
        [spin] + messages + local,
        [pltpu.VMEM((24, 4096), F32), pltpu.VMEM((384, 768), jnp.bfloat16), FULL, FULL],
        12,
    )
    arrived = swap_exchange(*rest[:5])
    phi, *rest = call(phi_kernel, 2, (*s, psi, u, *rest[5:], *arrived), [spin] + messages + local, halo + [FULL, FULL])
    arrived = swap_exchange(*rest[:5])
    y, w, o_t, o_x, o_m = call(
        response_kernel, 2, (*s, phi, u, *rest[5:], *arrived), [spin, 4 * FULL, FULL, FACE, FACE], halo + [FULL]
    )
    forces = all_forces(s, phi, u, y, w, o_t, o_x, o_m)
    u3, p3, q3 = call(early_update_kernel, 0, (phi, u, p, *forces[:2]), [18 * ROWS, 9 * ROWS, FULL], [])
    u, p1, o_t, o_x, o_m, q0, q2 = call(
        update_kernel,
        2,
        (*s, phi, u, p, u3, p3, *forces),
        [72 * ROWS, 36 * ROWS, FULL, FACE, FACE, FULL, FULL],
        [8 * ROWS, 8 * ROWS],
    )
    y, w, o_t, o_x, o_m = call(
        response2_kernel,
        2,
        (*s, phi, u, q0, q2, q3, *arrived, *on_exchange(o_t, o_x, o_m)),
        [spin, 4 * FULL, FULL, FACE, FACE],
        halo + [FULL],
    )
    forces = all_forces(s, phi, u, y, w, o_t, o_x, o_m)
    u3, p3 = call(early_last_kernel, 0, (u, p1, *forces[:2]), [18 * ROWS, 9 * ROWS], [])
    new_u, new_p = call(last_kernel, 2, (*s, u, p1, p, u3, p3, *forces), [72 * ROWS, 72 * ROWS], [8 * ROWS, 8 * ROWS])
    return new_u.reshape(gauge_links.shape), new_p.reshape(momenta.shape)


def solution(mesh):
    sites = P(None, None, None, None, "xd", "ta", None, None)
    return jax.shard_map(
        per_device,
        mesh=mesh,
        in_specs=(sites, sites, P(), P("xd", "ta", None, None), P("xd")),
        out_specs=(sites, sites),
        check_vma=False,
    )
```

```python
import jax
import jax.numpy as jnp
from jax import lax
from jax.experimental import pallas as pl
from jax.experimental.pallas import tpu as pltpu
from jax.sharding import PartitionSpec as P


HOPPING = 0.13
STEP = 0.25
DEGREE = 6
F32 = jnp.float32
GAMMA = (
    ((3, 2, 1, 0), ((0, 1), (0, 1), (0, -1), (0, -1))),
    ((2, 3, 0, 1), ((1, 0), (1, 0), (1, 0), (1, 0))),
    ((3, 2, 1, 0), ((-1, 0), (1, 0), (1, 0), (-1, 0))),
    ((2, 3, 0, 1), ((0, 1), (0, -1), (0, -1), (0, 1))),
)
ROWS = 16
HALO = 24


def ld(ref, k, h):
    return ref[k * ROWS + 8 * h : k * ROWS + 8 * h + 8, :]


def st(ref, k, h, value):
    ref[k * ROWS + 8 * h : k * ROWS + 8 * h + 8, :] = value


def cadd(a, b):
    return (a[0] + b[0], a[1] + b[1])


def csub(a, b):
    return (a[0] - b[0], a[1] - b[1])


def cmul(a, b):
    return (a[0] * b[0] - a[1] * b[1], a[0] * b[1] + a[1] * b[0])


def cmul_conj(a, b):
    return (a[0] * b[0] + a[1] * b[1], a[1] * b[0] - a[0] * b[1])


def add_unit(x, y, coef, sign):
    re, im = coef
    if re:
        if re * sign > 0:
            return cadd(x, y)
        return csub(x, y)
    if im * sign > 0:
        return (x[0] - y[1], x[1] + y[0])
    return (x[0] + y[1], x[1] - y[0])


def spinor(ref, h):
    return [[(ld(ref, c * 4 + s, h), ld(ref, 12 + c * 4 + s, h)) for c in range(3)] for s in range(4)]


def project(psi, mu, sign):
    source, coef = GAMMA[mu]
    return [[add_unit(psi[t][c], psi[source[t]][c], coef[t], sign) for c in range(3)] for t in range(2)]


def matrix(ref, mu, h):
    return [[(ld(ref, mu * 18 + i * 3 + j, h), ld(ref, mu * 18 + 9 + i * 3 + j, h)) for j in range(3)] for i in range(3)]


def mat_half(u, v):
    out = []
    for t in range(2):
        row = []
        for i in range(3):
            acc = cmul(u[i][0], v[t][0])
            for j in (1, 2):
                acc = cadd(acc, cmul(u[i][j], v[t][j]))
            row.append(acc)
        out.append(row)
    return out


def mat_dag_half(u, v):
    out = []
    for t in range(2):
        row = []
        for i in range(3):
            acc = cmul_conj(v[t][0], u[0][i])
            for j in (1, 2):
                acc = cadd(acc, cmul_conj(v[t][j], u[j][i]))
            row.append(acc)
        out.append(row)
    return out


def half_index(part, t, c):
    return part * 6 + t * 3 + c


def put_half(ref, h, v, base=0):
    for t in range(2):
        for c in range(3):
            for part in range(2):
                st(ref, base + half_index(part, t, c), h, v[t][c][part])


def get_half(fn):
    return [[tuple(fn(half_index(part, t, c)) for part in range(2)) for c in range(3)] for t in range(2)]


def map_half(fn, *vs):
    return [[tuple(fn(*(v[t][c][part] for v in vs)) for part in range(2)) for c in range(3)] for t in range(2)]


INFO_ROWS = 64


class Info:
    def __init__(self, info):
        self.even_t = info[24:32, :] == 0
        self.even_x = info[32:36, :] == 0
        self.sign_ahead = info[40:48, :].astype(F32)
        self.sign_behind = info[48:56, :].astype(F32)
        self.face_source = [info[16:20, :] == j for j in range(4)]
        self.edge_block = info[56:64, :]
        half = row_block()
        self.block_source = []
        for h in range(2):
            source = info[8 * h : 8 * h + 8, :]
            self.block_source.append((source == half, source == 1 - half, source == 2 + half))


def row_block():
    return lax.broadcasted_iota(jnp.int32, (8, 128), 0) >> 2


def write_info(info, odd_t, odd_x, sign_ahead, sign_behind, partner):
    row = lax.broadcasted_iota(jnp.int32, (8, 128), 0)

    def source_of(target):
        value = jnp.zeros((8, 128), jnp.int32)
        for j in range(4):
            value = jnp.where(target == partner[j], j, value)
        return value

    info[0:8, :] = source_of(row >> 2)
    info[8:16, :] = source_of(2 + (row >> 2))
    info[16:24, :] = source_of(row & 3)
    edge = jnp.int32(0)
    for j in range(4):
        edge = edge + jnp.where(partner[j] == 3, j, 0)
    for n, value in enumerate((odd_t, odd_x, sign_ahead, sign_behind, edge)):
        info[24 + 8 * n : 32 + 8 * n, :] = jnp.full((8, 128), value, jnp.int32)


def row_in_pair():
    return lax.broadcasted_iota(jnp.int32, (8, 128), 0) & 3


def send_rows(dst, base, src, k, info, row):
    def spread(j):
        at = k * ROWS + 4 * j + row
        return jnp.broadcast_to(src[at : at + 1, :], (4, 128))

    value = spread(0)
    for j in range(1, 4):
        value = jnp.where(info.face_source[j], spread(j), value)
    dst[base * 4 : base * 4 + 4, :] = value


def send_both(psi_ref, u_ref, info, t_a, t_b, x_a, x_b, mirror, q0, q2, q3, h0, h2):
    for h in range(2):
        psi = spinor(psi_ref, h)
        front = map_half(lambda a: a * info.sign_ahead, project(psi, 1, 1))
        back = map_half(
            lambda a: a * info.sign_behind, mat_dag_half(matrix(u_ref, 1, h), project(psi, 1, -1))
        )
        put_half(t_a, h, map_half(lambda a, b: jnp.where(info.even_t, b, a), front, back))
        put_half(t_b, h, map_half(lambda a, b: jnp.where(info.even_t, a, b), front, back))
        put_half(h0, h, project(psi, 0, 1))
        put_half(h2, h, project(psi, 2, 1))
        for mu, ref in ((0, q0), (2, q2), (3, q3)):
            put_half(ref, h, mat_dag_half(matrix(u_ref, mu, h), project(psi, mu, -1)))
    for k in range(12):
        front = h0[k * ROWS : k * ROWS + 4, :]
        back = q0[k * ROWS + 12 : k * ROWS + 16, :]
        x_a[k * 4 : k * 4 + 4, :] = jnp.where(info.even_x, back, front)
        x_b[k * 4 : k * 4 + 4, :] = jnp.where(info.even_x, front, back)
        send_rows(mirror, k, h2, k, info, 0)
        send_rows(mirror, 12 + k, q2, k, info, 3)


def dirac(psi_ref, u_ref, arrived, q0, q2, q3, scratch, out_ref, w_ref):
    ahead_t, behind_t, ahead_x, behind_x, ahead_m, behind_m = arrived
    a0, b0, fa, fb = scratch
    for k in range(12):
        a0[k * HALO + 16 : k * HALO + 20, :] = ahead_x(k)
        b0[k * HALO : k * HALO + 4, :] = behind_x(k)
        b0[k * HALO + 4 : k * HALO + 20, :] = q0[k * ROWS : k * ROWS + 16, :]
        fa[pl.ds(k * ROWS + 3, 4, stride=4), :] = ahead_m(k)
        fb[pl.ds(k * ROWS, 4, stride=4), :] = behind_m(k)
    for h in range(2):
        v = project(spinor(psi_ref, h), 0, 1)
        for t in range(2):
            for c in range(3):
                for part in range(2):
                    k = half_index(part, t, c)
                    a0[k * HALO + 8 * h : k * HALO + 8 * h + 8, :] = v[t][c][part]
    x2 = row_in_pair()
    for h in range(2):
        psi = spinor(psi_ref, h)
        acc = None
        for mu in range(4):
            if mu == 0:
                ahead = get_half(lambda k: a0[k * HALO + 8 * h + 4 : k * HALO + 8 * h + 12, :])
                behind = get_half(lambda k: b0[k * HALO + 8 * h : k * HALO + 8 * h + 8, :])
            elif mu == 1:
                ahead = get_half(lambda k: ahead_t(k, h))
                behind = get_half(lambda k: behind_t(k, h))
            elif mu == 2:
                raw = project(psi, 2, 1)
                face = get_half(lambda k: ld(fa, k, h))
                ahead = map_half(lambda r, f: jnp.where(x2 == 3, f, pltpu.roll(r, 7, 0)), raw, face)
                behind = get_half(lambda k: jnp.where(x2 == 0, ld(fb, k, h), pltpu.roll(ld(q2, k, h), 1, 0)))
            else:
                ahead = map_half(lambda r: pltpu.roll(r, 127, 1), project(psi, 3, 1))
                behind = get_half(lambda k: pltpu.roll(ld(q3, k, h), 1, 1))
            w = mat_half(matrix(u_ref, mu, h), ahead)
            if w_ref is not None:
                put_half(w_ref, h, w, mu * 12)
            total = map_half(lambda a, b: a + b, w, behind)
            delta = map_half(lambda a, b: a - b, w, behind)
            source, coef = GAMMA[mu]
            if acc is None:
                zero = jnp.zeros((8, 128), F32)
                acc = [total[0], total[1]] + [
                    [add_unit((zero, zero), delta[source[s]][c], coef[s], 1) for c in range(3)] for s in (2, 3)
                ]
            else:
                for s in range(2):
                    acc[s] = [cadd(acc[s][c], total[s][c]) for c in range(3)]
                for s in (2, 3):
                    acc[s] = [add_unit(acc[s][c], delta[source[s]][c], coef[s], 1) for c in range(3)]
        for s in range(4):
            for c in range(3):
                for part in range(2):
                    st(out_ref, part * 12 + c * 4 + s, h, psi[s][c][part] - HOPPING * acc[s][c][part])


def arrived_swap(info, t_a, t_b, x_a, x_b, mirror):
    def rows(ref, k):
        return ref[k * 4 : k * 4 + 4, :]

    return (
        lambda k, h: jnp.where(info.even_t, ld(t_a, k, h), ld(t_b, k, h)),
        lambda k, h: jnp.where(info.even_t, ld(t_b, k, h), ld(t_a, k, h)),
        lambda k: jnp.where(info.even_x, rows(x_a, k), rows(x_b, k)),
        lambda k: jnp.where(info.even_x, rows(x_b, k), rows(x_a, k)),
        lambda k: rows(mirror, k),
        lambda k: rows(mirror, 12 + k),
    )


def noise_kernel(table_i_hbm, partner_hbm, index_hbm, table_hbm, u_hbm, *rest):
    psi, t_a, t_b, x_a, x_b, mirror, q0, q2, q3, info_ref = rest[:10]
    flat, parts, h0, h2, table, u, index, table_i, partner, sems = rest[10:]
    copies = [
        pltpu.make_async_copy(src, dst, sems.at[n])
        for n, (src, dst) in enumerate(
            (
                (index_hbm, index),
                (table_hbm, table),
                (table_i_hbm, table_i),
                (partner_hbm, partner),
                (u_hbm, u),
            )
        )
    ]
    for copy in copies:
        copy.start()
    copies[1].wait()
    for part in range(2):
        for c in range(3):
            flat[(part * 3 + c) * 4 : (part * 3 + c) * 4 + 4, :] = table[part, c]
    for hi in range(16):
        block = flat[:, hi * 256 : hi * 256 + 256]
        first = block.astype(jnp.bfloat16)
        left = block - first.astype(F32)
        second = left.astype(jnp.bfloat16)
        third = (left - second.astype(F32)).astype(jnp.bfloat16)
        for n, value in enumerate((first, second, third)):
            parts[hi * 24 : hi * 24 + 24, n * 256 : n * 256 + 256] = value
    copies[0].wait()
    low_iota = lax.broadcasted_iota(jnp.int32, (256, 128), 0)
    table_parts = parts[...]
    for r in range(0, 16, 2):
        wanted = [index[r + n : r + n + 1, :] for n in range(2)]
        hot = jnp.concatenate(
            [jnp.where(low_iota == (w & 255), 1.0, 0.0).astype(jnp.bfloat16) for w in wanted], axis=1
        )
        found = jnp.dot(table_parts, jnp.concatenate([hot, hot, hot], axis=0), preferred_element_type=F32)
        for n in range(2):
            high = jnp.broadcast_to(wanted[n] >> 8, (24, 128))
            value = found[0:24, 128 * n : 128 * n + 128]
            for hi in range(1, 16):
                value = jnp.where(high == hi, found[hi * 24 : hi * 24 + 24, 128 * n : 128 * n + 128], value)
            psi[pl.ds(r + n, 24, stride=16), :] = value
    copies[2].wait()
    copies[3].wait()
    write_info(info_ref, *(table_i[n] for n in range(4)), [partner[j] & 3 for j in range(4)])
    info = Info(info_ref)
    copies[4].wait()
    send_both(psi, u, info, t_a, t_b, x_a, x_b, mirror, q0, q2, q3, h0, h2)


def phi_kernel(info_ref, psi, u, q0, q2, q3, t_a, t_b, x_a, x_b, mirror, *rest):
    phi, o_ta, o_tb, o_xa, o_xb, o_m, o_q0, o_q2, o_q3, a0, b0, fa, fb, h0, h2 = rest
    info = Info(info_ref)
    arrived = arrived_swap(info, t_a, t_b, x_a, x_b, mirror)
    dirac(psi, u, arrived, q0, q2, q3, (a0, b0, fa, fb), phi, None)
    send_both(phi, u, info, o_ta, o_tb, o_xa, o_xb, o_m, o_q0, o_q2, o_q3, h0, h2)


def send_response(y, info, o_t, o_x, o_m, h2):
    for h in range(2):
        v = spinor(y, h)
        put_half(o_t, h, map_half(lambda a: a * info.sign_ahead, project(v, 1, -1)))
        put_half(h2, h, project(v, 2, -1))
        if h == 0:
            face = project(v, 0, -1)
            for t in range(2):
                for c in range(3):
                    for part in range(2):
                        k = half_index(part, t, c)
                        o_x[k * 4 : k * 4 + 4, :] = face[t][c][part][0:4]
    for k in range(12):
        send_rows(o_m, k, h2, k, info, 0)


def response_kernel(info_ref, phi, u, q0, q2, q3, t_a, t_b, x_a, x_b, mirror, *rest):
    y, w, o_t, o_x, o_m, a0, b0, fa, fb, h2 = rest
    info = Info(info_ref)
    arrived = arrived_swap(info, t_a, t_b, x_a, x_b, mirror)
    dirac(phi, u, arrived, q0, q2, q3, (a0, b0, fa, fb), y, w)
    send_response(y, info, o_t, o_x, o_m, h2)


def response2_kernel(info_ref, phi, u, q0, q2, q3, t_a, t_b, x_a, x_b, mirror, b_t, b_x, b_m, *rest):
    y, w, o_t, o_x, o_m, a0, b0, fa, fb, h2 = rest
    info = Info(info_ref)
    arrived = list(arrived_swap(info, t_a, t_b, x_a, x_b, mirror))
    arrived[1] = lambda k, h: ld(b_t, k, h)
    arrived[3] = lambda k: b_x[k * 4 : k * 4 + 4, :]
    arrived[5] = lambda k: b_m[k * 4 : k * 4 + 4, :]
    dirac(phi, u, arrived, q0, q2, q3, (a0, b0, fa, fb), y, w)
    send_response(y, info, o_t, o_x, o_m, h2)


OFF = ((0, 1), (0, 2), (1, 2))
EARLY = (0, 2, 3)


def force_values(left, right):
    def g_im(i, j):
        return sum(left[n][i][1] * right[n][j][0] - left[n][i][0] * right[n][j][1] for n in range(4))

    def g_re(i, j):
        return sum(left[n][i][0] * right[n][j][0] + left[n][i][1] * right[n][j][1] for n in range(4))

    d = [g_im(i, i) for i in range(3)]
    third = (d[0] + d[1] + d[2]) * (1.0 / 3.0)
    scale = -2.0 * HOPPING
    values = [scale * (d[0] - third), scale * (d[1] - third)]
    for i, j in OFF:
        values.append((0.5 * scale) * (g_im(i, j) + g_im(j, i)))
        values.append((0.5 * scale) * (g_re(j, i) - g_re(i, j)))
    return values


def force_at(at, phi, u, y, w, mu, x):
    ysp = [[(at(y, c * 4 + s), at(y, 12 + c * 4 + s)) for c in range(3)] for s in range(4)]
    psp = [[(at(phi, c * 4 + s), at(phi, 12 + c * 4 + s)) for c in range(3)] for s in range(4)]
    link = [[(at(u, mu * 18 + i * 3 + j), at(u, mu * 18 + 9 + i * 3 + j)) for j in range(3)] for i in range(3)]
    left = mat_half(link, x(ysp)) + get_half(lambda k: at(w, mu * 12 + k))
    right = project(psp, mu, -1) + project(ysp, mu, 1)
    return force_values(left, right)


def early_force_kernel(info_ref, phi, u, y, w, force, sent, a0):
    info = Info(info_ref)
    nothing = jnp.zeros((4, 128), F32)
    for k in range(12):
        a0[k * HALO + 16 : k * HALO + 20, :] = nothing
    for h in range(2):
        v = project(spinor(y, h), 0, -1)
        for t in range(2):
            for c in range(3):
                for part in range(2):
                    k = half_index(part, t, c)
                    a0[k * HALO + 8 * h : k * HALO + 8 * h + 8, :] = v[t][c][part]
    for h in range(2):
        for e, mu in enumerate(EARLY):
            if mu == 0:
                x = lambda ysp: get_half(lambda k: a0[k * HALO + 8 * h + 4 : k * HALO + 8 * h + 12, :])
            elif mu == 2:
                x = lambda ysp: map_half(lambda r: pltpu.roll(r, 7, 0), project(ysp, 2, -1))
            else:
                x = lambda ysp: map_half(lambda r: pltpu.roll(r, 127, 1), project(ysp, 3, -1))
            for n, value in enumerate(force_at(lambda ref, k: ld(ref, k, h), phi, u, y, w, mu, x)):
                st(force, e * 8 + n, h, value)
    for k in range(24):
        send_blocks(sent, k, force, k, info)


def send_blocks(dst, base, src, k, info):
    low, high = ld(src, k, 0), ld(src, k, 1)
    low_turned, high_turned = pltpu.roll(low, 4, 0), pltpu.roll(high, 4, 0)
    for h in range(2):
        first, second, third = info.block_source[h]
        value = jnp.where(third, high, high_turned)
        value = jnp.where(second, low_turned, value)
        st(dst, base, h, jnp.where(first, low, value))


def late_force_kernel(info_ref, phi, u, y, w, r_t, r_x, r_m, f_t, f_x, f_m, sent):
    info = Info(info_ref)
    for h in range(2):
        arrived = get_half(lambda k: ld(r_t, k, h))
        for n, value in enumerate(force_at(lambda ref, k: ld(ref, k, h), phi, u, y, w, 1, lambda ysp: arrived)):
            st(f_t, n, h, value)
    for n in range(8):
        send_blocks(sent, n, f_t, n, info)
    face = lambda ref: get_half(lambda k: ref[k * 4 : k * 4 + 4, :])
    last_x = lambda ref, k: ref[k * ROWS + 12 : k * ROWS + 16, :]
    for n, value in enumerate(force_at(last_x, phi, u, y, w, 0, lambda ysp: face(r_x))):
        f_x[n * ROWS + 12 : n * ROWS + 16, :] = value
        sent[8 * ROWS + n * 4 : 8 * ROWS + n * 4 + 4, :] = value
    last_m = lambda ref, k: ref[pl.ds(k * ROWS + 3, 4, stride=4), :]
    for n, value in enumerate(force_at(last_m, phi, u, y, w, 2, lambda ysp: face(r_m))):
        f_m[pl.ds(n * ROWS + 3, 4, stride=4), :] = value
    for n in range(8):
        send_rows(sent, 40 + n, f_m, n, info, 3)


def place_faces(mirrored, m_x, m_m):
    for n in range(8):
        face = mirrored[8 * ROWS + n * 4 : 8 * ROWS + n * 4 + 4, :]
        for j in range(4):
            m_x[n * ROWS + 4 * j : n * ROWS + 4 * j + 4, :] = face
        m_m[pl.ds(n * ROWS + 3, 4, stride=4), :] = mirrored[8 * ROWS + 32 + n * 4 : 8 * ROWS + 32 + n * 4 + 4, :]


def both_forces(mu, h, block, early, mirror_early, f_t, f_x, f_m, mirrored, m_x, m_m):
    row = lax.broadcasted_iota(jnp.int32, (8, 128), 0)
    if mu == 1:
        return (lambda n: ld(f_t, n, h)), (lambda n: ld(mirrored, n, h))
    if mu == 2:
        edge = (row & 3) == 3
        return (
            lambda n: jnp.where(edge, ld(f_m, n, h), ld(early, 8 + n, h)),
            lambda n: jnp.where(edge, ld(m_m, n, h), ld(mirror_early, 8 + n, h)),
        )
    edge = (row >> 2) + 2 * h == block
    if h == 0:
        here = lambda n: ld(early, n, h)
    else:
        here = lambda n: jnp.where(row >= 4, ld(f_x, n, h), ld(early, n, h))
    return here, (lambda n: jnp.where(edge, ld(m_x, n, h), ld(mirror_early, n, h)))


def updated_momenta(read, force, mirrored):
    diag_force = [force(n) - mirrored(n) for n in range(2)]
    diag_force.append(-(diag_force[0] + diag_force[1]))
    diag = [read(n) + STEP * diag_force[n] for n in range(3)]
    upper = []
    for n in range(3):
        re = force(2 + 2 * n) - mirrored(2 + 2 * n)
        im = force(3 + 2 * n) + mirrored(3 + 2 * n)
        upper.append((read(3 + 2 * n) + STEP * re, read(4 + 2 * n) + STEP * im))
    return diag, upper


def link_step(diag, upper, u):
    b = [STEP * value for value in diag]
    b01, b02, b12 = ((STEP * value[0], STEP * value[1]) for value in upper)
    n01, n02, n12 = (v[0] * v[0] + v[1] * v[1] for v in (b01, b02, b12))
    square_diag = [b[0] * b[0] + n01 + n02, b[1] * b[1] + n01 + n12, b[2] * b[2] + n02 + n12]

    def scaled(v, by):
        return (v[0] * by, v[1] * by)

    square = [
        cadd(scaled(b01, b[0] + b[1]), cmul_conj(b02, b12)),
        cadd(scaled(b02, b[0] + b[2]), cmul(b01, b12)),
        cadd(scaled(b12, b[1] + b[2]), cmul_conj(b02, b01)),
    ]
    c1 = 0.5 * (square_diag[0] + square_diag[1] + square_diag[2])
    triple = cmul_conj(cmul(b01, b12), b02)[0]
    c0 = b[0] * (b[1] * b[2] - n12) - b[1] * n02 - b[2] * n01 + 2.0 * triple
    one = jnp.ones_like(c1)
    zero = jnp.zeros_like(c1)
    r0, r1, r2 = (one, zero), (zero, zero), (zero, zero)
    for k in range(DEGREE, 0, -1):
        inv = 1.0 / k
        new0 = (1.0 + (r2[1] * c0) * inv, -(r2[0] * c0) * inv)
        new1 = ((r0[0] - r2[0] * c1) * inv, (r0[1] - r2[1] * c1) * inv)
        new2 = (r1[0] * inv, r1[1] * inv)
        r0, r1, r2 = new0, new1, new2
    ir1 = (-r1[1], r1[0])
    e = [[None] * 3 for _ in range(3)]
    for i in range(3):
        e[i][i] = cadd(r0, csub(scaled(ir1, b[i]), scaled(r2, square_diag[i])))
    for (i, j), v, s in zip(OFF, (b01, b02, b12), square):
        e[i][j] = csub(cmul(ir1, v), cmul(r2, s))
        e[j][i] = csub(cmul_conj(ir1, v), cmul_conj(r2, s))
    return [[cadd(cadd(cmul(e[i][0], u[0][j]), cmul(e[i][1], u[1][j])), cmul(e[i][2], u[2][j])) for j in range(3)] for i in range(3)]


def input_momentum(ref, mu, h):
    def read(n):
        if n < 3:
            return ld(ref, mu * 18 + 4 * n, h)
        i, j = OFF[(n - 3) // 2]
        return ld(ref, mu * 18 + 9 * ((n - 3) % 2) + 3 * i + j, h)

    return read


def put_matrix(ref, mu, h, value):
    for i in range(3):
        for j in range(3):
            for part in range(2):
                st(ref, mu * 18 + part * 9 + i * 3 + j, h, value[i][j][part])


def put_momenta(ref, base, h, diag, upper):
    for n in range(3):
        st(ref, base + n, h, diag[n])
        st(ref, base + 3 + 2 * n, h, upper[n][0])
        st(ref, base + 4 + 2 * n, h, upper[n][1])


def put_full_momenta(new_p, old_p, at, mu, h, diag, upper):
    for i in range(3):
        st(new_p, at * 18 + 4 * i, h, diag[i])
        st(new_p, at * 18 + 9 + 4 * i, h, ld(old_p, mu * 18 + 9 + 4 * i, h))
    for (i, j), v in zip(OFF, upper):
        st(new_p, at * 18 + 3 * i + j, h, v[0])
        st(new_p, at * 18 + 3 * j + i, h, v[0])
        st(new_p, at * 18 + 9 + 3 * i + j, h, v[1])
        st(new_p, at * 18 + 9 + 3 * j + i, h, -v[1])


def early_update_kernel(phi, u, p, early, mirror_early, new_u, new_p, q3):
    for h in range(2):
        force, mirrored = (lambda n: ld(early, 16 + n, h)), (lambda n: ld(mirror_early, 16 + n, h))
        diag, upper = updated_momenta(input_momentum(p, 3, h), force, mirrored)
        put_momenta(new_p, 0, h, diag, upper)
        link = link_step(diag, upper, matrix(u, 3, h))
        put_matrix(new_u, 0, h, link)
        put_half(q3, h, mat_dag_half(link, project(spinor(phi, h), 3, -1)))


def early_last_kernel(u, p, old_p, early, mirror_early, new_u, new_p):
    for h in range(2):
        force, mirrored = (lambda n: ld(early, 16 + n, h)), (lambda n: ld(mirror_early, 16 + n, h))
        diag, upper = updated_momenta(lambda n: ld(p, 27 + n, h), force, mirrored)
        put_full_momenta(new_p, old_p, 0, 3, h, diag, upper)
        put_matrix(new_u, 0, h, link_step(diag, upper, matrix(u, 3, h)))


def update_kernel(info_ref, phi, u, p, u3, p3, *rest):
    forces = rest[:6]
    new_u, new_p, o_t, o_x, o_m, q0, q2, m_x, m_m = rest[6:]
    info = Info(info_ref)
    place_faces(forces[5], m_x, m_m)
    for h in range(2):
        psi = spinor(phi, h)
        for mu in range(3):
            diag, upper = updated_momenta(
                input_momentum(p, mu, h), *both_forces(mu, h, info.edge_block, *forces, m_x, m_m)
            )
            put_momenta(new_p, mu * 9, h, diag, upper)
            link = link_step(diag, upper, matrix(u, mu, h))
            put_matrix(new_u, mu, h, link)
            back = mat_dag_half(link, project(psi, mu, -1))
            if mu == 1:
                put_half(o_t, h, map_half(lambda a: a * info.sign_behind, back))
            else:
                put_half({0: q0, 2: q2}[mu], h, back)
    new_u[54 * ROWS : 72 * ROWS, :] = u3[...]
    new_p[27 * ROWS : 36 * ROWS, :] = p3[...]
    for k in range(12):
        o_x[k * 4 : k * 4 + 4, :] = q0[k * ROWS + 12 : k * ROWS + 16, :]
        send_rows(o_m, k, q2, k, info, 3)


def last_kernel(info_ref, u, p, old_p, u3, p3, *rest):
    forces = rest[:6]
    out_u, out_p, new_u, new_p, m_x, m_m, sems = rest[6:]
    info = Info(info_ref)
    size = 18 * ROWS
    copies = []

    def send(src, dst, mu):
        copies.append(pltpu.make_async_copy(src, dst.at[mu * size : mu * size + size, :], sems.at[len(copies)]))
        copies[-1].start()

    send(u3, out_u, 3)
    send(p3, out_p, 3)
    place_faces(forces[5], m_x, m_m)
    for mu in range(3):
        for h in range(2):
            diag, upper = updated_momenta(
                lambda n: ld(p, mu * 9 + n, h), *both_forces(mu, h, info.edge_block, *forces, m_x, m_m)
            )
            put_full_momenta(new_p, old_p, mu, mu, h, diag, upper)
            put_matrix(new_u, mu, h, link_step(diag, upper, matrix(u, mu, h)))
        send(new_p.at[mu * size : mu * size + size, :], out_p, mu)
        send(new_u.at[mu * size : mu * size + size, :], out_u, mu)
    for copy in copies:
        copy.wait()


VM = pl.BlockSpec(memory_space=pltpu.VMEM)
HBM = pl.BlockSpec(memory_space=pltpu.HBM)
FULL = ROWS * 12
FACE = 4 * 12


def call(kernel, args, outs, scratch, limit=4, from_hbm=False, to_hbm=False):
    return pl.pallas_call(
        kernel,
        out_shape=[jax.ShapeDtypeStruct((s, 128), F32) if isinstance(s, int) else s for s in outs],
        in_specs=[HBM if from_hbm else VM] * len(args),
        out_specs=[HBM if to_hbm else VM] * len(outs),
        scratch_shapes=[s if not isinstance(s, int) else pltpu.VMEM((s, 128), F32) for s in scratch],
        compiler_params=pltpu.CompilerParams(vmem_limit_bytes=limit << 20),
    )(*args)


def swap(value, axis, far):
    n = lax.axis_size(axis)
    if far:
        pairs = [(i, (i + 1) % n if i % 2 else (i - 1) % n) for i in range(n)]
    else:
        pairs = [(i, i ^ 1) for i in range(n)]
    return lax.ppermute(value, axis, pairs)


def shift(value, axis, by):
    n = lax.axis_size(axis)
    return lax.ppermute(value, axis, [(i, (i + by) % n) for i in range(n)])


def mirror_swap(value):
    n = lax.axis_size("xd")
    return lax.ppermute(value, "xd", [(i, i ^ (n // 2)) for i in range(n)])


def moved(name, value):
    if name == "far_t":
        return swap(value, "ta", True)
    if name == "near_t":
        return swap(value, "ta", False)
    if name == "far_x":
        return swap(value, "xd", True)
    if name == "near_x":
        return swap(value, "xd", False)
    if name == "back_t":
        return shift(value, "ta", -1)
    if name == "back_x":
        return shift(value, "xd", -1)
    if name == "on_t":
        return shift(value, "ta", 1)
    if name == "on_x":
        return shift(value, "xd", 1)
    return mirror_swap(value)


SWAP_ORDER = ("far_t", "mirror", "far_x", "near_x", "near_t")
BACK_ORDER = ("back_t", "mirror", "back_x", "early")
ON_ORDER = ("on_t", "mirror", "on_x")


def exchange(order, **values):
    return {name: moved(name, values[name]) for name in order}


def swap_exchange(t_a, t_b, x_a, x_b, m):
    got = exchange(SWAP_ORDER, near_t=t_a, far_t=t_b, near_x=x_a, far_x=x_b, mirror=m)
    return [got[name] for name in ("near_t", "far_t", "near_x", "far_x", "mirror")]


def all_forces(masks, phi, u, y, w, o_t, o_x, o_m):
    early, sent = call(early_force_kernel, (masks, phi, u, y, w), [24 * ROWS, 24 * ROWS], [12 * HALO])
    got = exchange(BACK_ORDER, back_t=o_t, back_x=o_x, mirror=o_m, early=sent)
    f_t, f_x, f_m, sent = call(
        late_force_kernel,
        (masks, phi, u, y, w, got["back_t"], got["back_x"], got["mirror"]),
        [8 * ROWS, 8 * ROWS, 8 * ROWS, 12 * ROWS],
        [],
    )
    late = exchange(("mirror",), mirror=sent)["mirror"]
    return early, got["early"], f_t, f_x, f_m, late


def on_exchange(t, x, m):
    got = exchange(ON_ORDER, on_t=t, on_x=x, mirror=m)
    return [got[name] for name in ("on_t", "on_x", "mirror")]


def per_device(gauge_links, momenta, noise_table, noise_index, partner):
    ta = lax.axis_index("ta")
    xd = lax.axis_index("xd")
    lane = lax.iota(jnp.int32, 8)
    last = lax.axis_size("ta") - 1
    info = jnp.where(
        lane == 0,
        ta & 1,
        jnp.where(
            lane == 1,
            xd & 1,
            jnp.where(lane == 2, jnp.where(ta == 0, -1, 1), jnp.where(ta == last, -1, 1)),
        ),
    ).astype(jnp.int32)
    u = gauge_links.reshape(72 * ROWS, 128)
    p = momenta.reshape(72 * ROWS, 128)
    table = jnp.transpose(noise_table, (0, 2, 1, 3))
    index = noise_index.reshape(ROWS, 128)
    messages = [FULL, FULL, FACE, FACE, 2 * FACE]
    local = [FULL, FULL, FULL]
    halo = [12 * HALO, 12 * HALO, FULL, FULL]
    spin = 24 * ROWS

    psi, *rest, masks = call(
        noise_kernel,
        [pltpu.with_memory_space_constraint(v, pltpu.HBM) for v in (info, partner, index, table, u)],
        [spin] + messages + local + [jax.ShapeDtypeStruct((INFO_ROWS, 128), jnp.int32)],
        [
            pltpu.VMEM((24, 4096), F32),
            pltpu.VMEM((384, 768), jnp.bfloat16),
            FULL,
            FULL,
            pltpu.VMEM((2, 3, 4, 4096), F32),
            72 * ROWS,
            pltpu.VMEM((ROWS, 128), jnp.int32),
            pltpu.SMEM((8,), jnp.int32),
            pltpu.SMEM((4,), jnp.int32),
            pltpu.SemaphoreType.DMA((5,)),
        ],
        12,
        from_hbm=True,
    )
    arrived = swap_exchange(*rest[:5])
    phi, *rest = call(phi_kernel, (masks, psi, u, *rest[5:], *arrived), [spin] + messages + local, halo + [FULL, FULL])
    arrived = swap_exchange(*rest[:5])
    y, w, o_t, o_x, o_m = call(
        response_kernel, (masks, phi, u, *rest[5:], *arrived), [spin, 4 * FULL, FULL, FACE, FACE], halo + [FULL]
    )
    forces = all_forces(masks, phi, u, y, w, o_t, o_x, o_m)
    u3, p3, q3 = call(early_update_kernel, (phi, u, p, *forces[:2]), [18 * ROWS, 9 * ROWS, FULL], [])
    u, p1, o_t, o_x, o_m, q0, q2 = call(
        update_kernel,
        (masks, phi, u, p, u3, p3, *forces),
        [72 * ROWS, 36 * ROWS, FULL, FACE, FACE, FULL, FULL],
        [8 * ROWS, 8 * ROWS],
    )
    y, w, o_t, o_x, o_m = call(
        response2_kernel,
        (masks, phi, u, q0, q2, q3, *arrived, *on_exchange(o_t, o_x, o_m)),
        [spin, 4 * FULL, FULL, FACE, FACE],
        halo + [FULL],
    )
    forces = all_forces(masks, phi, u, y, w, o_t, o_x, o_m)
    u3, p3 = call(early_last_kernel, (u, p1, p, *forces[:2]), [18 * ROWS, 18 * ROWS], [])
    new_u, new_p = call(
        last_kernel,
        (masks, u, p1, p, u3, p3, *forces),
        [72 * ROWS, 72 * ROWS],
        [54 * ROWS, 54 * ROWS, 8 * ROWS, 8 * ROWS, pltpu.SemaphoreType.DMA((8,))],
        to_hbm=True,
    )
    return new_u.reshape(gauge_links.shape), new_p.reshape(momenta.shape)


def solution(mesh):
    sites = P(None, None, None, None, "xd", "ta", None, None)
    return jax.shard_map(
        per_device,
        mesh=mesh,
        in_specs=(sites, sites, P(), P("xd", "ta", None, None), P("xd")),
        out_specs=(sites, sites),
        check_vma=False,
    )
```

```python
import jax
import jax.numpy as jnp
from jax import lax
from jax.experimental import pallas as pl
from jax.experimental.pallas import tpu as pltpu
from jax.sharding import PartitionSpec as P


HOPPING = 0.13
STEP = 0.25
DEGREE = 6
F32 = jnp.float32
GAMMA = (
    ((3, 2, 1, 0), ((0, 1), (0, 1), (0, -1), (0, -1))),
    ((2, 3, 0, 1), ((1, 0), (1, 0), (1, 0), (1, 0))),
    ((3, 2, 1, 0), ((-1, 0), (1, 0), (1, 0), (-1, 0))),
    ((2, 3, 0, 1), ((0, 1), (0, -1), (0, -1), (0, 1))),
)
ROWS = 16
HALO = 24


def ld(ref, k, h):
    return ref[k * ROWS + 8 * h : k * ROWS + 8 * h + 8, :]


def st(ref, k, h, value):
    ref[k * ROWS + 8 * h : k * ROWS + 8 * h + 8, :] = value


def cadd(a, b):
    return (a[0] + b[0], a[1] + b[1])


def csub(a, b):
    return (a[0] - b[0], a[1] - b[1])


def cmul(a, b):
    return (a[0] * b[0] - a[1] * b[1], a[0] * b[1] + a[1] * b[0])


def cmul_conj(a, b):
    return (a[0] * b[0] + a[1] * b[1], a[1] * b[0] - a[0] * b[1])


def add_unit(x, y, coef, sign):
    re, im = coef
    if re:
        if re * sign > 0:
            return cadd(x, y)
        return csub(x, y)
    if im * sign > 0:
        return (x[0] - y[1], x[1] + y[0])
    return (x[0] + y[1], x[1] - y[0])


def spinor(ref, h):
    return [[(ld(ref, c * 4 + s, h), ld(ref, 12 + c * 4 + s, h)) for c in range(3)] for s in range(4)]


def project(psi, mu, sign):
    source, coef = GAMMA[mu]
    return [[add_unit(psi[t][c], psi[source[t]][c], coef[t], sign) for c in range(3)] for t in range(2)]


def matrix(ref, mu, h):
    return [[(ld(ref, mu * 18 + i * 3 + j, h), ld(ref, mu * 18 + 9 + i * 3 + j, h)) for j in range(3)] for i in range(3)]


def mat_half(u, v):
    out = []
    for t in range(2):
        row = []
        for i in range(3):
            acc = cmul(u[i][0], v[t][0])
            for j in (1, 2):
                acc = cadd(acc, cmul(u[i][j], v[t][j]))
            row.append(acc)
        out.append(row)
    return out


def mat_dag_half(u, v):
    out = []
    for t in range(2):
        row = []
        for i in range(3):
            acc = cmul_conj(v[t][0], u[0][i])
            for j in (1, 2):
                acc = cadd(acc, cmul_conj(v[t][j], u[j][i]))
            row.append(acc)
        out.append(row)
    return out


def half_index(part, t, c):
    return part * 6 + t * 3 + c


def put_half(ref, h, v, base=0):
    for t in range(2):
        for c in range(3):
            for part in range(2):
                st(ref, base + half_index(part, t, c), h, v[t][c][part])


def get_half(fn):
    return [[tuple(fn(half_index(part, t, c)) for part in range(2)) for c in range(3)] for t in range(2)]


def map_half(fn, *vs):
    return [[tuple(fn(*(v[t][c][part] for v in vs)) for part in range(2)) for c in range(3)] for t in range(2)]


INFO_ROWS = 64


class Info:
    def __init__(self, info):
        self.even_t = info[24:32, :] == 0
        self.even_x = info[32:36, :] == 0
        self.sign_ahead = info[40:48, :].astype(F32)
        self.sign_behind = info[48:56, :].astype(F32)
        self.face_source = [info[16:20, :] == j for j in range(4)]
        self.edge_block = info[56:64, :]
        half = row_block()
        self.block_source = []
        for h in range(2):
            source = info[8 * h : 8 * h + 8, :]
            self.block_source.append((source == half, source == 1 - half, source == 2 + half))


def row_block():
    return lax.broadcasted_iota(jnp.int32, (8, 128), 0) >> 2


def write_info(info, odd_t, odd_x, sign_ahead, sign_behind, partner):
    row = lax.broadcasted_iota(jnp.int32, (8, 128), 0)

    def source_of(target):
        value = jnp.zeros((8, 128), jnp.int32)
        for j in range(4):
            value = jnp.where(target == partner[j], j, value)
        return value

    info[0:8, :] = source_of(row >> 2)
    info[8:16, :] = source_of(2 + (row >> 2))
    info[16:24, :] = source_of(row & 3)
    edge = jnp.int32(0)
    for j in range(4):
        edge = edge + jnp.where(partner[j] == 3, j, 0)
    for n, value in enumerate((odd_t, odd_x, sign_ahead, sign_behind, edge)):
        info[24 + 8 * n : 32 + 8 * n, :] = jnp.full((8, 128), value, jnp.int32)


def row_in_pair():
    return lax.broadcasted_iota(jnp.int32, (8, 128), 0) & 3


def send_rows(dst, base, src, k, info, row):
    def spread(j):
        at = k * ROWS + 4 * j + row
        return jnp.broadcast_to(src[at : at + 1, :], (4, 128))

    value = spread(0)
    for j in range(1, 4):
        value = jnp.where(info.face_source[j], spread(j), value)
    dst[base * 4 : base * 4 + 4, :] = value


def send_both(psi_ref, u_ref, info, t_a, t_b, x_a, x_b, mirror, q0, q2, q3, h0, h2):
    for h in range(2):
        psi = spinor(psi_ref, h)
        front = map_half(lambda a: a * info.sign_ahead, project(psi, 1, 1))
        back = map_half(
            lambda a: a * info.sign_behind, mat_dag_half(matrix(u_ref, 1, h), project(psi, 1, -1))
        )
        put_half(t_a, h, map_half(lambda a, b: jnp.where(info.even_t, b, a), front, back))
        put_half(t_b, h, map_half(lambda a, b: jnp.where(info.even_t, a, b), front, back))
        put_half(h0, h, project(psi, 0, 1))
        put_half(h2, h, project(psi, 2, 1))
        for mu, ref in ((0, q0), (2, q2), (3, q3)):
            put_half(ref, h, mat_dag_half(matrix(u_ref, mu, h), project(psi, mu, -1)))
    for k in range(12):
        front = h0[k * ROWS : k * ROWS + 4, :]
        back = q0[k * ROWS + 12 : k * ROWS + 16, :]
        x_a[k * 4 : k * 4 + 4, :] = jnp.where(info.even_x, back, front)
        x_b[k * 4 : k * 4 + 4, :] = jnp.where(info.even_x, front, back)
        send_rows(mirror, k, h2, k, info, 0)
        send_rows(mirror, 12 + k, q2, k, info, 3)


def dirac(psi_ref, u_ref, arrived, q0, q2, q3, scratch, out_ref, w_ref):
    ahead_t, behind_t, ahead_x, behind_x, ahead_m, behind_m = arrived
    a0, b0, fa, fb = scratch
    for k in range(12):
        a0[k * HALO + 16 : k * HALO + 20, :] = ahead_x(k)
        b0[k * HALO : k * HALO + 4, :] = behind_x(k)
        b0[k * HALO + 4 : k * HALO + 20, :] = q0[k * ROWS : k * ROWS + 16, :]
        fa[pl.ds(k * ROWS + 3, 4, stride=4), :] = ahead_m(k)
        fb[pl.ds(k * ROWS, 4, stride=4), :] = behind_m(k)
    for h in range(2):
        v = project(spinor(psi_ref, h), 0, 1)
        for t in range(2):
            for c in range(3):
                for part in range(2):
                    k = half_index(part, t, c)
                    a0[k * HALO + 8 * h : k * HALO + 8 * h + 8, :] = v[t][c][part]
    x2 = row_in_pair()
    for h in range(2):
        psi = spinor(psi_ref, h)
        acc = None
        for mu in range(4):
            if mu == 0:
                ahead = get_half(lambda k: a0[k * HALO + 8 * h + 4 : k * HALO + 8 * h + 12, :])
                behind = get_half(lambda k: b0[k * HALO + 8 * h : k * HALO + 8 * h + 8, :])
            elif mu == 1:
                ahead = get_half(lambda k: ahead_t(k, h))
                behind = get_half(lambda k: behind_t(k, h))
            elif mu == 2:
                raw = project(psi, 2, 1)
                face = get_half(lambda k: ld(fa, k, h))
                ahead = map_half(lambda r, f: jnp.where(x2 == 3, f, pltpu.roll(r, 7, 0)), raw, face)
                behind = get_half(lambda k: jnp.where(x2 == 0, ld(fb, k, h), pltpu.roll(ld(q2, k, h), 1, 0)))
            else:
                ahead = map_half(lambda r: pltpu.roll(r, 127, 1), project(psi, 3, 1))
                behind = get_half(lambda k: pltpu.roll(ld(q3, k, h), 1, 1))
            w = mat_half(matrix(u_ref, mu, h), ahead)
            if w_ref is not None:
                put_half(w_ref, h, w, mu * 12)
            total = map_half(lambda a, b: a + b, w, behind)
            delta = map_half(lambda a, b: a - b, w, behind)
            source, coef = GAMMA[mu]
            if acc is None:
                zero = jnp.zeros((8, 128), F32)
                acc = [total[0], total[1]] + [
                    [add_unit((zero, zero), delta[source[s]][c], coef[s], 1) for c in range(3)] for s in (2, 3)
                ]
            else:
                for s in range(2):
                    acc[s] = [cadd(acc[s][c], total[s][c]) for c in range(3)]
                for s in (2, 3):
                    acc[s] = [add_unit(acc[s][c], delta[source[s]][c], coef[s], 1) for c in range(3)]
        for s in range(4):
            for c in range(3):
                for part in range(2):
                    st(out_ref, part * 12 + c * 4 + s, h, psi[s][c][part] - HOPPING * acc[s][c][part])


def arrived_swap(info, t_a, t_b, x_a, x_b, mirror):
    def rows(ref, k):
        return ref[k * 4 : k * 4 + 4, :]

    return (
        lambda k, h: jnp.where(info.even_t, ld(t_a, k, h), ld(t_b, k, h)),
        lambda k, h: jnp.where(info.even_t, ld(t_b, k, h), ld(t_a, k, h)),
        lambda k: jnp.where(info.even_x, rows(x_a, k), rows(x_b, k)),
        lambda k: jnp.where(info.even_x, rows(x_b, k), rows(x_a, k)),
        lambda k: rows(mirror, k),
        lambda k: rows(mirror, 12 + k),
    )


def noise_kernel(partner_hbm, index_hbm, table_hbm, u_hbm, *rest):
    psi, t_a, t_b, x_a, x_b, mirror, q0, q2, q3, info_ref = rest[:10]
    flat, parts, h0, h2, table, u, index, partner, sems = rest[10:]
    copies = [
        pltpu.make_async_copy(src, dst, sems.at[n])
        for n, (src, dst) in enumerate(
            (
                (index_hbm, index),
                (table_hbm, table),
                (partner_hbm, partner),
                (u_hbm, u),
            )
        )
    ]
    for copy in copies:
        copy.start()
    copies[1].wait()
    for part in range(2):
        for c in range(3):
            flat[(part * 3 + c) * 4 : (part * 3 + c) * 4 + 4, :] = table[part, c]
    for hi in range(16):
        block = flat[:, hi * 256 : hi * 256 + 256]
        first = block.astype(jnp.bfloat16)
        left = block - first.astype(F32)
        second = left.astype(jnp.bfloat16)
        third = (left - second.astype(F32)).astype(jnp.bfloat16)
        for n, value in enumerate((first, second, third)):
            parts[hi * 24 : hi * 24 + 24, n * 256 : n * 256 + 256] = value
    copies[0].wait()
    low_iota = lax.broadcasted_iota(jnp.int32, (256, 128), 0)
    table_parts = parts[...]
    for r in range(0, 16, 2):
        wanted = [index[r + n : r + n + 1, :] for n in range(2)]
        hot = jnp.concatenate(
            [jnp.where(low_iota == (w & 255), 1.0, 0.0).astype(jnp.bfloat16) for w in wanted], axis=1
        )
        found = jnp.dot(table_parts, jnp.concatenate([hot, hot, hot], axis=0), preferred_element_type=F32)
        for n in range(2):
            high = jnp.broadcast_to(wanted[n] >> 8, (24, 128))
            value = found[0:24, 128 * n : 128 * n + 128]
            for hi in range(1, 16):
                value = jnp.where(high == hi, found[hi * 24 : hi * 24 + 24, 128 * n : 128 * n + 128], value)
            psi[pl.ds(r + n, 24, stride=16), :] = value
    copies[2].wait()
    ta, xd = lax.axis_index("ta"), lax.axis_index("xd")
    sign_ahead = jnp.where(ta == 0, -1, 1)
    sign_behind = jnp.where(ta == lax.axis_size("ta") - 1, -1, 1)
    write_info(info_ref, ta & 1, xd & 1, sign_ahead, sign_behind, [partner[j] & 3 for j in range(4)])
    info = Info(info_ref)
    copies[3].wait()
    send_both(psi, u, info, t_a, t_b, x_a, x_b, mirror, q0, q2, q3, h0, h2)


def phi_kernel(info_ref, psi, u, q0, q2, q3, t_a, t_b, x_a, x_b, mirror, *rest):
    phi, o_ta, o_tb, o_xa, o_xb, o_m, o_q0, o_q2, o_q3, a0, b0, fa, fb, h0, h2 = rest
    info = Info(info_ref)
    arrived = arrived_swap(info, t_a, t_b, x_a, x_b, mirror)
    dirac(psi, u, arrived, q0, q2, q3, (a0, b0, fa, fb), phi, None)
    send_both(phi, u, info, o_ta, o_tb, o_xa, o_xb, o_m, o_q0, o_q2, o_q3, h0, h2)


def send_response(y, info, o_t, o_x, o_m, h2):
    for h in range(2):
        v = spinor(y, h)
        put_half(o_t, h, map_half(lambda a: a * info.sign_ahead, project(v, 1, -1)))
        put_half(h2, h, project(v, 2, -1))
        if h == 0:
            face = project(v, 0, -1)
            for t in range(2):
                for c in range(3):
                    for part in range(2):
                        k = half_index(part, t, c)
                        o_x[k * 4 : k * 4 + 4, :] = face[t][c][part][0:4]
    for k in range(12):
        send_rows(o_m, k, h2, k, info, 0)


def response_kernel(info_ref, phi, u, q0, q2, q3, t_a, t_b, x_a, x_b, mirror, *rest):
    y, w, o_t, o_x, o_m, a0, b0, fa, fb, h2 = rest
    info = Info(info_ref)
    arrived = arrived_swap(info, t_a, t_b, x_a, x_b, mirror)
    dirac(phi, u, arrived, q0, q2, q3, (a0, b0, fa, fb), y, w)
    send_response(y, info, o_t, o_x, o_m, h2)


def response2_kernel(info_ref, phi, u, q0, q2, q3, t_a, t_b, x_a, x_b, mirror, b_t, b_x, b_m, *rest):
    y, w, o_t, o_x, o_m, a0, b0, fa, fb, h2 = rest
    info = Info(info_ref)
    arrived = list(arrived_swap(info, t_a, t_b, x_a, x_b, mirror))
    arrived[1] = lambda k, h: ld(b_t, k, h)
    arrived[3] = lambda k: b_x[k * 4 : k * 4 + 4, :]
    arrived[5] = lambda k: b_m[k * 4 : k * 4 + 4, :]
    dirac(phi, u, arrived, q0, q2, q3, (a0, b0, fa, fb), y, w)
    send_response(y, info, o_t, o_x, o_m, h2)


OFF = ((0, 1), (0, 2), (1, 2))
EARLY = (0, 2, 3)


def force_values(left, right):
    def g_im(i, j):
        return sum(left[n][i][1] * right[n][j][0] - left[n][i][0] * right[n][j][1] for n in range(4))

    def g_re(i, j):
        return sum(left[n][i][0] * right[n][j][0] + left[n][i][1] * right[n][j][1] for n in range(4))

    d = [g_im(i, i) for i in range(3)]
    third = (d[0] + d[1] + d[2]) * (1.0 / 3.0)
    scale = -2.0 * HOPPING
    values = [scale * (d[0] - third), scale * (d[1] - third)]
    for i, j in OFF:
        values.append((0.5 * scale) * (g_im(i, j) + g_im(j, i)))
        values.append((0.5 * scale) * (g_re(j, i) - g_re(i, j)))
    return values


def force_at(at, phi, u, y, w, mu, x):
    ysp = [[(at(y, c * 4 + s), at(y, 12 + c * 4 + s)) for c in range(3)] for s in range(4)]
    psp = [[(at(phi, c * 4 + s), at(phi, 12 + c * 4 + s)) for c in range(3)] for s in range(4)]
    link = [[(at(u, mu * 18 + i * 3 + j), at(u, mu * 18 + 9 + i * 3 + j)) for j in range(3)] for i in range(3)]
    left = mat_half(link, x(ysp)) + get_half(lambda k: at(w, mu * 12 + k))
    right = project(psp, mu, -1) + project(ysp, mu, 1)
    return force_values(left, right)


def early_force_kernel(info_ref, phi, u, y, w, force, sent, a0):
    info = Info(info_ref)
    nothing = jnp.zeros((4, 128), F32)
    for k in range(12):
        a0[k * HALO + 16 : k * HALO + 20, :] = nothing
    for h in range(2):
        v = project(spinor(y, h), 0, -1)
        for t in range(2):
            for c in range(3):
                for part in range(2):
                    k = half_index(part, t, c)
                    a0[k * HALO + 8 * h : k * HALO + 8 * h + 8, :] = v[t][c][part]
    for h in range(2):
        for e, mu in enumerate(EARLY):
            if mu == 0:
                x = lambda ysp: get_half(lambda k: a0[k * HALO + 8 * h + 4 : k * HALO + 8 * h + 12, :])
            elif mu == 2:
                x = lambda ysp: map_half(lambda r: pltpu.roll(r, 7, 0), project(ysp, 2, -1))
            else:
                x = lambda ysp: map_half(lambda r: pltpu.roll(r, 127, 1), project(ysp, 3, -1))
            for n, value in enumerate(force_at(lambda ref, k: ld(ref, k, h), phi, u, y, w, mu, x)):
                st(force, e * 8 + n, h, value)
    for k in range(24):
        send_blocks(sent, k, force, k, info)


def send_blocks(dst, base, src, k, info):
    low, high = ld(src, k, 0), ld(src, k, 1)
    low_turned, high_turned = pltpu.roll(low, 4, 0), pltpu.roll(high, 4, 0)
    for h in range(2):
        first, second, third = info.block_source[h]
        value = jnp.where(third, high, high_turned)
        value = jnp.where(second, low_turned, value)
        st(dst, base, h, jnp.where(first, low, value))


def late_force_kernel(info_ref, phi, u, y, w, r_t, r_x, r_m, f_t, f_x, f_m, sent):
    info = Info(info_ref)
    for h in range(2):
        arrived = get_half(lambda k: ld(r_t, k, h))
        for n, value in enumerate(force_at(lambda ref, k: ld(ref, k, h), phi, u, y, w, 1, lambda ysp: arrived)):
            st(f_t, n, h, value)
    for n in range(8):
        send_blocks(sent, n, f_t, n, info)
    face = lambda ref: get_half(lambda k: ref[k * 4 : k * 4 + 4, :])
    last_x = lambda ref, k: ref[k * ROWS + 12 : k * ROWS + 16, :]
    for n, value in enumerate(force_at(last_x, phi, u, y, w, 0, lambda ysp: face(r_x))):
        f_x[n * ROWS + 12 : n * ROWS + 16, :] = value
        sent[8 * ROWS + n * 4 : 8 * ROWS + n * 4 + 4, :] = value
    last_m = lambda ref, k: ref[pl.ds(k * ROWS + 3, 4, stride=4), :]
    for n, value in enumerate(force_at(last_m, phi, u, y, w, 2, lambda ysp: face(r_m))):
        f_m[pl.ds(n * ROWS + 3, 4, stride=4), :] = value
    for n in range(8):
        send_rows(sent, 40 + n, f_m, n, info, 3)


def place_faces(mirrored, m_x, m_m):
    for n in range(8):
        face = mirrored[8 * ROWS + n * 4 : 8 * ROWS + n * 4 + 4, :]
        for j in range(4):
            m_x[n * ROWS + 4 * j : n * ROWS + 4 * j + 4, :] = face
        m_m[pl.ds(n * ROWS + 3, 4, stride=4), :] = mirrored[8 * ROWS + 32 + n * 4 : 8 * ROWS + 32 + n * 4 + 4, :]


def both_forces(mu, h, block, early, mirror_early, f_t, f_x, f_m, mirrored, m_x, m_m):
    row = lax.broadcasted_iota(jnp.int32, (8, 128), 0)
    if mu == 1:
        return (lambda n: ld(f_t, n, h)), (lambda n: ld(mirrored, n, h))
    if mu == 2:
        edge = (row & 3) == 3
        return (
            lambda n: jnp.where(edge, ld(f_m, n, h), ld(early, 8 + n, h)),
            lambda n: jnp.where(edge, ld(m_m, n, h), ld(mirror_early, 8 + n, h)),
        )
    edge = (row >> 2) + 2 * h == block
    if h == 0:
        here = lambda n: ld(early, n, h)
    else:
        here = lambda n: jnp.where(row >= 4, ld(f_x, n, h), ld(early, n, h))
    return here, (lambda n: jnp.where(edge, ld(m_x, n, h), ld(mirror_early, n, h)))


def updated_momenta(read, force, mirrored):
    diag_force = [force(n) - mirrored(n) for n in range(2)]
    diag_force.append(-(diag_force[0] + diag_force[1]))
    diag = [read(n) + STEP * diag_force[n] for n in range(3)]
    upper = []
    for n in range(3):
        re = force(2 + 2 * n) - mirrored(2 + 2 * n)
        im = force(3 + 2 * n) + mirrored(3 + 2 * n)
        upper.append((read(3 + 2 * n) + STEP * re, read(4 + 2 * n) + STEP * im))
    return diag, upper


def link_step(diag, upper, u):
    b = [STEP * value for value in diag]
    b01, b02, b12 = ((STEP * value[0], STEP * value[1]) for value in upper)
    n01, n02, n12 = (v[0] * v[0] + v[1] * v[1] for v in (b01, b02, b12))
    square_diag = [b[0] * b[0] + n01 + n02, b[1] * b[1] + n01 + n12, b[2] * b[2] + n02 + n12]

    def scaled(v, by):
        return (v[0] * by, v[1] * by)

    square = [
        cadd(scaled(b01, b[0] + b[1]), cmul_conj(b02, b12)),
        cadd(scaled(b02, b[0] + b[2]), cmul(b01, b12)),
        cadd(scaled(b12, b[1] + b[2]), cmul_conj(b02, b01)),
    ]
    c1 = 0.5 * (square_diag[0] + square_diag[1] + square_diag[2])
    triple = cmul_conj(cmul(b01, b12), b02)[0]
    c0 = b[0] * (b[1] * b[2] - n12) - b[1] * n02 - b[2] * n01 + 2.0 * triple
    one = jnp.ones_like(c1)
    zero = jnp.zeros_like(c1)
    r0, r1, r2 = (one, zero), (zero, zero), (zero, zero)
    for k in range(DEGREE, 0, -1):
        inv = 1.0 / k
        new0 = (1.0 + (r2[1] * c0) * inv, -(r2[0] * c0) * inv)
        new1 = ((r0[0] - r2[0] * c1) * inv, (r0[1] - r2[1] * c1) * inv)
        new2 = (r1[0] * inv, r1[1] * inv)
        r0, r1, r2 = new0, new1, new2
    ir1 = (-r1[1], r1[0])
    e = [[None] * 3 for _ in range(3)]
    for i in range(3):
        e[i][i] = cadd(r0, csub(scaled(ir1, b[i]), scaled(r2, square_diag[i])))
    for (i, j), v, s in zip(OFF, (b01, b02, b12), square):
        e[i][j] = csub(cmul(ir1, v), cmul(r2, s))
        e[j][i] = csub(cmul_conj(ir1, v), cmul_conj(r2, s))
    return [[cadd(cadd(cmul(e[i][0], u[0][j]), cmul(e[i][1], u[1][j])), cmul(e[i][2], u[2][j])) for j in range(3)] for i in range(3)]


def input_momentum(ref, mu, h):
    def read(n):
        if n < 3:
            return ld(ref, mu * 18 + 4 * n, h)
        i, j = OFF[(n - 3) // 2]
        return ld(ref, mu * 18 + 9 * ((n - 3) % 2) + 3 * i + j, h)

    return read


def put_matrix(ref, mu, h, value):
    for i in range(3):
        for j in range(3):
            for part in range(2):
                st(ref, mu * 18 + part * 9 + i * 3 + j, h, value[i][j][part])


def put_momenta(ref, base, h, diag, upper):
    for n in range(3):
        st(ref, base + n, h, diag[n])
        st(ref, base + 3 + 2 * n, h, upper[n][0])
        st(ref, base + 4 + 2 * n, h, upper[n][1])


def put_full_momenta(new_p, old_p, at, mu, h, diag, upper):
    for i in range(3):
        st(new_p, at * 18 + 4 * i, h, diag[i])
        st(new_p, at * 18 + 9 + 4 * i, h, ld(old_p, mu * 18 + 9 + 4 * i, h))
    for (i, j), v in zip(OFF, upper):
        st(new_p, at * 18 + 3 * i + j, h, v[0])
        st(new_p, at * 18 + 3 * j + i, h, v[0])
        st(new_p, at * 18 + 9 + 3 * i + j, h, v[1])
        st(new_p, at * 18 + 9 + 3 * j + i, h, -v[1])


def early_update_kernel(phi, u, p, early, mirror_early, new_u, new_p, q3):
    for h in range(2):
        force, mirrored = (lambda n: ld(early, 16 + n, h)), (lambda n: ld(mirror_early, 16 + n, h))
        diag, upper = updated_momenta(input_momentum(p, 3, h), force, mirrored)
        put_momenta(new_p, 0, h, diag, upper)
        link = link_step(diag, upper, matrix(u, 3, h))
        put_matrix(new_u, 0, h, link)
        put_half(q3, h, mat_dag_half(link, project(spinor(phi, h), 3, -1)))


def early_last_kernel(u, p, old_p, early, mirror_early, new_u, new_p):
    for h in range(2):
        force, mirrored = (lambda n: ld(early, 16 + n, h)), (lambda n: ld(mirror_early, 16 + n, h))
        diag, upper = updated_momenta(lambda n: ld(p, 27 + n, h), force, mirrored)
        put_full_momenta(new_p, old_p, 0, 3, h, diag, upper)
        put_matrix(new_u, 0, h, link_step(diag, upper, matrix(u, 3, h)))


def update_kernel(info_ref, phi, u, p, u3, p3, *rest):
    forces = rest[:6]
    new_u, new_p, o_t, o_x, o_m, q0, q2, m_x, m_m = rest[6:]
    info = Info(info_ref)
    place_faces(forces[5], m_x, m_m)
    for h in range(2):
        psi = spinor(phi, h)
        for mu in range(3):
            diag, upper = updated_momenta(
                input_momentum(p, mu, h), *both_forces(mu, h, info.edge_block, *forces, m_x, m_m)
            )
            put_momenta(new_p, mu * 9, h, diag, upper)
            link = link_step(diag, upper, matrix(u, mu, h))
            put_matrix(new_u, mu, h, link)
            back = mat_dag_half(link, project(psi, mu, -1))
            if mu == 1:
                put_half(o_t, h, map_half(lambda a: a * info.sign_behind, back))
            else:
                put_half({0: q0, 2: q2}[mu], h, back)
    new_u[54 * ROWS : 72 * ROWS, :] = u3[...]
    new_p[27 * ROWS : 36 * ROWS, :] = p3[...]
    for k in range(12):
        o_x[k * 4 : k * 4 + 4, :] = q0[k * ROWS + 12 : k * ROWS + 16, :]
        send_rows(o_m, k, q2, k, info, 3)


def last_kernel(info_ref, u, p, old_p, u3, p3, *rest):
    forces = rest[:6]
    out_u, out_p, new_u, new_p, m_x, m_m, sems = rest[6:]
    info = Info(info_ref)
    size = 18 * ROWS
    copies = []

    def send(src, dst, mu):
        copies.append(pltpu.make_async_copy(src, dst.at[mu * size : mu * size + size, :], sems.at[len(copies)]))
        copies[-1].start()

    send(u3, out_u, 3)
    send(p3, out_p, 3)
    place_faces(forces[5], m_x, m_m)
    for mu in range(3):
        for h in range(2):
            diag, upper = updated_momenta(
                lambda n: ld(p, mu * 9 + n, h), *both_forces(mu, h, info.edge_block, *forces, m_x, m_m)
            )
            put_full_momenta(new_p, old_p, mu, mu, h, diag, upper)
            put_matrix(new_u, mu, h, link_step(diag, upper, matrix(u, mu, h)))
        send(new_p.at[mu * size : mu * size + size, :], out_p, mu)
        send(new_u.at[mu * size : mu * size + size, :], out_u, mu)
    for copy in copies:
        copy.wait()


VM = pl.BlockSpec(memory_space=pltpu.VMEM)
HBM = pl.BlockSpec(memory_space=pltpu.HBM)
FULL = ROWS * 12
FACE = 4 * 12


def call(kernel, args, outs, scratch, limit=4, from_hbm=False, to_hbm=False):
    return pl.pallas_call(
        kernel,
        out_shape=[jax.ShapeDtypeStruct((s, 128), F32) if isinstance(s, int) else s for s in outs],
        in_specs=[HBM if from_hbm else VM] * len(args),
        out_specs=[HBM if to_hbm else VM] * len(outs),
        scratch_shapes=[s if not isinstance(s, int) else pltpu.VMEM((s, 128), F32) for s in scratch],
        compiler_params=pltpu.CompilerParams(vmem_limit_bytes=limit << 20),
    )(*args)


def swap(value, axis, far):
    n = lax.axis_size(axis)
    if far:
        pairs = [(i, (i + 1) % n if i % 2 else (i - 1) % n) for i in range(n)]
    else:
        pairs = [(i, i ^ 1) for i in range(n)]
    return lax.ppermute(value, axis, pairs)


def shift(value, axis, by):
    n = lax.axis_size(axis)
    return lax.ppermute(value, axis, [(i, (i + by) % n) for i in range(n)])


def mirror_swap(value):
    n = lax.axis_size("xd")
    return lax.ppermute(value, "xd", [(i, i ^ (n // 2)) for i in range(n)])


def moved(name, value):
    if name == "far_t":
        return swap(value, "ta", True)
    if name == "near_t":
        return swap(value, "ta", False)
    if name == "far_x":
        return swap(value, "xd", True)
    if name == "near_x":
        return swap(value, "xd", False)
    if name == "back_t":
        return shift(value, "ta", -1)
    if name == "back_x":
        return shift(value, "xd", -1)
    if name == "on_t":
        return shift(value, "ta", 1)
    if name == "on_x":
        return shift(value, "xd", 1)
    return mirror_swap(value)


SWAP_ORDER = ("far_t", "mirror", "far_x", "near_x", "near_t")
BACK_ORDER = ("mirror", "back_t", "back_x", "early")
ON_ORDER = ("on_t", "mirror", "on_x")


def exchange(order, **values):
    return {name: moved(name, values[name]) for name in order}


def swap_exchange(t_a, t_b, x_a, x_b, m):
    got = exchange(SWAP_ORDER, near_t=t_a, far_t=t_b, near_x=x_a, far_x=x_b, mirror=m)
    return [got[name] for name in ("near_t", "far_t", "near_x", "far_x", "mirror")]


def all_forces(masks, phi, u, y, w, o_t, o_x, o_m):
    early, sent = call(early_force_kernel, (masks, phi, u, y, w), [24 * ROWS, 24 * ROWS], [12 * HALO])
    got = exchange(BACK_ORDER, back_t=o_t, back_x=o_x, mirror=o_m, early=sent)
    f_t, f_x, f_m, sent = call(
        late_force_kernel,
        (masks, phi, u, y, w, got["back_t"], got["back_x"], got["mirror"]),
        [8 * ROWS, 8 * ROWS, 8 * ROWS, 12 * ROWS],
        [],
    )
    late = exchange(("mirror",), mirror=sent)["mirror"]
    return early, got["early"], f_t, f_x, f_m, late


def on_exchange(t, x, m):
    got = exchange(ON_ORDER, on_t=t, on_x=x, mirror=m)
    return [got[name] for name in ("on_t", "on_x", "mirror")]


def per_device(gauge_links, momenta, noise_table, noise_index, partner):
    u = gauge_links.reshape(72 * ROWS, 128)
    p = momenta.reshape(72 * ROWS, 128)
    table = jnp.transpose(noise_table, (0, 2, 1, 3))
    index = noise_index.reshape(ROWS, 128)
    messages = [FULL, FULL, FACE, FACE, 2 * FACE]
    local = [FULL, FULL, FULL]
    halo = [12 * HALO, 12 * HALO, FULL, FULL]
    spin = 24 * ROWS

    psi, *rest, masks = call(
        noise_kernel,
        [pltpu.with_memory_space_constraint(v, pltpu.HBM) for v in (partner, index, table, u)],
        [spin] + messages + local + [jax.ShapeDtypeStruct((INFO_ROWS, 128), jnp.int32)],
        [
            pltpu.VMEM((24, 4096), F32),
            pltpu.VMEM((384, 768), jnp.bfloat16),
            FULL,
            FULL,
            pltpu.VMEM((2, 3, 4, 4096), F32),
            72 * ROWS,
            pltpu.VMEM((ROWS, 128), jnp.int32),
            pltpu.SMEM((4,), jnp.int32),
            pltpu.SemaphoreType.DMA((4,)),
        ],
        12,
        from_hbm=True,
    )
    arrived = swap_exchange(*rest[:5])
    phi, *rest = call(phi_kernel, (masks, psi, u, *rest[5:], *arrived), [spin] + messages + local, halo + [FULL, FULL])
    arrived = swap_exchange(*rest[:5])
    y, w, o_t, o_x, o_m = call(
        response_kernel, (masks, phi, u, *rest[5:], *arrived), [spin, 4 * FULL, FULL, FACE, FACE], halo + [FULL]
    )
    forces = all_forces(masks, phi, u, y, w, o_t, o_x, o_m)
    u3, p3, q3 = call(early_update_kernel, (phi, u, p, *forces[:2]), [18 * ROWS, 9 * ROWS, FULL], [])
    u, p1, o_t, o_x, o_m, q0, q2 = call(
        update_kernel,
        (masks, phi, u, p, u3, p3, *forces),
        [72 * ROWS, 36 * ROWS, FULL, FACE, FACE, FULL, FULL],
        [8 * ROWS, 8 * ROWS],
    )
    y, w, o_t, o_x, o_m = call(
        response2_kernel,
        (masks, phi, u, q0, q2, q3, *arrived, *on_exchange(o_t, o_x, o_m)),
        [spin, 4 * FULL, FULL, FACE, FACE],
        halo + [FULL],
    )
    forces = all_forces(masks, phi, u, y, w, o_t, o_x, o_m)
    u3, p3 = call(early_last_kernel, (u, p1, p, *forces[:2]), [18 * ROWS, 18 * ROWS], [])
    new_u, new_p = call(
        last_kernel,
        (masks, u, p1, p, u3, p3, *forces),
        [72 * ROWS, 72 * ROWS],
        [54 * ROWS, 54 * ROWS, 8 * ROWS, 8 * ROWS, pltpu.SemaphoreType.DMA((8,))],
        to_hbm=True,
    )
    return new_u.reshape(gauge_links.shape), new_p.reshape(momenta.shape)


def solution(mesh):
    sites = P(None, None, None, None, "xd", "ta", None, None)
    return jax.shard_map(
        per_device,
        mesh=mesh,
        in_specs=(sites, sites, P(), P("xd", "ta", None, None), P("xd")),
        out_specs=(sites, sites),
        check_vma=False,
    )
```

```python
import jax
import jax.numpy as jnp
from jax import lax
from jax.experimental import pallas as pl
from jax.experimental.pallas import tpu as pltpu
from jax.sharding import PartitionSpec as P


HOPPING = 0.13
STEP = 0.25
DEGREE = 6
F32 = jnp.float32
GAMMA = (
    ((3, 2, 1, 0), ((0, 1), (0, 1), (0, -1), (0, -1))),
    ((2, 3, 0, 1), ((1, 0), (1, 0), (1, 0), (1, 0))),
    ((3, 2, 1, 0), ((-1, 0), (1, 0), (1, 0), (-1, 0))),
    ((2, 3, 0, 1), ((0, 1), (0, -1), (0, -1), (0, 1))),
)
ROWS = 16
HALO = 24


def ld(ref, k, h):
    return ref[k * ROWS + 8 * h : k * ROWS + 8 * h + 8, :]


def st(ref, k, h, value):
    ref[k * ROWS + 8 * h : k * ROWS + 8 * h + 8, :] = value


def cadd(a, b):
    return (a[0] + b[0], a[1] + b[1])


def csub(a, b):
    return (a[0] - b[0], a[1] - b[1])


def cmul(a, b):
    return (a[0] * b[0] - a[1] * b[1], a[0] * b[1] + a[1] * b[0])


def cmul_conj(a, b):
    return (a[0] * b[0] + a[1] * b[1], a[1] * b[0] - a[0] * b[1])


def add_unit(x, y, coef, sign):
    re, im = coef
    if re:
        if re * sign > 0:
            return cadd(x, y)
        return csub(x, y)
    if im * sign > 0:
        return (x[0] - y[1], x[1] + y[0])
    return (x[0] + y[1], x[1] - y[0])


def spinor(ref, h):
    return [[(ld(ref, c * 4 + s, h), ld(ref, 12 + c * 4 + s, h)) for c in range(3)] for s in range(4)]


def project(psi, mu, sign):
    source, coef = GAMMA[mu]
    return [[add_unit(psi[t][c], psi[source[t]][c], coef[t], sign) for c in range(3)] for t in range(2)]


def matrix(ref, mu, h):
    return [[(ld(ref, mu * 18 + i * 3 + j, h), ld(ref, mu * 18 + 9 + i * 3 + j, h)) for j in range(3)] for i in range(3)]


def mat_half(u, v):
    out = []
    for t in range(2):
        row = []
        for i in range(3):
            acc = cmul(u[i][0], v[t][0])
            for j in (1, 2):
                acc = cadd(acc, cmul(u[i][j], v[t][j]))
            row.append(acc)
        out.append(row)
    return out


def mat_dag_half(u, v):
    out = []
    for t in range(2):
        row = []
        for i in range(3):
            acc = cmul_conj(v[t][0], u[0][i])
            for j in (1, 2):
                acc = cadd(acc, cmul_conj(v[t][j], u[j][i]))
            row.append(acc)
        out.append(row)
    return out


def half_index(part, t, c):
    return part * 6 + t * 3 + c


def put_half(ref, h, v, base=0):
    for t in range(2):
        for c in range(3):
            for part in range(2):
                st(ref, base + half_index(part, t, c), h, v[t][c][part])


def get_half(fn):
    return [[tuple(fn(half_index(part, t, c)) for part in range(2)) for c in range(3)] for t in range(2)]


def map_half(fn, *vs):
    return [[tuple(fn(*(v[t][c][part] for v in vs)) for part in range(2)) for c in range(3)] for t in range(2)]


INFO_ROWS = 64


class Info:
    def __init__(self, info):
        self.even_t = info[24:32, :] == 0
        self.even_x = info[32:36, :] == 0
        self.sign_ahead = info[40:48, :].astype(F32)
        self.sign_behind = info[48:56, :].astype(F32)
        self.face_source = [info[16:20, :] == j for j in range(4)]
        self.edge_block = info[56:64, :]
        half = row_block()
        self.block_source = []
        for h in range(2):
            source = info[8 * h : 8 * h + 8, :]
            self.block_source.append((source == half, source == 1 - half, source == 2 + half))


def row_block():
    return lax.broadcasted_iota(jnp.int32, (8, 128), 0) >> 2


def write_info(info, odd_t, odd_x, sign_ahead, sign_behind, partner):
    row = lax.broadcasted_iota(jnp.int32, (8, 128), 0)

    def source_of(target):
        value = jnp.zeros((8, 128), jnp.int32)
        for j in range(4):
            value = jnp.where(target == partner[j], j, value)
        return value

    info[0:8, :] = source_of(row >> 2)
    info[8:16, :] = source_of(2 + (row >> 2))
    info[16:24, :] = source_of(row & 3)
    edge = jnp.int32(0)
    for j in range(4):
        edge = edge + jnp.where(partner[j] == 3, j, 0)
    for n, value in enumerate((odd_t, odd_x, sign_ahead, sign_behind, edge)):
        info[24 + 8 * n : 32 + 8 * n, :] = jnp.full((8, 128), value, jnp.int32)


def row_in_pair():
    return lax.broadcasted_iota(jnp.int32, (8, 128), 0) & 3


def send_rows(dst, base, src, k, info, row):
    def spread(j):
        at = k * ROWS + 4 * j + row
        return jnp.broadcast_to(src[at : at + 1, :], (4, 128))

    value = spread(0)
    for j in range(1, 4):
        value = jnp.where(info.face_source[j], spread(j), value)
    dst[base * 4 : base * 4 + 4, :] = value


def send_both(psi_ref, u_ref, info, t_a, t_b, x_a, x_b, mirror, q0, q2, q3, h0, h2):
    for h in range(2):
        psi = spinor(psi_ref, h)
        front = map_half(lambda a: a * info.sign_ahead, project(psi, 1, 1))
        back = map_half(
            lambda a: a * info.sign_behind, mat_dag_half(matrix(u_ref, 1, h), project(psi, 1, -1))
        )
        put_half(t_a, h, map_half(lambda a, b: jnp.where(info.even_t, b, a), front, back))
        put_half(t_b, h, map_half(lambda a, b: jnp.where(info.even_t, a, b), front, back))
        put_half(h0, h, project(psi, 0, 1))
        put_half(h2, h, project(psi, 2, 1))
        for mu, ref in ((0, q0), (2, q2), (3, q3)):
            put_half(ref, h, mat_dag_half(matrix(u_ref, mu, h), project(psi, mu, -1)))
    for k in range(12):
        front = h0[k * ROWS : k * ROWS + 4, :]
        back = q0[k * ROWS + 12 : k * ROWS + 16, :]
        x_a[k * 4 : k * 4 + 4, :] = jnp.where(info.even_x, back, front)
        x_b[k * 4 : k * 4 + 4, :] = jnp.where(info.even_x, front, back)
        send_rows(mirror, k, h2, k, info, 0)
        send_rows(mirror, 12 + k, q2, k, info, 3)


def dirac_rest(psi_ref, u_ref, ahead_t, behind_t, ahead_m, behind_m, q2, q3, fa, fb, acc_ref, w_ref):
    for k in range(12):
        fa[pl.ds(k * ROWS + 3, 4, stride=4), :] = ahead_m(k)
        fb[pl.ds(k * ROWS, 4, stride=4), :] = behind_m(k)
    x2 = row_in_pair()
    for h in range(2):
        psi = spinor(psi_ref, h)
        acc = None
        for mu in (1, 2, 3):
            if mu == 1:
                ahead = get_half(lambda k: ahead_t(k, h))
                behind = get_half(lambda k: behind_t(k, h))
            elif mu == 2:
                raw = project(psi, 2, 1)
                face = get_half(lambda k: ld(fa, k, h))
                ahead = map_half(lambda r, f: jnp.where(x2 == 3, f, pltpu.roll(r, 7, 0)), raw, face)
                behind = get_half(lambda k: jnp.where(x2 == 0, ld(fb, k, h), pltpu.roll(ld(q2, k, h), 1, 0)))
            else:
                ahead = map_half(lambda r: pltpu.roll(r, 127, 1), project(psi, 3, 1))
                behind = get_half(lambda k: pltpu.roll(ld(q3, k, h), 1, 1))
            acc = add_direction(acc, u_ref, w_ref, mu, h, ahead, behind)
        for s in range(4):
            for c in range(3):
                for part in range(2):
                    st(acc_ref, part * 12 + c * 4 + s, h, acc[s][c][part])


def add_direction(acc, u_ref, w_ref, mu, h, ahead, behind):
    w = mat_half(matrix(u_ref, mu, h), ahead)
    if w_ref is not None:
        put_half(w_ref, h, w, (mu - 1) * 12 if mu else 0)
    total = map_half(lambda a, b: a + b, w, behind)
    delta = map_half(lambda a, b: a - b, w, behind)
    source, coef = GAMMA[mu]
    if acc is None:
        zero = jnp.zeros((8, 128), F32)
        acc = [[(zero, zero)] * 3] * 4
    upper = [[cadd(acc[s][c], total[s][c]) for c in range(3)] for s in range(2)]
    lower = [[add_unit(acc[s][c], delta[source[s]][c], coef[s], 1) for c in range(3)] for s in (2, 3)]
    return upper + lower


def dirac_rows(psi_ref, u_ref, acc_ref, ahead_x, behind_x, q0, a0, b0, out_ref, w_ref):
    for k in range(12):
        a0[k * HALO + 16 : k * HALO + 20, :] = ahead_x(k)
        b0[k * HALO : k * HALO + 4, :] = behind_x(k)
        b0[k * HALO + 4 : k * HALO + 20, :] = q0[k * ROWS : k * ROWS + 16, :]
    for h in range(2):
        v = project(spinor(psi_ref, h), 0, 1)
        for t in range(2):
            for c in range(3):
                for part in range(2):
                    k = half_index(part, t, c)
                    a0[k * HALO + 8 * h : k * HALO + 8 * h + 8, :] = v[t][c][part]
    for h in range(2):
        psi = spinor(psi_ref, h)
        ahead = get_half(lambda k: a0[k * HALO + 8 * h + 4 : k * HALO + 8 * h + 12, :])
        behind = get_half(lambda k: b0[k * HALO + 8 * h : k * HALO + 8 * h + 8, :])
        acc = add_direction(spinor(acc_ref, h), u_ref, w_ref, 0, h, ahead, behind)
        for s in range(4):
            for c in range(3):
                for part in range(2):
                    st(out_ref, part * 12 + c * 4 + s, h, psi[s][c][part] - HOPPING * acc[s][c][part])


def rows_of(ref, k):
    return ref[k * 4 : k * 4 + 4, :]


def rest_kernel(info_ref, psi, u, q2, q3, t_a, t_b, mirror, acc, *scratch, w=None):
    info = Info(info_ref)
    dirac_rest(
        psi,
        u,
        lambda k, h: jnp.where(info.even_t, ld(t_a, k, h), ld(t_b, k, h)),
        lambda k, h: jnp.where(info.even_t, ld(t_b, k, h), ld(t_a, k, h)),
        lambda k: rows_of(mirror, k),
        lambda k: rows_of(mirror, 12 + k),
        q2,
        q3,
        *scratch,
        acc,
        w,
    )


def rest_w_kernel(info_ref, psi, u, q2, q3, t_a, t_b, mirror, acc, w, *scratch):
    rest_kernel(info_ref, psi, u, q2, q3, t_a, t_b, mirror, acc, *scratch, w=w)


def rest2_kernel(info_ref, psi, u, q2, q3, t_a, t_b, mirror, b_t, b_m, acc, w, *scratch):
    info = Info(info_ref)
    dirac_rest(
        psi,
        u,
        lambda k, h: jnp.where(info.even_t, ld(t_a, k, h), ld(t_b, k, h)),
        lambda k, h: ld(b_t, k, h),
        lambda k: rows_of(mirror, k),
        lambda k: rows_of(b_m, k),
        q2,
        q3,
        *scratch,
        acc,
        w,
    )


def arrived_rows(info, x_a, x_b):
    return (
        lambda k: jnp.where(info.even_x, rows_of(x_a, k), rows_of(x_b, k)),
        lambda k: jnp.where(info.even_x, rows_of(x_b, k), rows_of(x_a, k)),
    )


def noise_kernel(partner_hbm, index_hbm, table_hbm, u_hbm, *rest):
    psi, t_a, t_b, x_a, x_b, mirror, q0, q2, q3, info_ref = rest[:10]
    flat, parts, h0, h2, table, u, index, partner, sems = rest[10:]
    copies = [
        pltpu.make_async_copy(src, dst, sems.at[n])
        for n, (src, dst) in enumerate(
            (
                (index_hbm, index),
                (table_hbm, table),
                (partner_hbm, partner),
                (u_hbm, u),
            )
        )
    ]
    for copy in copies:
        copy.start()
    copies[1].wait()
    for part in range(2):
        for c in range(3):
            flat[(part * 3 + c) * 4 : (part * 3 + c) * 4 + 4, :] = table[part, c]
    for hi in range(16):
        block = flat[:, hi * 256 : hi * 256 + 256]
        first = block.astype(jnp.bfloat16)
        left = block - first.astype(F32)
        second = left.astype(jnp.bfloat16)
        third = (left - second.astype(F32)).astype(jnp.bfloat16)
        for n, value in enumerate((first, second, third)):
            parts[hi * 24 : hi * 24 + 24, n * 256 : n * 256 + 256] = value
    copies[0].wait()
    low_iota = lax.broadcasted_iota(jnp.int32, (256, 128), 0)
    table_parts = parts[...]
    for r in range(0, 16, 2):
        wanted = [index[r + n : r + n + 1, :] for n in range(2)]
        hot = jnp.concatenate(
            [jnp.where(low_iota == (w & 255), 1.0, 0.0).astype(jnp.bfloat16) for w in wanted], axis=1
        )
        found = jnp.dot(table_parts, jnp.concatenate([hot, hot, hot], axis=0), preferred_element_type=F32)
        for n in range(2):
            high = jnp.broadcast_to(wanted[n] >> 8, (24, 128))
            value = found[0:24, 128 * n : 128 * n + 128]
            for hi in range(1, 16):
                value = jnp.where(high == hi, found[hi * 24 : hi * 24 + 24, 128 * n : 128 * n + 128], value)
            psi[pl.ds(r + n, 24, stride=16), :] = value
    copies[2].wait()
    ta, xd = lax.axis_index("ta"), lax.axis_index("xd")
    sign_ahead = jnp.where(ta == 0, -1, 1)
    sign_behind = jnp.where(ta == lax.axis_size("ta") - 1, -1, 1)
    write_info(info_ref, ta & 1, xd & 1, sign_ahead, sign_behind, [partner[j] & 3 for j in range(4)])
    info = Info(info_ref)
    copies[3].wait()
    send_both(psi, u, info, t_a, t_b, x_a, x_b, mirror, q0, q2, q3, h0, h2)


def phi_kernel(info_ref, psi, u, acc, q0, x_a, x_b, *rest):
    phi, o_ta, o_tb, o_xa, o_xb, o_m, o_q0, o_q2, o_q3, a0, b0, h0, h2 = rest
    info = Info(info_ref)
    dirac_rows(psi, u, acc, *arrived_rows(info, x_a, x_b), q0, a0, b0, phi, None)
    send_both(phi, u, info, o_ta, o_tb, o_xa, o_xb, o_m, o_q0, o_q2, o_q3, h0, h2)


def send_response(y, info, o_t, o_x, o_m, h2):
    for h in range(2):
        v = spinor(y, h)
        put_half(o_t, h, map_half(lambda a: a * info.sign_ahead, project(v, 1, -1)))
        put_half(h2, h, project(v, 2, -1))
        if h == 0:
            face = project(v, 0, -1)
            for t in range(2):
                for c in range(3):
                    for part in range(2):
                        k = half_index(part, t, c)
                        o_x[k * 4 : k * 4 + 4, :] = face[t][c][part][0:4]
    for k in range(12):
        send_rows(o_m, k, h2, k, info, 0)


def response_kernel(info_ref, phi, u, acc, q0, x_a, x_b, *rest):
    y, w, o_t, o_x, o_m, a0, b0, h2 = rest
    info = Info(info_ref)
    dirac_rows(phi, u, acc, *arrived_rows(info, x_a, x_b), q0, a0, b0, y, w)
    send_response(y, info, o_t, o_x, o_m, h2)


def response2_kernel(info_ref, phi, u, acc, q0, x_a, x_b, b_x, *rest):
    y, w, o_t, o_x, o_m, a0, b0, h2 = rest
    info = Info(info_ref)
    ahead_x = arrived_rows(info, x_a, x_b)[0]
    dirac_rows(phi, u, acc, ahead_x, lambda k: rows_of(b_x, k), q0, a0, b0, y, w)
    send_response(y, info, o_t, o_x, o_m, h2)


OFF = ((0, 1), (0, 2), (1, 2))
EARLY = (0, 2, 3)


def force_values(left, right):
    def g_im(i, j):
        return sum(left[n][i][1] * right[n][j][0] - left[n][i][0] * right[n][j][1] for n in range(4))

    def g_re(i, j):
        return sum(left[n][i][0] * right[n][j][0] + left[n][i][1] * right[n][j][1] for n in range(4))

    d = [g_im(i, i) for i in range(3)]
    third = (d[0] + d[1] + d[2]) * (1.0 / 3.0)
    scale = -2.0 * HOPPING
    values = [scale * (d[0] - third), scale * (d[1] - third)]
    for i, j in OFF:
        values.append((0.5 * scale) * (g_im(i, j) + g_im(j, i)))
        values.append((0.5 * scale) * (g_re(j, i) - g_re(i, j)))
    return values


def force_at(at, phi, u, y, w, mu, x):
    ysp = [[(at(y, c * 4 + s), at(y, 12 + c * 4 + s)) for c in range(3)] for s in range(4)]
    psp = [[(at(phi, c * 4 + s), at(phi, 12 + c * 4 + s)) for c in range(3)] for s in range(4)]
    link = [[(at(u, mu * 18 + i * 3 + j), at(u, mu * 18 + 9 + i * 3 + j)) for j in range(3)] for i in range(3)]
    ref, base = (w[1], (mu - 1) * 12) if mu else (w[0], 0)
    left = mat_half(link, x(ysp)) + get_half(lambda k: at(ref, base + k))
    right = project(psp, mu, -1) + project(ysp, mu, 1)
    return force_values(left, right)


def early_force_kernel(info_ref, phi, u, y, w0, w1, force, sent, a0):
    w = (w0, w1)
    info = Info(info_ref)
    nothing = jnp.zeros((4, 128), F32)
    for k in range(12):
        a0[k * HALO + 16 : k * HALO + 20, :] = nothing
    for h in range(2):
        v = project(spinor(y, h), 0, -1)
        for t in range(2):
            for c in range(3):
                for part in range(2):
                    k = half_index(part, t, c)
                    a0[k * HALO + 8 * h : k * HALO + 8 * h + 8, :] = v[t][c][part]
    for h in range(2):
        for e, mu in enumerate(EARLY):
            if mu == 0:
                x = lambda ysp: get_half(lambda k: a0[k * HALO + 8 * h + 4 : k * HALO + 8 * h + 12, :])
            elif mu == 2:
                x = lambda ysp: map_half(lambda r: pltpu.roll(r, 7, 0), project(ysp, 2, -1))
            else:
                x = lambda ysp: map_half(lambda r: pltpu.roll(r, 127, 1), project(ysp, 3, -1))
            for n, value in enumerate(force_at(lambda ref, k: ld(ref, k, h), phi, u, y, w, mu, x)):
                st(force, e * 8 + n, h, value)
    for k in range(24):
        send_blocks(sent, k, force, k, info)


def send_blocks(dst, base, src, k, info):
    low, high = ld(src, k, 0), ld(src, k, 1)
    low_turned, high_turned = pltpu.roll(low, 4, 0), pltpu.roll(high, 4, 0)
    for h in range(2):
        first, second, third = info.block_source[h]
        value = jnp.where(third, high, high_turned)
        value = jnp.where(second, low_turned, value)
        st(dst, base, h, jnp.where(first, low, value))


def late_force_kernel(info_ref, phi, u, y, w0, w1, r_t, r_x, r_m, f_t, f_x, f_m, sent):
    w = (w0, w1)
    info = Info(info_ref)
    for h in range(2):
        arrived = get_half(lambda k: ld(r_t, k, h))
        for n, value in enumerate(force_at(lambda ref, k: ld(ref, k, h), phi, u, y, w, 1, lambda ysp: arrived)):
            st(f_t, n, h, value)
    for n in range(8):
        send_blocks(sent, n, f_t, n, info)
    face = lambda ref: get_half(lambda k: ref[k * 4 : k * 4 + 4, :])
    last_x = lambda ref, k: ref[k * ROWS + 12 : k * ROWS + 16, :]
    for n, value in enumerate(force_at(last_x, phi, u, y, w, 0, lambda ysp: face(r_x))):
        f_x[n * ROWS + 12 : n * ROWS + 16, :] = value
        sent[8 * ROWS + n * 4 : 8 * ROWS + n * 4 + 4, :] = value
    last_m = lambda ref, k: ref[pl.ds(k * ROWS + 3, 4, stride=4), :]
    for n, value in enumerate(force_at(last_m, phi, u, y, w, 2, lambda ysp: face(r_m))):
        f_m[pl.ds(n * ROWS + 3, 4, stride=4), :] = value
    for n in range(8):
        send_rows(sent, 40 + n, f_m, n, info, 3)


def place_faces(mirrored, m_x, m_m):
    for n in range(8):
        face = mirrored[8 * ROWS + n * 4 : 8 * ROWS + n * 4 + 4, :]
        for j in range(4):
            m_x[n * ROWS + 4 * j : n * ROWS + 4 * j + 4, :] = face
        m_m[pl.ds(n * ROWS + 3, 4, stride=4), :] = mirrored[8 * ROWS + 32 + n * 4 : 8 * ROWS + 32 + n * 4 + 4, :]


def both_forces(mu, h, block, early, mirror_early, f_t, f_x, f_m, mirrored, m_x, m_m):
    row = lax.broadcasted_iota(jnp.int32, (8, 128), 0)
    if mu == 1:
        return (lambda n: ld(f_t, n, h)), (lambda n: ld(mirrored, n, h))
    if mu == 2:
        edge = (row & 3) == 3
        return (
            lambda n: jnp.where(edge, ld(f_m, n, h), ld(early, 8 + n, h)),
            lambda n: jnp.where(edge, ld(m_m, n, h), ld(mirror_early, 8 + n, h)),
        )
    edge = (row >> 2) + 2 * h == block
    if h == 0:
        here = lambda n: ld(early, n, h)
    else:
        here = lambda n: jnp.where(row >= 4, ld(f_x, n, h), ld(early, n, h))
    return here, (lambda n: jnp.where(edge, ld(m_x, n, h), ld(mirror_early, n, h)))


def updated_momenta(read, force, mirrored):
    diag_force = [force(n) - mirrored(n) for n in range(2)]
    diag_force.append(-(diag_force[0] + diag_force[1]))
    diag = [read(n) + STEP * diag_force[n] for n in range(3)]
    upper = []
    for n in range(3):
        re = force(2 + 2 * n) - mirrored(2 + 2 * n)
        im = force(3 + 2 * n) + mirrored(3 + 2 * n)
        upper.append((read(3 + 2 * n) + STEP * re, read(4 + 2 * n) + STEP * im))
    return diag, upper


def link_step(diag, upper, u):
    b = [STEP * value for value in diag]
    b01, b02, b12 = ((STEP * value[0], STEP * value[1]) for value in upper)
    n01, n02, n12 = (v[0] * v[0] + v[1] * v[1] for v in (b01, b02, b12))
    square_diag = [b[0] * b[0] + n01 + n02, b[1] * b[1] + n01 + n12, b[2] * b[2] + n02 + n12]

    def scaled(v, by):
        return (v[0] * by, v[1] * by)

    square = [
        cadd(scaled(b01, b[0] + b[1]), cmul_conj(b02, b12)),
        cadd(scaled(b02, b[0] + b[2]), cmul(b01, b12)),
        cadd(scaled(b12, b[1] + b[2]), cmul_conj(b02, b01)),
    ]
    c1 = 0.5 * (square_diag[0] + square_diag[1] + square_diag[2])
    triple = cmul_conj(cmul(b01, b12), b02)[0]
    c0 = b[0] * (b[1] * b[2] - n12) - b[1] * n02 - b[2] * n01 + 2.0 * triple
    one = jnp.ones_like(c1)
    zero = jnp.zeros_like(c1)
    r0, r1, r2 = (one, zero), (zero, zero), (zero, zero)
    for k in range(DEGREE, 0, -1):
        inv = 1.0 / k
        new0 = (1.0 + (r2[1] * c0) * inv, -(r2[0] * c0) * inv)
        new1 = ((r0[0] - r2[0] * c1) * inv, (r0[1] - r2[1] * c1) * inv)
        new2 = (r1[0] * inv, r1[1] * inv)
        r0, r1, r2 = new0, new1, new2
    ir1 = (-r1[1], r1[0])
    e = [[None] * 3 for _ in range(3)]
    for i in range(3):
        e[i][i] = cadd(r0, csub(scaled(ir1, b[i]), scaled(r2, square_diag[i])))
    for (i, j), v, s in zip(OFF, (b01, b02, b12), square):
        e[i][j] = csub(cmul(ir1, v), cmul(r2, s))
        e[j][i] = csub(cmul_conj(ir1, v), cmul_conj(r2, s))
    return [[cadd(cadd(cmul(e[i][0], u[0][j]), cmul(e[i][1], u[1][j])), cmul(e[i][2], u[2][j])) for j in range(3)] for i in range(3)]


def input_momentum(ref, mu, h):
    def read(n):
        if n < 3:
            return ld(ref, mu * 18 + 4 * n, h)
        i, j = OFF[(n - 3) // 2]
        return ld(ref, mu * 18 + 9 * ((n - 3) % 2) + 3 * i + j, h)

    return read


def put_matrix(ref, mu, h, value):
    for i in range(3):
        for j in range(3):
            for part in range(2):
                st(ref, mu * 18 + part * 9 + i * 3 + j, h, value[i][j][part])


def put_momenta(ref, base, h, diag, upper):
    for n in range(3):
        st(ref, base + n, h, diag[n])
        st(ref, base + 3 + 2 * n, h, upper[n][0])
        st(ref, base + 4 + 2 * n, h, upper[n][1])


def put_full_momenta(new_p, old_p, at, mu, h, diag, upper):
    for i in range(3):
        st(new_p, at * 18 + 4 * i, h, diag[i])
        st(new_p, at * 18 + 9 + 4 * i, h, ld(old_p, mu * 18 + 9 + 4 * i, h))
    for (i, j), v in zip(OFF, upper):
        st(new_p, at * 18 + 3 * i + j, h, v[0])
        st(new_p, at * 18 + 3 * j + i, h, v[0])
        st(new_p, at * 18 + 9 + 3 * i + j, h, v[1])
        st(new_p, at * 18 + 9 + 3 * j + i, h, -v[1])


def early_update_kernel(phi, u, p, early, mirror_early, new_u, new_p, q3):
    for h in range(2):
        force, mirrored = (lambda n: ld(early, 16 + n, h)), (lambda n: ld(mirror_early, 16 + n, h))
        diag, upper = updated_momenta(input_momentum(p, 3, h), force, mirrored)
        put_momenta(new_p, 0, h, diag, upper)
        link = link_step(diag, upper, matrix(u, 3, h))
        put_matrix(new_u, 0, h, link)
        put_half(q3, h, mat_dag_half(link, project(spinor(phi, h), 3, -1)))


def early_last_kernel(u, p, old_p, early, mirror_early, new_u, new_p):
    for h in range(2):
        force, mirrored = (lambda n: ld(early, 16 + n, h)), (lambda n: ld(mirror_early, 16 + n, h))
        diag, upper = updated_momenta(lambda n: ld(p, 27 + n, h), force, mirrored)
        put_full_momenta(new_p, old_p, 0, 3, h, diag, upper)
        put_matrix(new_u, 0, h, link_step(diag, upper, matrix(u, 3, h)))


def update_kernel(info_ref, phi, u, p, u3, p3, *rest):
    forces = rest[:6]
    new_u, new_p, o_t, o_x, o_m, q0, q2, m_x, m_m = rest[6:]
    info = Info(info_ref)
    place_faces(forces[5], m_x, m_m)
    for h in range(2):
        psi = spinor(phi, h)
        for mu in range(3):
            diag, upper = updated_momenta(
                input_momentum(p, mu, h), *both_forces(mu, h, info.edge_block, *forces, m_x, m_m)
            )
            put_momenta(new_p, mu * 9, h, diag, upper)
            link = link_step(diag, upper, matrix(u, mu, h))
            put_matrix(new_u, mu, h, link)
            back = mat_dag_half(link, project(psi, mu, -1))
            if mu == 1:
                put_half(o_t, h, map_half(lambda a: a * info.sign_behind, back))
            else:
                put_half({0: q0, 2: q2}[mu], h, back)
    new_u[54 * ROWS : 72 * ROWS, :] = u3[...]
    new_p[27 * ROWS : 36 * ROWS, :] = p3[...]
    for k in range(12):
        o_x[k * 4 : k * 4 + 4, :] = q0[k * ROWS + 12 : k * ROWS + 16, :]
        send_rows(o_m, k, q2, k, info, 3)


def last_kernel(info_ref, u, p, old_p, u3, p3, *rest):
    forces = rest[:6]
    out_u, out_p, new_u, new_p, m_x, m_m, sems = rest[6:]
    info = Info(info_ref)
    size = 18 * ROWS
    copies = []

    def send(src, dst, mu):
        copies.append(pltpu.make_async_copy(src, dst.at[mu * size : mu * size + size, :], sems.at[len(copies)]))
        copies[-1].start()

    send(u3, out_u, 3)
    send(p3, out_p, 3)
    place_faces(forces[5], m_x, m_m)
    for mu in range(3):
        for h in range(2):
            diag, upper = updated_momenta(
                lambda n: ld(p, mu * 9 + n, h), *both_forces(mu, h, info.edge_block, *forces, m_x, m_m)
            )
            put_full_momenta(new_p, old_p, mu, mu, h, diag, upper)
            put_matrix(new_u, mu, h, link_step(diag, upper, matrix(u, mu, h)))
        send(new_p.at[mu * size : mu * size + size, :], out_p, mu)
        send(new_u.at[mu * size : mu * size + size, :], out_u, mu)
    for copy in copies:
        copy.wait()


VM = pl.BlockSpec(memory_space=pltpu.VMEM)
HBM = pl.BlockSpec(memory_space=pltpu.HBM)
FULL = ROWS * 12
FACE = 4 * 12


def call(kernel, args, outs, scratch, limit=4, from_hbm=False, to_hbm=False):
    return pl.pallas_call(
        kernel,
        out_shape=[jax.ShapeDtypeStruct((s, 128), F32) if isinstance(s, int) else s for s in outs],
        in_specs=[HBM if from_hbm else VM] * len(args),
        out_specs=[HBM if to_hbm else VM] * len(outs),
        scratch_shapes=[s if not isinstance(s, int) else pltpu.VMEM((s, 128), F32) for s in scratch],
        compiler_params=pltpu.CompilerParams(vmem_limit_bytes=limit << 20),
    )(*args)


def swap(value, axis, far):
    n = lax.axis_size(axis)
    if far:
        pairs = [(i, (i + 1) % n if i % 2 else (i - 1) % n) for i in range(n)]
    else:
        pairs = [(i, i ^ 1) for i in range(n)]
    return lax.ppermute(value, axis, pairs)


def shift(value, axis, by):
    n = lax.axis_size(axis)
    return lax.ppermute(value, axis, [(i, (i + by) % n) for i in range(n)])


def mirror_swap(value):
    n = lax.axis_size("xd")
    return lax.ppermute(value, "xd", [(i, i ^ (n // 2)) for i in range(n)])


def moved(name, value):
    if name == "far_t":
        return swap(value, "ta", True)
    if name == "near_t":
        return swap(value, "ta", False)
    if name == "far_x":
        return swap(value, "xd", True)
    if name == "near_x":
        return swap(value, "xd", False)
    if name == "back_t":
        return shift(value, "ta", -1)
    if name == "back_x":
        return shift(value, "xd", -1)
    if name == "on_t":
        return shift(value, "ta", 1)
    if name == "on_x":
        return shift(value, "xd", 1)
    return mirror_swap(value)


SWAP_ORDER = ("far_t", "mirror", "far_x", "near_x", "near_t")
BACK_ORDER = ("mirror", "back_t", "back_x", "early")
ON_ORDER = ("on_t", "mirror", "on_x")


def exchange(order, **values):
    return {name: moved(name, values[name]) for name in order}


def swap_exchange(t_a, t_b, x_a, x_b, m):
    got = exchange(SWAP_ORDER, near_t=t_a, far_t=t_b, near_x=x_a, far_x=x_b, mirror=m)
    return [got[name] for name in ("near_t", "far_t", "near_x", "far_x", "mirror")]


def all_forces(masks, phi, u, y, w, o_t, o_x, o_m):
    early, sent = call(early_force_kernel, (masks, phi, u, y, *w), [24 * ROWS, 24 * ROWS], [12 * HALO])
    got = exchange(BACK_ORDER, back_t=o_t, back_x=o_x, mirror=o_m, early=sent)
    f_t, f_x, f_m, sent = call(
        late_force_kernel,
        (masks, phi, u, y, *w, got["back_t"], got["back_x"], got["mirror"]),
        [8 * ROWS, 8 * ROWS, 8 * ROWS, 12 * ROWS],
        [],
    )
    late = exchange(("mirror",), mirror=sent)["mirror"]
    return early, got["early"], f_t, f_x, f_m, late


def on_exchange(t, x, m):
    got = exchange(ON_ORDER, on_t=t, on_x=x, mirror=m)
    return [got[name] for name in ("on_t", "on_x", "mirror")]


def per_device(gauge_links, momenta, noise_table, noise_index, partner):
    u = gauge_links.reshape(72 * ROWS, 128)
    p = momenta.reshape(72 * ROWS, 128)
    table = jnp.transpose(noise_table, (0, 2, 1, 3))
    index = noise_index.reshape(ROWS, 128)
    messages = [FULL, FULL, FACE, FACE, 2 * FACE]
    local = [FULL, FULL, FULL]
    halo = [12 * HALO, 12 * HALO]
    spin = 24 * ROWS

    psi, *rest, masks = call(
        noise_kernel,
        [pltpu.with_memory_space_constraint(v, pltpu.HBM) for v in (partner, index, table, u)],
        [spin] + messages + local + [jax.ShapeDtypeStruct((INFO_ROWS, 128), jnp.int32)],
        [
            pltpu.VMEM((24, 4096), F32),
            pltpu.VMEM((384, 768), jnp.bfloat16),
            FULL,
            FULL,
            pltpu.VMEM((2, 3, 4, 4096), F32),
            72 * ROWS,
            pltpu.VMEM((ROWS, 128), jnp.int32),
            pltpu.SMEM((4,), jnp.int32),
            pltpu.SemaphoreType.DMA((4,)),
        ],
        12,
        from_hbm=True,
    )
    t_a, t_b, x_a, x_b, m = swap_exchange(*rest[:5])
    q0, q2, q3 = rest[5:]
    (acc,) = call(rest_kernel, (masks, psi, u, q2, q3, t_a, t_b, m), [spin], [FULL, FULL])
    phi, *rest = call(phi_kernel, (masks, psi, u, acc, q0, x_a, x_b), [spin] + messages + local, halo + [FULL, FULL])
    t_a, t_b, x_a, x_b, m = swap_exchange(*rest[:5])
    q0, q2, q3 = rest[5:]
    acc, w1 = call(rest_w_kernel, (masks, phi, u, q2, q3, t_a, t_b, m), [spin, 3 * FULL], [FULL, FULL])
    y, w0, o_t, o_x, o_m = call(
        response_kernel, (masks, phi, u, acc, q0, x_a, x_b), [spin, FULL, FULL, FACE, FACE], halo + [FULL]
    )
    w = (w0, w1)
    forces = all_forces(masks, phi, u, y, w, o_t, o_x, o_m)
    u3, p3, q3 = call(early_update_kernel, (phi, u, p, *forces[:2]), [18 * ROWS, 9 * ROWS, FULL], [])
    u, p1, o_t, o_x, o_m, q0, q2 = call(
        update_kernel,
        (masks, phi, u, p, u3, p3, *forces),
        [72 * ROWS, 36 * ROWS, FULL, FACE, FACE, FULL, FULL],
        [8 * ROWS, 8 * ROWS],
    )
    b_t, b_x, b_m = on_exchange(o_t, o_x, o_m)
    acc, w1 = call(rest2_kernel, (masks, phi, u, q2, q3, t_a, t_b, m, b_t, b_m), [spin, 3 * FULL], [FULL, FULL])
    y, w0, o_t, o_x, o_m = call(
        response2_kernel, (masks, phi, u, acc, q0, x_a, x_b, b_x), [spin, FULL, FULL, FACE, FACE], halo + [FULL]
    )
    w = (w0, w1)
    forces = all_forces(masks, phi, u, y, w, o_t, o_x, o_m)
    u3, p3 = call(early_last_kernel, (u, p1, p, *forces[:2]), [18 * ROWS, 18 * ROWS], [])
    new_u, new_p = call(
        last_kernel,
        (masks, u, p1, p, u3, p3, *forces),
        [72 * ROWS, 72 * ROWS],
        [54 * ROWS, 54 * ROWS, 8 * ROWS, 8 * ROWS, pltpu.SemaphoreType.DMA((8,))],
        to_hbm=True,
    )
    return new_u.reshape(gauge_links.shape), new_p.reshape(momenta.shape)


def solution(mesh):
    sites = P(None, None, None, None, "xd", "ta", None, None)
    return jax.shard_map(
        per_device,
        mesh=mesh,
        in_specs=(sites, sites, P(), P("xd", "ta", None, None), P("xd")),
        out_specs=(sites, sites),
        check_vma=False,
    )
```

```python
import jax
import jax.numpy as jnp
from jax import lax
from jax.experimental import pallas as pl
from jax.experimental.pallas import tpu as pltpu
from jax.sharding import PartitionSpec as P


HOPPING = 0.13
STEP = 0.25
F32 = jnp.float32
GAMMA = (
    ((3, 2, 1, 0), ((0, 1), (0, 1), (0, -1), (0, -1))),
    ((2, 3, 0, 1), ((1, 0), (1, 0), (1, 0), (1, 0))),
    ((3, 2, 1, 0), ((-1, 0), (1, 0), (1, 0), (-1, 0))),
    ((2, 3, 0, 1), ((0, 1), (0, -1), (0, -1), (0, 1))),
)
ROWS = 16
HALO = 24


def ld(ref, k, h):
    return ref[k * ROWS + 8 * h : k * ROWS + 8 * h + 8, :]


def st(ref, k, h, value):
    ref[k * ROWS + 8 * h : k * ROWS + 8 * h + 8, :] = value


def cadd(a, b):
    return (a[0] + b[0], a[1] + b[1])


def csub(a, b):
    return (a[0] - b[0], a[1] - b[1])


def cmul(a, b):
    return (a[0] * b[0] - a[1] * b[1], a[0] * b[1] + a[1] * b[0])


def cmul_conj(a, b):
    return (a[0] * b[0] + a[1] * b[1], a[1] * b[0] - a[0] * b[1])


def add_unit(x, y, coef, sign):
    re, im = coef
    if re:
        if re * sign > 0:
            return cadd(x, y)
        return csub(x, y)
    if im * sign > 0:
        return (x[0] - y[1], x[1] + y[0])
    return (x[0] + y[1], x[1] - y[0])


def spinor(ref, h):
    return [[(ld(ref, c * 4 + s, h), ld(ref, 12 + c * 4 + s, h)) for c in range(3)] for s in range(4)]


def project(psi, mu, sign):
    source, coef = GAMMA[mu]
    return [[add_unit(psi[t][c], psi[source[t]][c], coef[t], sign) for c in range(3)] for t in range(2)]


def matrix(ref, mu, h):
    return [[(ld(ref, mu * 18 + i * 3 + j, h), ld(ref, mu * 18 + 9 + i * 3 + j, h)) for j in range(3)] for i in range(3)]


def mat_half(u, v):
    out = []
    for t in range(2):
        row = []
        for i in range(3):
            acc = cmul(u[i][0], v[t][0])
            for j in (1, 2):
                acc = cadd(acc, cmul(u[i][j], v[t][j]))
            row.append(acc)
        out.append(row)
    return out


def mat_dag_half(u, v):
    out = []
    for t in range(2):
        row = []
        for i in range(3):
            acc = cmul_conj(v[t][0], u[0][i])
            for j in (1, 2):
                acc = cadd(acc, cmul_conj(v[t][j], u[j][i]))
            row.append(acc)
        out.append(row)
    return out


def half_index(part, t, c):
    return part * 6 + t * 3 + c


def put_half(ref, h, v, base=0):
    for t in range(2):
        for c in range(3):
            for part in range(2):
                st(ref, base + half_index(part, t, c), h, v[t][c][part])


def get_half(fn):
    return [[tuple(fn(half_index(part, t, c)) for part in range(2)) for c in range(3)] for t in range(2)]


def map_half(fn, *vs):
    return [[tuple(fn(*(v[t][c][part] for v in vs)) for part in range(2)) for c in range(3)] for t in range(2)]


INFO_ROWS = 64


class Info:
    def __init__(self, info):
        self.even_t = info[24:32, :] == 0
        self.even_x = info[32:36, :] == 0
        self.sign_ahead = info[40:48, :].astype(F32)
        self.sign_behind = info[48:56, :].astype(F32)
        self.face_source = [info[16:20, :] == j for j in range(4)]
        self.edge_block = info[56:64, :]
        half = row_block()
        self.block_source = []
        for h in range(2):
            source = info[8 * h : 8 * h + 8, :]
            self.block_source.append((source == half, source == 1 - half, source == 2 + half))


def row_block():
    return lax.broadcasted_iota(jnp.int32, (8, 128), 0) >> 2


def write_info(info, odd_t, odd_x, sign_ahead, sign_behind, partner):
    row = lax.broadcasted_iota(jnp.int32, (8, 128), 0)

    def source_of(target):
        value = jnp.zeros((8, 128), jnp.int32)
        for j in range(4):
            value = jnp.where(target == partner[j], j, value)
        return value

    info[0:8, :] = source_of(row >> 2)
    info[8:16, :] = source_of(2 + (row >> 2))
    info[16:24, :] = source_of(row & 3)
    edge = jnp.int32(0)
    for j in range(4):
        edge = edge + jnp.where(partner[j] == 3, j, 0)
    for n, value in enumerate((odd_t, odd_x, sign_ahead, sign_behind, edge)):
        info[24 + 8 * n : 32 + 8 * n, :] = jnp.full((8, 128), value, jnp.int32)


def row_in_pair():
    return lax.broadcasted_iota(jnp.int32, (8, 128), 0) & 3


def send_rows(dst, base, src, k, info, row):
    def spread(j):
        at = k * ROWS + 4 * j + row
        return jnp.broadcast_to(src[at : at + 1, :], (4, 128))

    value = spread(0)
    for j in range(1, 4):
        value = jnp.where(info.face_source[j], spread(j), value)
    dst[base * 4 : base * 4 + 4, :] = value


def send_both(psi_ref, u_ref, info, t_a, t_b, x_a, x_b, mirror, q0, q2, q3, h0, h2):
    for h in range(2):
        psi = spinor(psi_ref, h)
        front = map_half(lambda a: a * info.sign_ahead, project(psi, 1, 1))
        back = map_half(
            lambda a: a * info.sign_behind, mat_dag_half(matrix(u_ref, 1, h), project(psi, 1, -1))
        )
        put_half(t_a, h, map_half(lambda a, b: jnp.where(info.even_t, b, a), front, back))
        put_half(t_b, h, map_half(lambda a, b: jnp.where(info.even_t, a, b), front, back))
        put_half(h0, h, project(psi, 0, 1))
        put_half(h2, h, project(psi, 2, 1))
        for mu, ref in ((0, q0), (2, q2), (3, q3)):
            put_half(ref, h, mat_dag_half(matrix(u_ref, mu, h), project(psi, mu, -1)))
    for k in range(12):
        front = h0[k * ROWS : k * ROWS + 4, :]
        back = q0[k * ROWS + 12 : k * ROWS + 16, :]
        x_a[k * 4 : k * 4 + 4, :] = jnp.where(info.even_x, back, front)
        x_b[k * 4 : k * 4 + 4, :] = jnp.where(info.even_x, front, back)
        send_rows(mirror, k, h2, k, info, 0)
        send_rows(mirror, 12 + k, q2, k, info, 3)


def dirac_rest(psi_ref, u_ref, ahead_t, behind_t, ahead_m, behind_m, q2, q3, fa, fb, acc_ref, w_ref):
    for k in range(12):
        fa[pl.ds(k * ROWS + 3, 4, stride=4), :] = ahead_m(k)
        fb[pl.ds(k * ROWS, 4, stride=4), :] = behind_m(k)
    x2 = row_in_pair()
    for h in range(2):
        psi = spinor(psi_ref, h)
        acc = None
        for mu in (1, 2, 3):
            if mu == 1:
                ahead = get_half(lambda k: ahead_t(k, h))
                behind = get_half(lambda k: behind_t(k, h))
            elif mu == 2:
                raw = project(psi, 2, 1)
                face = get_half(lambda k: ld(fa, k, h))
                ahead = map_half(lambda r, f: jnp.where(x2 == 3, f, pltpu.roll(r, 7, 0)), raw, face)
                behind = get_half(lambda k: jnp.where(x2 == 0, ld(fb, k, h), pltpu.roll(ld(q2, k, h), 1, 0)))
            else:
                ahead = map_half(lambda r: pltpu.roll(r, 127, 1), project(psi, 3, 1))
                behind = get_half(lambda k: pltpu.roll(ld(q3, k, h), 1, 1))
            acc = add_direction(acc, u_ref, w_ref, mu, h, ahead, behind)
        for s in range(4):
            for c in range(3):
                for part in range(2):
                    st(acc_ref, part * 12 + c * 4 + s, h, acc[s][c][part])


def add_direction(acc, u_ref, w_ref, mu, h, ahead, behind):
    w = mat_half(matrix(u_ref, mu, h), ahead)
    if w_ref is not None:
        put_half(w_ref, h, w, (mu - 1) * 12 if mu else 0)
    total = map_half(lambda a, b: a + b, w, behind)
    delta = map_half(lambda a, b: a - b, w, behind)
    source, coef = GAMMA[mu]
    if acc is None:
        zero = jnp.zeros((8, 128), F32)
        acc = [[(zero, zero)] * 3] * 4
    upper = [[cadd(acc[s][c], total[s][c]) for c in range(3)] for s in range(2)]
    lower = [[add_unit(acc[s][c], delta[source[s]][c], coef[s], 1) for c in range(3)] for s in (2, 3)]
    return upper + lower


def dirac_rows(psi_ref, u_ref, acc_ref, ahead_x, behind_x, q0, a0, b0, out_ref, w_ref):
    for k in range(12):
        a0[k * HALO + 16 : k * HALO + 20, :] = ahead_x(k)
        b0[k * HALO : k * HALO + 4, :] = behind_x(k)
        b0[k * HALO + 4 : k * HALO + 20, :] = q0[k * ROWS : k * ROWS + 16, :]
    for h in range(2):
        v = project(spinor(psi_ref, h), 0, 1)
        for t in range(2):
            for c in range(3):
                for part in range(2):
                    k = half_index(part, t, c)
                    a0[k * HALO + 8 * h : k * HALO + 8 * h + 8, :] = v[t][c][part]
    for h in range(2):
        psi = spinor(psi_ref, h)
        ahead = get_half(lambda k: a0[k * HALO + 8 * h + 4 : k * HALO + 8 * h + 12, :])
        behind = get_half(lambda k: b0[k * HALO + 8 * h : k * HALO + 8 * h + 8, :])
        acc = add_direction(spinor(acc_ref, h), u_ref, w_ref, 0, h, ahead, behind)
        for s in range(4):
            for c in range(3):
                for part in range(2):
                    st(out_ref, part * 12 + c * 4 + s, h, psi[s][c][part] - HOPPING * acc[s][c][part])


def rows_of(ref, k):
    return ref[k * 4 : k * 4 + 4, :]


def rest_kernel(info_ref, psi, u, q2, q3, t_a, t_b, mirror, acc, *scratch, w=None):
    info = Info(info_ref)
    dirac_rest(
        psi,
        u,
        lambda k, h: jnp.where(info.even_t, ld(t_a, k, h), ld(t_b, k, h)),
        lambda k, h: jnp.where(info.even_t, ld(t_b, k, h), ld(t_a, k, h)),
        lambda k: rows_of(mirror, k),
        lambda k: rows_of(mirror, 12 + k),
        q2,
        q3,
        *scratch,
        acc,
        w,
    )


def rest_w_kernel(info_ref, psi, u, q2, q3, t_a, t_b, mirror, acc, w, *scratch):
    rest_kernel(info_ref, psi, u, q2, q3, t_a, t_b, mirror, acc, *scratch, w=w)


def rest2_kernel(info_ref, psi, u, q2, q3, t_a, t_b, mirror, b_t, b_m, acc, w, *scratch):
    info = Info(info_ref)
    dirac_rest(
        psi,
        u,
        lambda k, h: jnp.where(info.even_t, ld(t_a, k, h), ld(t_b, k, h)),
        lambda k, h: ld(b_t, k, h),
        lambda k: rows_of(mirror, k),
        lambda k: rows_of(b_m, k),
        q2,
        q3,
        *scratch,
        acc,
        w,
    )


def arrived_rows(info, x_a, x_b):
    return (
        lambda k: jnp.where(info.even_x, rows_of(x_a, k), rows_of(x_b, k)),
        lambda k: jnp.where(info.even_x, rows_of(x_b, k), rows_of(x_a, k)),
    )


def noise_kernel(partner_hbm, index_hbm, table_hbm, u_hbm, *rest):
    psi, t_a, t_b, x_a, x_b, mirror, q0, q2, q3, info_ref = rest[:10]
    flat, parts, h0, h2, table, u, index, partner, sems = rest[10:]
    copies = [
        pltpu.make_async_copy(src, dst, sems.at[n])
        for n, (src, dst) in enumerate(
            (
                (index_hbm, index),
                (table_hbm, table),
                (partner_hbm, partner),
                (u_hbm, u),
            )
        )
    ]
    for copy in copies:
        copy.start()
    copies[1].wait()
    for part in range(2):
        for c in range(3):
            flat[(part * 3 + c) * 4 : (part * 3 + c) * 4 + 4, :] = table[part, c]
    for hi in range(16):
        block = flat[:, hi * 256 : hi * 256 + 256]
        first = block.astype(jnp.bfloat16)
        left = block - first.astype(F32)
        second = left.astype(jnp.bfloat16)
        third = (left - second.astype(F32)).astype(jnp.bfloat16)
        for n, value in enumerate((first, second, third)):
            parts[hi * 24 : hi * 24 + 24, n * 256 : n * 256 + 256] = value
    copies[0].wait()
    low_iota = lax.broadcasted_iota(jnp.int32, (256, 128), 0)
    table_parts = parts[...]
    for r in range(0, 16, 2):
        wanted = [index[r + n : r + n + 1, :] for n in range(2)]
        hot = jnp.concatenate(
            [jnp.where(low_iota == (w & 255), 1.0, 0.0).astype(jnp.bfloat16) for w in wanted], axis=1
        )
        found = jnp.dot(table_parts, jnp.concatenate([hot, hot, hot], axis=0), preferred_element_type=F32)
        for n in range(2):
            high = jnp.broadcast_to(wanted[n] >> 8, (24, 128))
            value = found[0:24, 128 * n : 128 * n + 128]
            for hi in range(1, 16):
                value = jnp.where(high == hi, found[hi * 24 : hi * 24 + 24, 128 * n : 128 * n + 128], value)
            psi[pl.ds(r + n, 24, stride=16), :] = value
    copies[2].wait()
    ta, xd = lax.axis_index("ta"), lax.axis_index("xd")
    sign_ahead = jnp.where(ta == 0, -1, 1)
    sign_behind = jnp.where(ta == lax.axis_size("ta") - 1, -1, 1)
    write_info(info_ref, ta & 1, xd & 1, sign_ahead, sign_behind, [partner[j] & 3 for j in range(4)])
    info = Info(info_ref)
    copies[3].wait()
    send_both(psi, u, info, t_a, t_b, x_a, x_b, mirror, q0, q2, q3, h0, h2)


def phi_kernel(info_ref, psi, u, acc, q0, x_a, x_b, *rest):
    phi, o_ta, o_tb, o_xa, o_xb, o_m, o_q0, o_q2, o_q3, a0, b0, h0, h2 = rest
    info = Info(info_ref)
    dirac_rows(psi, u, acc, *arrived_rows(info, x_a, x_b), q0, a0, b0, phi, None)
    send_both(phi, u, info, o_ta, o_tb, o_xa, o_xb, o_m, o_q0, o_q2, o_q3, h0, h2)


def send_response(y, info, o_t, o_x, o_m, h2):
    for h in range(2):
        v = spinor(y, h)
        put_half(o_t, h, map_half(lambda a: a * info.sign_ahead, project(v, 1, -1)))
        put_half(h2, h, project(v, 2, -1))
        if h == 0:
            face = project(v, 0, -1)
            for t in range(2):
                for c in range(3):
                    for part in range(2):
                        k = half_index(part, t, c)
                        o_x[k * 4 : k * 4 + 4, :] = face[t][c][part][0:4]
    for k in range(12):
        send_rows(o_m, k, h2, k, info, 0)


def response_kernel(info_ref, phi, u, acc, q0, x_a, x_b, *rest):
    y, w, o_t, o_x, o_m, a0, b0, h2 = rest
    info = Info(info_ref)
    dirac_rows(phi, u, acc, *arrived_rows(info, x_a, x_b), q0, a0, b0, y, w)
    send_response(y, info, o_t, o_x, o_m, h2)


def response2_kernel(info_ref, phi, u, acc, q0, x_a, x_b, b_x, *rest):
    y, w, o_t, o_x, o_m, a0, b0, h2 = rest
    info = Info(info_ref)
    ahead_x = arrived_rows(info, x_a, x_b)[0]
    dirac_rows(phi, u, acc, ahead_x, lambda k: rows_of(b_x, k), q0, a0, b0, y, w)
    send_response(y, info, o_t, o_x, o_m, h2)


OFF = ((0, 1), (0, 2), (1, 2))
EARLY = (0, 2, 3)


def force_values(left, right):
    def g_im(i, j):
        return sum(left[n][i][1] * right[n][j][0] - left[n][i][0] * right[n][j][1] for n in range(4))

    def g_re(i, j):
        return sum(left[n][i][0] * right[n][j][0] + left[n][i][1] * right[n][j][1] for n in range(4))

    d = [g_im(i, i) for i in range(3)]
    third = (d[0] + d[1] + d[2]) * (1.0 / 3.0)
    scale = -2.0 * HOPPING
    values = [scale * (d[0] - third), scale * (d[1] - third)]
    for i, j in OFF:
        values.append((0.5 * scale) * (g_im(i, j) + g_im(j, i)))
        values.append((0.5 * scale) * (g_re(j, i) - g_re(i, j)))
    return values


def force_at(at, phi, u, y, w, mu, x):
    ysp = [[(at(y, c * 4 + s), at(y, 12 + c * 4 + s)) for c in range(3)] for s in range(4)]
    psp = [[(at(phi, c * 4 + s), at(phi, 12 + c * 4 + s)) for c in range(3)] for s in range(4)]
    link = [[(at(u, mu * 18 + i * 3 + j), at(u, mu * 18 + 9 + i * 3 + j)) for j in range(3)] for i in range(3)]
    ref, base = (w[1], (mu - 1) * 12) if mu else (w[0], 0)
    left = mat_half(link, x(ysp)) + get_half(lambda k: at(ref, base + k))
    right = project(psp, mu, -1) + project(ysp, mu, 1)
    return force_values(left, right)


def early_force_kernel(info_ref, phi, u, y, w0, w1, force, sent, a0):
    w = (w0, w1)
    info = Info(info_ref)
    nothing = jnp.zeros((4, 128), F32)
    for k in range(12):
        a0[k * HALO + 16 : k * HALO + 20, :] = nothing
    for h in range(2):
        v = project(spinor(y, h), 0, -1)
        for t in range(2):
            for c in range(3):
                for part in range(2):
                    k = half_index(part, t, c)
                    a0[k * HALO + 8 * h : k * HALO + 8 * h + 8, :] = v[t][c][part]
    for h in range(2):
        for e, mu in enumerate(EARLY):
            if mu == 0:
                x = lambda ysp: get_half(lambda k: a0[k * HALO + 8 * h + 4 : k * HALO + 8 * h + 12, :])
            elif mu == 2:
                x = lambda ysp: map_half(lambda r: pltpu.roll(r, 7, 0), project(ysp, 2, -1))
            else:
                x = lambda ysp: map_half(lambda r: pltpu.roll(r, 127, 1), project(ysp, 3, -1))
            for n, value in enumerate(force_at(lambda ref, k: ld(ref, k, h), phi, u, y, w, mu, x)):
                st(force, e * 8 + n, h, value)
    for k in range(24):
        send_blocks(sent, k, force, k, info)


def send_blocks(dst, base, src, k, info):
    low, high = ld(src, k, 0), ld(src, k, 1)
    low_turned, high_turned = pltpu.roll(low, 4, 0), pltpu.roll(high, 4, 0)
    for h in range(2):
        first, second, third = info.block_source[h]
        value = jnp.where(third, high, high_turned)
        value = jnp.where(second, low_turned, value)
        st(dst, base, h, jnp.where(first, low, value))


def late_force_kernel(info_ref, phi, u, y, w0, w1, r_t, r_x, r_m, f_t, f_x, f_m, sent):
    w = (w0, w1)
    info = Info(info_ref)
    for h in range(2):
        arrived = get_half(lambda k: ld(r_t, k, h))
        for n, value in enumerate(force_at(lambda ref, k: ld(ref, k, h), phi, u, y, w, 1, lambda ysp: arrived)):
            st(f_t, n, h, value)
    for n in range(8):
        send_blocks(sent, n, f_t, n, info)
    face = lambda ref: get_half(lambda k: ref[k * 4 : k * 4 + 4, :])
    last_x = lambda ref, k: ref[k * ROWS + 12 : k * ROWS + 16, :]
    for n, value in enumerate(force_at(last_x, phi, u, y, w, 0, lambda ysp: face(r_x))):
        f_x[n * ROWS + 12 : n * ROWS + 16, :] = value
        sent[8 * ROWS + n * 4 : 8 * ROWS + n * 4 + 4, :] = value
    last_m = lambda ref, k: ref[pl.ds(k * ROWS + 3, 4, stride=4), :]
    for n, value in enumerate(force_at(last_m, phi, u, y, w, 2, lambda ysp: face(r_m))):
        f_m[pl.ds(n * ROWS + 3, 4, stride=4), :] = value
    for n in range(8):
        send_rows(sent, 40 + n, f_m, n, info, 3)


def place_faces(mirrored, m_x, m_m):
    for n in range(8):
        face = mirrored[8 * ROWS + n * 4 : 8 * ROWS + n * 4 + 4, :]
        for j in range(4):
            m_x[n * ROWS + 4 * j : n * ROWS + 4 * j + 4, :] = face
        m_m[pl.ds(n * ROWS + 3, 4, stride=4), :] = mirrored[8 * ROWS + 32 + n * 4 : 8 * ROWS + 32 + n * 4 + 4, :]


def both_forces(mu, h, block, early, mirror_early, f_t, f_x, f_m, mirrored, m_x, m_m):
    row = lax.broadcasted_iota(jnp.int32, (8, 128), 0)
    if mu == 1:
        return (lambda n: ld(f_t, n, h)), (lambda n: ld(mirrored, n, h))
    if mu == 2:
        edge = (row & 3) == 3
        return (
            lambda n: jnp.where(edge, ld(f_m, n, h), ld(early, 8 + n, h)),
            lambda n: jnp.where(edge, ld(m_m, n, h), ld(mirror_early, 8 + n, h)),
        )
    edge = (row >> 2) + 2 * h == block
    if h == 0:
        here = lambda n: ld(early, n, h)
    else:
        here = lambda n: jnp.where(row >= 4, ld(f_x, n, h), ld(early, n, h))
    return here, (lambda n: jnp.where(edge, ld(m_x, n, h), ld(mirror_early, n, h)))


def updated_momenta(read, force, mirrored):
    diag_force = [force(n) - mirrored(n) for n in range(2)]
    diag_force.append(-(diag_force[0] + diag_force[1]))
    diag = [read(n) + STEP * diag_force[n] for n in range(3)]
    upper = []
    for n in range(3):
        re = force(2 + 2 * n) - mirrored(2 + 2 * n)
        im = force(3 + 2 * n) + mirrored(3 + 2 * n)
        upper.append((read(3 + 2 * n) + STEP * re, read(4 + 2 * n) + STEP * im))
    return diag, upper


def link_step(diag, upper, u):
    b = [STEP * value for value in diag]
    b01, b02, b12 = ((STEP * value[0], STEP * value[1]) for value in upper)
    n01, n02, n12 = (v[0] * v[0] + v[1] * v[1] for v in (b01, b02, b12))
    square_diag = [b[0] * b[0] + n01 + n02, b[1] * b[1] + n01 + n12, b[2] * b[2] + n02 + n12]

    def scaled(v, by):
        return (v[0] * by, v[1] * by)

    square = [
        cadd(scaled(b01, b[0] + b[1]), cmul_conj(b02, b12)),
        cadd(scaled(b02, b[0] + b[2]), cmul(b01, b12)),
        cadd(scaled(b12, b[1] + b[2]), cmul_conj(b02, b01)),
    ]
    c1 = 0.5 * (square_diag[0] + square_diag[1] + square_diag[2])
    triple = cmul_conj(cmul(b01, b12), b02)[0]
    c0 = b[0] * (b[1] * b[2] - n12) - b[1] * n02 - b[2] * n01 + 2.0 * triple
    i0 = c0 * (-1.0 / 60)
    r1 = (1.0 / 3 - c1 * (1.0 / 60), c0 * (-1.0 / 360))
    r2 = 1.0 / 12 - c1 * (1.0 / 360)
    i0, r1, r2 = (r2 * c0) * -0.5, (0.5 - (r2 * c1) * 0.5, i0 * 0.5), (r1[0] * 0.5, r1[1] * 0.5)
    r0, r1, r2 = (1.0 + r2[1] * c0, -(r2[0] * c0)), (1.0 - r2[0] * c1, i0 - r2[1] * c1), r1
    ir1 = (-r1[1], r1[0])
    e = [[None] * 3 for _ in range(3)]
    for i in range(3):
        e[i][i] = cadd(r0, csub(scaled(ir1, b[i]), scaled(r2, square_diag[i])))
    for (i, j), v, s in zip(OFF, (b01, b02, b12), square):
        e[i][j] = csub(cmul(ir1, v), cmul(r2, s))
        e[j][i] = csub(cmul_conj(ir1, v), cmul_conj(r2, s))
    return [[cadd(cadd(cmul(e[i][0], u[0][j]), cmul(e[i][1], u[1][j])), cmul(e[i][2], u[2][j])) for j in range(3)] for i in range(3)]


def input_momentum(ref, mu, h):
    def read(n):
        if n < 3:
            return ld(ref, mu * 18 + 4 * n, h)
        i, j = OFF[(n - 3) // 2]
        return ld(ref, mu * 18 + 9 * ((n - 3) % 2) + 3 * i + j, h)

    return read


def put_matrix(ref, mu, h, value):
    for i in range(3):
        for j in range(3):
            for part in range(2):
                st(ref, mu * 18 + part * 9 + i * 3 + j, h, value[i][j][part])


def put_momenta(ref, base, h, diag, upper):
    for n in range(3):
        st(ref, base + n, h, diag[n])
        st(ref, base + 3 + 2 * n, h, upper[n][0])
        st(ref, base + 4 + 2 * n, h, upper[n][1])


def put_full_momenta(new_p, old_p, at, mu, h, diag, upper):
    for i in range(3):
        st(new_p, at * 18 + 4 * i, h, diag[i])
        st(new_p, at * 18 + 9 + 4 * i, h, ld(old_p, mu * 18 + 9 + 4 * i, h))
    for (i, j), v in zip(OFF, upper):
        st(new_p, at * 18 + 3 * i + j, h, v[0])
        st(new_p, at * 18 + 3 * j + i, h, v[0])
        st(new_p, at * 18 + 9 + 3 * i + j, h, v[1])
        st(new_p, at * 18 + 9 + 3 * j + i, h, -v[1])


def early_update_kernel(phi, u, p, early, mirror_early, new_u, new_p, q3):
    for h in range(2):
        force, mirrored = (lambda n: ld(early, 16 + n, h)), (lambda n: ld(mirror_early, 16 + n, h))
        diag, upper = updated_momenta(input_momentum(p, 3, h), force, mirrored)
        put_momenta(new_p, 0, h, diag, upper)
        link = link_step(diag, upper, matrix(u, 3, h))
        put_matrix(new_u, 0, h, link)
        put_half(q3, h, mat_dag_half(link, project(spinor(phi, h), 3, -1)))


def early_last_kernel(u, p, old_p, early, mirror_early, new_u, new_p):
    for h in range(2):
        force, mirrored = (lambda n: ld(early, 16 + n, h)), (lambda n: ld(mirror_early, 16 + n, h))
        diag, upper = updated_momenta(lambda n: ld(p, 27 + n, h), force, mirrored)
        put_full_momenta(new_p, old_p, 0, 3, h, diag, upper)
        put_matrix(new_u, 0, h, link_step(diag, upper, matrix(u, 3, h)))


def update_kernel(info_ref, phi, u, p, u3, p3, *rest):
    forces = rest[:6]
    new_u, new_p, o_t, o_x, o_m, q0, q2, m_x, m_m = rest[6:]
    info = Info(info_ref)
    place_faces(forces[5], m_x, m_m)
    for h in range(2):
        psi = spinor(phi, h)
        for mu in range(3):
            diag, upper = updated_momenta(
                input_momentum(p, mu, h), *both_forces(mu, h, info.edge_block, *forces, m_x, m_m)
            )
            put_momenta(new_p, mu * 9, h, diag, upper)
            link = link_step(diag, upper, matrix(u, mu, h))
            put_matrix(new_u, mu, h, link)
            back = mat_dag_half(link, project(psi, mu, -1))
            if mu == 1:
                put_half(o_t, h, map_half(lambda a: a * info.sign_behind, back))
            else:
                put_half({0: q0, 2: q2}[mu], h, back)
    new_u[54 * ROWS : 72 * ROWS, :] = u3[...]
    new_p[27 * ROWS : 36 * ROWS, :] = p3[...]
    for k in range(12):
        o_x[k * 4 : k * 4 + 4, :] = q0[k * ROWS + 12 : k * ROWS + 16, :]
        send_rows(o_m, k, q2, k, info, 3)


def last_kernel(info_ref, u, p, old_p, u3, p3, *rest):
    forces = rest[:6]
    out_u, out_p, new_u, new_p, m_x, m_m, sems = rest[6:]
    info = Info(info_ref)
    size = 18 * ROWS
    copies = []

    def send(src, dst, mu):
        copies.append(pltpu.make_async_copy(src, dst.at[mu * size : mu * size + size, :], sems.at[len(copies)]))
        copies[-1].start()

    send(u3, out_u, 3)
    send(p3, out_p, 3)
    place_faces(forces[5], m_x, m_m)
    for mu in range(3):
        for h in range(2):
            diag, upper = updated_momenta(
                lambda n: ld(p, mu * 9 + n, h), *both_forces(mu, h, info.edge_block, *forces, m_x, m_m)
            )
            put_full_momenta(new_p, old_p, mu, mu, h, diag, upper)
            put_matrix(new_u, mu, h, link_step(diag, upper, matrix(u, mu, h)))
        send(new_p.at[mu * size : mu * size + size, :], out_p, mu)
        send(new_u.at[mu * size : mu * size + size, :], out_u, mu)
    for copy in copies:
        copy.wait()


VM = pl.BlockSpec(memory_space=pltpu.VMEM)
HBM = pl.BlockSpec(memory_space=pltpu.HBM)
FULL = ROWS * 12
FACE = 4 * 12


def call(kernel, args, outs, scratch, limit=4, from_hbm=False, to_hbm=False):
    return pl.pallas_call(
        kernel,
        out_shape=[jax.ShapeDtypeStruct((s, 128), F32) if isinstance(s, int) else s for s in outs],
        in_specs=[HBM if from_hbm else VM] * len(args),
        out_specs=[HBM if to_hbm else VM] * len(outs),
        scratch_shapes=[s if not isinstance(s, int) else pltpu.VMEM((s, 128), F32) for s in scratch],
        compiler_params=pltpu.CompilerParams(vmem_limit_bytes=limit << 20),
    )(*args)


def swap(value, axis, far):
    n = lax.axis_size(axis)
    if far:
        pairs = [(i, (i + 1) % n if i % 2 else (i - 1) % n) for i in range(n)]
    else:
        pairs = [(i, i ^ 1) for i in range(n)]
    return lax.ppermute(value, axis, pairs)


def shift(value, axis, by):
    n = lax.axis_size(axis)
    return lax.ppermute(value, axis, [(i, (i + by) % n) for i in range(n)])


def mirror_swap(value):
    n = lax.axis_size("xd")
    return lax.ppermute(value, "xd", [(i, i ^ (n // 2)) for i in range(n)])


def moved(name, value):
    if name == "far_t":
        return swap(value, "ta", True)
    if name == "near_t":
        return swap(value, "ta", False)
    if name == "far_x":
        return swap(value, "xd", True)
    if name == "near_x":
        return swap(value, "xd", False)
    if name == "back_t":
        return shift(value, "ta", -1)
    if name == "back_x":
        return shift(value, "xd", -1)
    if name == "on_t":
        return shift(value, "ta", 1)
    if name == "on_x":
        return shift(value, "xd", 1)
    return mirror_swap(value)


SWAP_ORDER = ("far_t", "mirror", "far_x", "near_x", "near_t")
BACK_ORDER = ("mirror", "back_t", "back_x", "early")
ON_ORDER = ("on_t", "mirror", "on_x")


def exchange(order, **values):
    return {name: moved(name, values[name]) for name in order}


def swap_exchange(t_a, t_b, x_a, x_b, m):
    got = exchange(SWAP_ORDER, near_t=t_a, far_t=t_b, near_x=x_a, far_x=x_b, mirror=m)
    return [got[name] for name in ("near_t", "far_t", "near_x", "far_x", "mirror")]


def all_forces(masks, phi, u, y, w, o_t, o_x, o_m):
    early, sent = call(early_force_kernel, (masks, phi, u, y, *w), [24 * ROWS, 24 * ROWS], [12 * HALO])
    got = exchange(BACK_ORDER, back_t=o_t, back_x=o_x, mirror=o_m, early=sent)
    f_t, f_x, f_m, sent = call(
        late_force_kernel,
        (masks, phi, u, y, *w, got["back_t"], got["back_x"], got["mirror"]),
        [8 * ROWS, 8 * ROWS, 8 * ROWS, 12 * ROWS],
        [],
    )
    late = exchange(("mirror",), mirror=sent)["mirror"]
    return early, got["early"], f_t, f_x, f_m, late


def on_exchange(t, x, m):
    got = exchange(ON_ORDER, on_t=t, on_x=x, mirror=m)
    return [got[name] for name in ("on_t", "on_x", "mirror")]


def per_device(gauge_links, momenta, noise_table, noise_index, partner):
    u = gauge_links.reshape(72 * ROWS, 128)
    p = momenta.reshape(72 * ROWS, 128)
    table = jnp.transpose(noise_table, (0, 2, 1, 3))
    index = noise_index.reshape(ROWS, 128)
    messages = [FULL, FULL, FACE, FACE, 2 * FACE]
    local = [FULL, FULL, FULL]
    halo = [12 * HALO, 12 * HALO]
    spin = 24 * ROWS

    psi, *rest, masks = call(
        noise_kernel,
        [pltpu.with_memory_space_constraint(v, pltpu.HBM) for v in (partner, index, table, u)],
        [spin] + messages + local + [jax.ShapeDtypeStruct((INFO_ROWS, 128), jnp.int32)],
        [
            pltpu.VMEM((24, 4096), F32),
            pltpu.VMEM((384, 768), jnp.bfloat16),
            FULL,
            FULL,
            pltpu.VMEM((2, 3, 4, 4096), F32),
            72 * ROWS,
            pltpu.VMEM((ROWS, 128), jnp.int32),
            pltpu.SMEM((4,), jnp.int32),
            pltpu.SemaphoreType.DMA((4,)),
        ],
        12,
        from_hbm=True,
    )
    t_a, t_b, x_a, x_b, m = swap_exchange(*rest[:5])
    q0, q2, q3 = rest[5:]
    (acc,) = call(rest_kernel, (masks, psi, u, q2, q3, t_a, t_b, m), [spin], [FULL, FULL])
    phi, *rest = call(phi_kernel, (masks, psi, u, acc, q0, x_a, x_b), [spin] + messages + local, halo + [FULL, FULL])
    t_a, t_b, x_a, x_b, m = swap_exchange(*rest[:5])
    q0, q2, q3 = rest[5:]
    acc, w1 = call(rest_w_kernel, (masks, phi, u, q2, q3, t_a, t_b, m), [spin, 3 * FULL], [FULL, FULL])
    y, w0, o_t, o_x, o_m = call(
        response_kernel, (masks, phi, u, acc, q0, x_a, x_b), [spin, FULL, FULL, FACE, FACE], halo + [FULL]
    )
    w = (w0, w1)
    forces = all_forces(masks, phi, u, y, w, o_t, o_x, o_m)
    u3, p3, q3 = call(early_update_kernel, (phi, u, p, *forces[:2]), [18 * ROWS, 9 * ROWS, FULL], [])
    u, p1, o_t, o_x, o_m, q0, q2 = call(
        update_kernel,
        (masks, phi, u, p, u3, p3, *forces),
        [72 * ROWS, 36 * ROWS, FULL, FACE, FACE, FULL, FULL],
        [8 * ROWS, 8 * ROWS],
    )
    b_t, b_x, b_m = on_exchange(o_t, o_x, o_m)
    acc, w1 = call(rest2_kernel, (masks, phi, u, q2, q3, t_a, t_b, m, b_t, b_m), [spin, 3 * FULL], [FULL, FULL])
    y, w0, o_t, o_x, o_m = call(
        response2_kernel, (masks, phi, u, acc, q0, x_a, x_b, b_x), [spin, FULL, FULL, FACE, FACE], halo + [FULL]
    )
    w = (w0, w1)
    forces = all_forces(masks, phi, u, y, w, o_t, o_x, o_m)
    u3, p3 = call(early_last_kernel, (u, p1, p, *forces[:2]), [18 * ROWS, 18 * ROWS], [])
    new_u, new_p = call(
        last_kernel,
        (masks, u, p1, p, u3, p3, *forces),
        [72 * ROWS, 72 * ROWS],
        [54 * ROWS, 54 * ROWS, 8 * ROWS, 8 * ROWS, pltpu.SemaphoreType.DMA((8,))],
        to_hbm=True,
    )
    return new_u.reshape(gauge_links.shape), new_p.reshape(momenta.shape)


def solution(mesh):
    sites = P(None, None, None, None, "xd", "ta", None, None)
    return jax.shard_map(
        per_device,
        mesh=mesh,
        in_specs=(sites, sites, P(), P("xd", "ta", None, None), P("xd")),
        out_specs=(sites, sites),
        check_vma=False,
    )
```

```python
import jax
import jax.numpy as jnp
from jax import lax
from jax.experimental import pallas as pl
from jax.experimental.pallas import tpu as pltpu
from jax.sharding import PartitionSpec as P


HOPPING = 0.13
STEP = 0.25
F32 = jnp.float32
GAMMA = (
    ((3, 2, 1, 0), ((0, 1), (0, 1), (0, -1), (0, -1))),
    ((2, 3, 0, 1), ((1, 0), (1, 0), (1, 0), (1, 0))),
    ((3, 2, 1, 0), ((-1, 0), (1, 0), (1, 0), (-1, 0))),
    ((2, 3, 0, 1), ((0, 1), (0, -1), (0, -1), (0, 1))),
)
ROWS = 16
HALO = 24


def ld(ref, k, h):
    return ref[k * ROWS + 8 * h : k * ROWS + 8 * h + 8, :]


def st(ref, k, h, value):
    ref[k * ROWS + 8 * h : k * ROWS + 8 * h + 8, :] = value


def cadd(a, b):
    return (a[0] + b[0], a[1] + b[1])


def csub(a, b):
    return (a[0] - b[0], a[1] - b[1])


def cmul(a, b):
    return (a[0] * b[0] - a[1] * b[1], a[0] * b[1] + a[1] * b[0])


def cmul_conj(a, b):
    return (a[0] * b[0] + a[1] * b[1], a[1] * b[0] - a[0] * b[1])


def add_unit(x, y, coef, sign):
    re, im = coef
    if re:
        if re * sign > 0:
            return cadd(x, y)
        return csub(x, y)
    if im * sign > 0:
        return (x[0] - y[1], x[1] + y[0])
    return (x[0] + y[1], x[1] - y[0])


def spinor(ref, h):
    return [[(ld(ref, c * 4 + s, h), ld(ref, 12 + c * 4 + s, h)) for c in range(3)] for s in range(4)]


def project(psi, mu, sign):
    source, coef = GAMMA[mu]
    return [[add_unit(psi[t][c], psi[source[t]][c], coef[t], sign) for c in range(3)] for t in range(2)]


def matrix(ref, mu, h):
    return [[(ld(ref, mu * 18 + i * 3 + j, h), ld(ref, mu * 18 + 9 + i * 3 + j, h)) for j in range(3)] for i in range(3)]


def mat_half(u, v):
    out = []
    for t in range(2):
        row = []
        for i in range(3):
            acc = cmul(u[i][0], v[t][0])
            for j in (1, 2):
                acc = cadd(acc, cmul(u[i][j], v[t][j]))
            row.append(acc)
        out.append(row)
    return out


def mat_dag_half(u, v):
    out = []
    for t in range(2):
        row = []
        for i in range(3):
            acc = cmul_conj(v[t][0], u[0][i])
            for j in (1, 2):
                acc = cadd(acc, cmul_conj(v[t][j], u[j][i]))
            row.append(acc)
        out.append(row)
    return out


def half_index(part, t, c):
    return part * 6 + t * 3 + c


def put_half(ref, h, v, base=0):
    for t in range(2):
        for c in range(3):
            for part in range(2):
                st(ref, base + half_index(part, t, c), h, v[t][c][part])


def get_half(fn):
    return [[tuple(fn(half_index(part, t, c)) for part in range(2)) for c in range(3)] for t in range(2)]


def map_half(fn, *vs):
    return [[tuple(fn(*(v[t][c][part] for v in vs)) for part in range(2)) for c in range(3)] for t in range(2)]


INFO_ROWS = 64


class Info:
    def __init__(self, info):
        self.even_t = info[24:32, :] == 0
        self.even_x = info[32:36, :] == 0
        self.sign_ahead = info[40:48, :].astype(F32)
        self.sign_behind = info[48:56, :].astype(F32)
        self.face_source = [info[16:20, :] == j for j in range(4)]
        self.edge_block = info[56:64, :]
        half = row_block()
        self.block_source = []
        for h in range(2):
            source = info[8 * h : 8 * h + 8, :]
            self.block_source.append((source == half, source == 1 - half, source == 2 + half))


def row_block():
    return lax.broadcasted_iota(jnp.int32, (8, 128), 0) >> 2


def write_info(info, odd_t, odd_x, sign_ahead, sign_behind, partner):
    row = lax.broadcasted_iota(jnp.int32, (8, 128), 0)

    def source_of(target):
        value = jnp.zeros((8, 128), jnp.int32)
        for j in range(4):
            value = jnp.where(target == partner[j], j, value)
        return value

    info[0:8, :] = source_of(row >> 2)
    info[8:16, :] = source_of(2 + (row >> 2))
    info[16:24, :] = source_of(row & 3)
    edge = jnp.int32(0)
    for j in range(4):
        edge = edge + jnp.where(partner[j] == 3, j, 0)
    for n, value in enumerate((odd_t, odd_x, sign_ahead, sign_behind, edge)):
        info[24 + 8 * n : 32 + 8 * n, :] = jnp.full((8, 128), value, jnp.int32)


def row_in_pair():
    return lax.broadcasted_iota(jnp.int32, (8, 128), 0) & 3


def send_rows(dst, base, src, k, info, row):
    def spread(j):
        at = k * ROWS + 4 * j + row
        return jnp.broadcast_to(src[at : at + 1, :], (4, 128))

    value = spread(0)
    for j in range(1, 4):
        value = jnp.where(info.face_source[j], spread(j), value)
    dst[base * 4 : base * 4 + 4, :] = value


def send_both(psi_ref, u_ref, info, t_a, t_b, x_a, x_b, mirror, q0, q2, q3, h0, h2):
    for h in range(2):
        psi = spinor(psi_ref, h)
        front = map_half(lambda a: a * info.sign_ahead, project(psi, 1, 1))
        back = map_half(
            lambda a: a * info.sign_behind, mat_dag_half(matrix(u_ref, 1, h), project(psi, 1, -1))
        )
        put_half(t_a, h, map_half(lambda a, b: jnp.where(info.even_t, b, a), front, back))
        put_half(t_b, h, map_half(lambda a, b: jnp.where(info.even_t, a, b), front, back))
        put_half(h0, h, project(psi, 0, 1))
        put_half(h2, h, project(psi, 2, 1))
        for mu, ref in ((0, q0), (2, q2), (3, q3)):
            put_half(ref, h, mat_dag_half(matrix(u_ref, mu, h), project(psi, mu, -1)))
    for k in range(12):
        front = h0[k * ROWS : k * ROWS + 4, :]
        back = q0[k * ROWS + 12 : k * ROWS + 16, :]
        x_a[k * 4 : k * 4 + 4, :] = jnp.where(info.even_x, back, front)
        x_b[k * 4 : k * 4 + 4, :] = jnp.where(info.even_x, front, back)
        send_rows(mirror, k, h2, k, info, 0)
        send_rows(mirror, 12 + k, q2, k, info, 3)


def dirac_rest(psi_ref, u_ref, ahead_t, behind_t, ahead_m, behind_m, q2, q3, fa, fb, acc_ref, w_ref):
    for k in range(12):
        fa[pl.ds(k * ROWS + 3, 4, stride=4), :] = ahead_m(k)
        fb[pl.ds(k * ROWS, 4, stride=4), :] = behind_m(k)
    x2 = row_in_pair()
    for h in range(2):
        psi = spinor(psi_ref, h)
        acc = None
        for mu in (1, 2, 3):
            if mu == 1:
                ahead = get_half(lambda k: ahead_t(k, h))
                behind = get_half(lambda k: behind_t(k, h))
            elif mu == 2:
                raw = project(psi, 2, 1)
                face = get_half(lambda k: ld(fa, k, h))
                ahead = map_half(lambda r, f: jnp.where(x2 == 3, f, pltpu.roll(r, 7, 0)), raw, face)
                behind = get_half(lambda k: jnp.where(x2 == 0, ld(fb, k, h), pltpu.roll(ld(q2, k, h), 1, 0)))
            else:
                ahead = map_half(lambda r: pltpu.roll(r, 127, 1), project(psi, 3, 1))
                behind = get_half(lambda k: pltpu.roll(ld(q3, k, h), 1, 1))
            acc = add_direction(acc, u_ref, w_ref, mu, h, ahead, behind)
        for s in range(4):
            for c in range(3):
                for part in range(2):
                    st(acc_ref, part * 12 + c * 4 + s, h, acc[s][c][part])


def add_direction(acc, u_ref, w_ref, mu, h, ahead, behind):
    w = mat_half(matrix(u_ref, mu, h), ahead)
    if w_ref is not None:
        put_half(w_ref, h, w, (mu - 1) * 12 if mu else 0)
    total = map_half(lambda a, b: a + b, w, behind)
    delta = map_half(lambda a, b: a - b, w, behind)
    source, coef = GAMMA[mu]
    if acc is None:
        zero = jnp.zeros((8, 128), F32)
        acc = [[(zero, zero)] * 3] * 4
    upper = [[cadd(acc[s][c], total[s][c]) for c in range(3)] for s in range(2)]
    lower = [[add_unit(acc[s][c], delta[source[s]][c], coef[s], 1) for c in range(3)] for s in (2, 3)]
    return upper + lower


def dirac_rows(psi_ref, u_ref, acc_ref, ahead_x, behind_x, q0, a0, b0, out_ref, w_ref):
    for k in range(12):
        a0[k * HALO + 16 : k * HALO + 20, :] = ahead_x(k)
        b0[k * HALO : k * HALO + 4, :] = behind_x(k)
        b0[k * HALO + 4 : k * HALO + 20, :] = q0[k * ROWS : k * ROWS + 16, :]
    for h in range(2):
        v = project(spinor(psi_ref, h), 0, 1)
        for t in range(2):
            for c in range(3):
                for part in range(2):
                    k = half_index(part, t, c)
                    a0[k * HALO + 8 * h : k * HALO + 8 * h + 8, :] = v[t][c][part]
    for h in range(2):
        psi = spinor(psi_ref, h)
        ahead = get_half(lambda k: a0[k * HALO + 8 * h + 4 : k * HALO + 8 * h + 12, :])
        behind = get_half(lambda k: b0[k * HALO + 8 * h : k * HALO + 8 * h + 8, :])
        acc = add_direction(spinor(acc_ref, h), u_ref, w_ref, 0, h, ahead, behind)
        for s in range(4):
            for c in range(3):
                for part in range(2):
                    st(out_ref, part * 12 + c * 4 + s, h, psi[s][c][part] - HOPPING * acc[s][c][part])


def rows_of(ref, k):
    return ref[k * 4 : k * 4 + 4, :]


def rest_kernel(info_ref, psi, u, q2, q3, t_a, t_b, mirror, acc, *scratch, w=None):
    info = Info(info_ref)
    dirac_rest(
        psi,
        u,
        lambda k, h: jnp.where(info.even_t, ld(t_a, k, h), ld(t_b, k, h)),
        lambda k, h: jnp.where(info.even_t, ld(t_b, k, h), ld(t_a, k, h)),
        lambda k: rows_of(mirror, k),
        lambda k: rows_of(mirror, 12 + k),
        q2,
        q3,
        *scratch,
        acc,
        w,
    )


def rest_w_kernel(info_ref, psi, u, q2, q3, t_a, t_b, mirror, acc, w, *scratch):
    rest_kernel(info_ref, psi, u, q2, q3, t_a, t_b, mirror, acc, *scratch, w=w)


def rest2_kernel(info_ref, psi, u, q2, q3, t_a, t_b, mirror, b_t, b_m, acc, w, *scratch):
    info = Info(info_ref)
    dirac_rest(
        psi,
        u,
        lambda k, h: jnp.where(info.even_t, ld(t_a, k, h), ld(t_b, k, h)),
        lambda k, h: ld(b_t, k, h),
        lambda k: rows_of(mirror, k),
        lambda k: rows_of(b_m, k),
        q2,
        q3,
        *scratch,
        acc,
        w,
    )


def arrived_rows(info, x_a, x_b):
    return (
        lambda k: jnp.where(info.even_x, rows_of(x_a, k), rows_of(x_b, k)),
        lambda k: jnp.where(info.even_x, rows_of(x_b, k), rows_of(x_a, k)),
    )


def noise_kernel(partner_hbm, index_hbm, table_hbm, u_hbm, *rest):
    psi, t_a, t_b, x_a, x_b, mirror, q0, q2, q3, info_ref, u = rest[:11]
    flat, parts, h0, h2, table, index, partner, sems = rest[11:]
    copies = [
        pltpu.make_async_copy(src, dst, sems.at[n])
        for n, (src, dst) in enumerate(
            (
                (index_hbm, index),
                (table_hbm, table),
                (partner_hbm, partner),
                (u_hbm, u),
            )
        )
    ]
    for copy in copies:
        copy.start()
    copies[1].wait()
    for part in range(2):
        for c in range(3):
            flat[(part * 3 + c) * 4 : (part * 3 + c) * 4 + 4, :] = table[part, c]
    for hi in range(16):
        block = flat[:, hi * 256 : hi * 256 + 256]
        first = block.astype(jnp.bfloat16)
        left = block - first.astype(F32)
        second = left.astype(jnp.bfloat16)
        third = (left - second.astype(F32)).astype(jnp.bfloat16)
        for n, value in enumerate((first, second, third)):
            parts[hi * 24 : hi * 24 + 24, n * 256 : n * 256 + 256] = value
    copies[0].wait()
    low_iota = lax.broadcasted_iota(jnp.int32, (256, 128), 0)
    table_parts = parts[...]
    for r in range(0, 16, 2):
        wanted = [index[r + n : r + n + 1, :] for n in range(2)]
        hot = jnp.concatenate(
            [jnp.where(low_iota == (w & 255), 1.0, 0.0).astype(jnp.bfloat16) for w in wanted], axis=1
        )
        found = jnp.dot(table_parts, jnp.concatenate([hot, hot, hot], axis=0), preferred_element_type=F32)
        for n in range(2):
            high = jnp.broadcast_to(wanted[n] >> 8, (24, 128))
            value = found[0:24, 128 * n : 128 * n + 128]
            for hi in range(1, 16):
                value = jnp.where(high == hi, found[hi * 24 : hi * 24 + 24, 128 * n : 128 * n + 128], value)
            psi[pl.ds(r + n, 24, stride=16), :] = value
    copies[2].wait()
    ta, xd = lax.axis_index("ta"), lax.axis_index("xd")
    sign_ahead = jnp.where(ta == 0, -1, 1)
    sign_behind = jnp.where(ta == lax.axis_size("ta") - 1, -1, 1)
    write_info(info_ref, ta & 1, xd & 1, sign_ahead, sign_behind, [partner[j] & 3 for j in range(4)])
    info = Info(info_ref)
    copies[3].wait()
    send_both(psi, u, info, t_a, t_b, x_a, x_b, mirror, q0, q2, q3, h0, h2)


def phi_kernel(info_ref, psi, u, acc, q0, x_a, x_b, *rest):
    phi, o_ta, o_tb, o_xa, o_xb, o_m, o_q0, o_q2, o_q3, a0, b0, h0, h2 = rest
    info = Info(info_ref)
    dirac_rows(psi, u, acc, *arrived_rows(info, x_a, x_b), q0, a0, b0, phi, None)
    send_both(phi, u, info, o_ta, o_tb, o_xa, o_xb, o_m, o_q0, o_q2, o_q3, h0, h2)


def send_response(y, info, o_t, o_x, o_m, h2):
    for h in range(2):
        v = spinor(y, h)
        put_half(o_t, h, map_half(lambda a: a * info.sign_ahead, project(v, 1, -1)))
        put_half(h2, h, project(v, 2, -1))
        if h == 0:
            face = project(v, 0, -1)
            for t in range(2):
                for c in range(3):
                    for part in range(2):
                        k = half_index(part, t, c)
                        o_x[k * 4 : k * 4 + 4, :] = face[t][c][part][0:4]
    for k in range(12):
        send_rows(o_m, k, h2, k, info, 0)


def response_kernel(info_ref, phi, u, acc, q0, x_a, x_b, *rest):
    y, w, o_t, o_x, o_m, a0, b0, h2 = rest
    info = Info(info_ref)
    dirac_rows(phi, u, acc, *arrived_rows(info, x_a, x_b), q0, a0, b0, y, w)
    send_response(y, info, o_t, o_x, o_m, h2)


def response2_kernel(info_ref, phi, u, acc, q0, x_a, x_b, b_x, *rest):
    y, w, o_t, o_x, o_m, a0, b0, h2 = rest
    info = Info(info_ref)
    ahead_x = arrived_rows(info, x_a, x_b)[0]
    dirac_rows(phi, u, acc, ahead_x, lambda k: rows_of(b_x, k), q0, a0, b0, y, w)
    send_response(y, info, o_t, o_x, o_m, h2)


OFF = ((0, 1), (0, 2), (1, 2))
EARLY = (0, 2, 3)


def force_values(left, right):
    def g_im(i, j):
        return sum(left[n][i][1] * right[n][j][0] - left[n][i][0] * right[n][j][1] for n in range(4))

    def g_re(i, j):
        return sum(left[n][i][0] * right[n][j][0] + left[n][i][1] * right[n][j][1] for n in range(4))

    d = [g_im(i, i) for i in range(3)]
    third = (d[0] + d[1] + d[2]) * (1.0 / 3.0)
    scale = -2.0 * HOPPING
    values = [scale * (d[0] - third), scale * (d[1] - third)]
    for i, j in OFF:
        values.append((0.5 * scale) * (g_im(i, j) + g_im(j, i)))
        values.append((0.5 * scale) * (g_re(j, i) - g_re(i, j)))
    return values


def force_at(at, phi, u, y, w, mu, x):
    ysp = [[(at(y, c * 4 + s), at(y, 12 + c * 4 + s)) for c in range(3)] for s in range(4)]
    psp = [[(at(phi, c * 4 + s), at(phi, 12 + c * 4 + s)) for c in range(3)] for s in range(4)]
    link = [[(at(u, mu * 18 + i * 3 + j), at(u, mu * 18 + 9 + i * 3 + j)) for j in range(3)] for i in range(3)]
    ref, base = (w[1], (mu - 1) * 12) if mu else (w[0], 0)
    left = mat_half(link, x(ysp)) + get_half(lambda k: at(ref, base + k))
    right = project(psp, mu, -1) + project(ysp, mu, 1)
    return force_values(left, right)


def early_force_kernel(info_ref, phi, u, y, w0, w1, force, sent, a0):
    w = (w0, w1)
    info = Info(info_ref)
    nothing = jnp.zeros((4, 128), F32)
    for k in range(12):
        a0[k * HALO + 16 : k * HALO + 20, :] = nothing
    for h in range(2):
        v = project(spinor(y, h), 0, -1)
        for t in range(2):
            for c in range(3):
                for part in range(2):
                    k = half_index(part, t, c)
                    a0[k * HALO + 8 * h : k * HALO + 8 * h + 8, :] = v[t][c][part]
    for h in range(2):
        for e, mu in enumerate(EARLY):
            if mu == 0:
                x = lambda ysp: get_half(lambda k: a0[k * HALO + 8 * h + 4 : k * HALO + 8 * h + 12, :])
            elif mu == 2:
                x = lambda ysp: map_half(lambda r: pltpu.roll(r, 7, 0), project(ysp, 2, -1))
            else:
                x = lambda ysp: map_half(lambda r: pltpu.roll(r, 127, 1), project(ysp, 3, -1))
            for n, value in enumerate(force_at(lambda ref, k: ld(ref, k, h), phi, u, y, w, mu, x)):
                st(force, e * 8 + n, h, value)
    for k in range(24):
        send_blocks(sent, k, force, k, info)


def send_blocks(dst, base, src, k, info):
    low, high = ld(src, k, 0), ld(src, k, 1)
    low_turned, high_turned = pltpu.roll(low, 4, 0), pltpu.roll(high, 4, 0)
    for h in range(2):
        first, second, third = info.block_source[h]
        value = jnp.where(third, high, high_turned)
        value = jnp.where(second, low_turned, value)
        st(dst, base, h, jnp.where(first, low, value))


def late_force_kernel(info_ref, phi, u, y, w0, w1, r_t, r_x, r_m, f_t, f_x, f_m, sent):
    w = (w0, w1)
    info = Info(info_ref)
    for h in range(2):
        arrived = get_half(lambda k: ld(r_t, k, h))
        for n, value in enumerate(force_at(lambda ref, k: ld(ref, k, h), phi, u, y, w, 1, lambda ysp: arrived)):
            st(f_t, n, h, value)
    for n in range(8):
        send_blocks(sent, n, f_t, n, info)
    face = lambda ref: get_half(lambda k: ref[k * 4 : k * 4 + 4, :])
    last_x = lambda ref, k: ref[k * ROWS + 12 : k * ROWS + 16, :]
    for n, value in enumerate(force_at(last_x, phi, u, y, w, 0, lambda ysp: face(r_x))):
        f_x[n * ROWS + 12 : n * ROWS + 16, :] = value
        sent[8 * ROWS + n * 4 : 8 * ROWS + n * 4 + 4, :] = value
    last_m = lambda ref, k: ref[pl.ds(k * ROWS + 3, 4, stride=4), :]
    for n, value in enumerate(force_at(last_m, phi, u, y, w, 2, lambda ysp: face(r_m))):
        f_m[pl.ds(n * ROWS + 3, 4, stride=4), :] = value
    for n in range(8):
        send_rows(sent, 40 + n, f_m, n, info, 3)


def place_faces(mirrored, m_x, m_m):
    for n in range(8):
        face = mirrored[8 * ROWS + n * 4 : 8 * ROWS + n * 4 + 4, :]
        for j in range(4):
            m_x[n * ROWS + 4 * j : n * ROWS + 4 * j + 4, :] = face
        m_m[pl.ds(n * ROWS + 3, 4, stride=4), :] = mirrored[8 * ROWS + 32 + n * 4 : 8 * ROWS + 32 + n * 4 + 4, :]


def both_forces(mu, h, block, early, mirror_early, f_t, f_x, f_m, mirrored, m_x, m_m):
    row = lax.broadcasted_iota(jnp.int32, (8, 128), 0)
    if mu == 1:
        return (lambda n: ld(f_t, n, h)), (lambda n: ld(mirrored, n, h))
    if mu == 2:
        edge = (row & 3) == 3
        return (
            lambda n: jnp.where(edge, ld(f_m, n, h), ld(early, 8 + n, h)),
            lambda n: jnp.where(edge, ld(m_m, n, h), ld(mirror_early, 8 + n, h)),
        )
    edge = (row >> 2) + 2 * h == block
    if h == 0:
        here = lambda n: ld(early, n, h)
    else:
        here = lambda n: jnp.where(row >= 4, ld(f_x, n, h), ld(early, n, h))
    return here, (lambda n: jnp.where(edge, ld(m_x, n, h), ld(mirror_early, n, h)))


def updated_momenta(read, force, mirrored):
    diag_force = [force(n) - mirrored(n) for n in range(2)]
    diag_force.append(-(diag_force[0] + diag_force[1]))
    diag = [read(n) + STEP * diag_force[n] for n in range(3)]
    upper = []
    for n in range(3):
        re = force(2 + 2 * n) - mirrored(2 + 2 * n)
        im = force(3 + 2 * n) + mirrored(3 + 2 * n)
        upper.append((read(3 + 2 * n) + STEP * re, read(4 + 2 * n) + STEP * im))
    return diag, upper


def link_step(diag, upper, u):
    b = [STEP * value for value in diag]
    b01, b02, b12 = ((STEP * value[0], STEP * value[1]) for value in upper)
    n01, n02, n12 = (v[0] * v[0] + v[1] * v[1] for v in (b01, b02, b12))
    square_diag = [b[0] * b[0] + n01 + n02, b[1] * b[1] + n01 + n12, b[2] * b[2] + n02 + n12]

    def scaled(v, by):
        return (v[0] * by, v[1] * by)

    square = [
        cadd(scaled(b01, b[0] + b[1]), cmul_conj(b02, b12)),
        cadd(scaled(b02, b[0] + b[2]), cmul(b01, b12)),
        cadd(scaled(b12, b[1] + b[2]), cmul_conj(b02, b01)),
    ]
    c1 = 0.5 * (square_diag[0] + square_diag[1] + square_diag[2])
    triple = cmul_conj(cmul(b01, b12), b02)[0]
    c0 = b[0] * (b[1] * b[2] - n12) - b[1] * n02 - b[2] * n01 + 2.0 * triple
    i0 = c0 * (-1.0 / 60)
    r1 = (1.0 / 3 - c1 * (1.0 / 60), c0 * (-1.0 / 360))
    r2 = 1.0 / 12 - c1 * (1.0 / 360)
    i0, r1, r2 = (r2 * c0) * -0.5, (0.5 - (r2 * c1) * 0.5, i0 * 0.5), (r1[0] * 0.5, r1[1] * 0.5)
    r0, r1, r2 = (1.0 + r2[1] * c0, -(r2[0] * c0)), (1.0 - r2[0] * c1, i0 - r2[1] * c1), r1
    ir1 = (-r1[1], r1[0])
    e = [[None] * 3 for _ in range(3)]
    for i in range(3):
        e[i][i] = cadd(r0, csub(scaled(ir1, b[i]), scaled(r2, square_diag[i])))
    for (i, j), v, s in zip(OFF, (b01, b02, b12), square):
        e[i][j] = csub(cmul(ir1, v), cmul(r2, s))
        e[j][i] = csub(cmul_conj(ir1, v), cmul_conj(r2, s))
    return [[cadd(cadd(cmul(e[i][0], u[0][j]), cmul(e[i][1], u[1][j])), cmul(e[i][2], u[2][j])) for j in range(3)] for i in range(3)]


def input_momentum(ref, mu, h):
    def read(n):
        if n < 3:
            return ld(ref, mu * 18 + 4 * n, h)
        i, j = OFF[(n - 3) // 2]
        return ld(ref, mu * 18 + 9 * ((n - 3) % 2) + 3 * i + j, h)

    return read


def put_matrix(ref, mu, h, value):
    for i in range(3):
        for j in range(3):
            for part in range(2):
                st(ref, mu * 18 + part * 9 + i * 3 + j, h, value[i][j][part])


def put_momenta(ref, base, h, diag, upper):
    for n in range(3):
        st(ref, base + n, h, diag[n])
        st(ref, base + 3 + 2 * n, h, upper[n][0])
        st(ref, base + 4 + 2 * n, h, upper[n][1])


def put_full_momenta(new_p, old_p, at, mu, h, diag, upper):
    for i in range(3):
        st(new_p, at * 18 + 4 * i, h, diag[i])
        st(new_p, at * 18 + 9 + 4 * i, h, ld(old_p, mu * 18 + 9 + 4 * i, h))
    for (i, j), v in zip(OFF, upper):
        st(new_p, at * 18 + 3 * i + j, h, v[0])
        st(new_p, at * 18 + 3 * j + i, h, v[0])
        st(new_p, at * 18 + 9 + 3 * i + j, h, v[1])
        st(new_p, at * 18 + 9 + 3 * j + i, h, -v[1])


def early_update_kernel(phi, u, p, early, mirror_early, new_u, new_p, q3):
    for h in range(2):
        force, mirrored = (lambda n: ld(early, 16 + n, h)), (lambda n: ld(mirror_early, 16 + n, h))
        diag, upper = updated_momenta(input_momentum(p, 3, h), force, mirrored)
        put_momenta(new_p, 0, h, diag, upper)
        link = link_step(diag, upper, matrix(u, 3, h))
        put_matrix(new_u, 0, h, link)
        put_half(q3, h, mat_dag_half(link, project(spinor(phi, h), 3, -1)))


def early_last_kernel(u, p, old_p, early, mirror_early, new_u, new_p):
    for h in range(2):
        force, mirrored = (lambda n: ld(early, 16 + n, h)), (lambda n: ld(mirror_early, 16 + n, h))
        diag, upper = updated_momenta(lambda n: ld(p, 27 + n, h), force, mirrored)
        put_full_momenta(new_p, old_p, 0, 3, h, diag, upper)
        put_matrix(new_u, 0, h, link_step(diag, upper, matrix(u, 3, h)))


def update_kernel(info_ref, phi, u, p, u3, p3, *rest):
    forces = rest[:6]
    new_u, new_p, o_t, o_x, o_m, q0, q2, m_x, m_m = rest[6:]
    info = Info(info_ref)
    place_faces(forces[5], m_x, m_m)
    for h in range(2):
        psi = spinor(phi, h)
        for mu in range(3):
            diag, upper = updated_momenta(
                input_momentum(p, mu, h), *both_forces(mu, h, info.edge_block, *forces, m_x, m_m)
            )
            put_momenta(new_p, mu * 9, h, diag, upper)
            link = link_step(diag, upper, matrix(u, mu, h))
            put_matrix(new_u, mu, h, link)
            back = mat_dag_half(link, project(psi, mu, -1))
            if mu == 1:
                put_half(o_t, h, map_half(lambda a: a * info.sign_behind, back))
            else:
                put_half({0: q0, 2: q2}[mu], h, back)
    new_u[54 * ROWS : 72 * ROWS, :] = u3[...]
    new_p[27 * ROWS : 36 * ROWS, :] = p3[...]
    for k in range(12):
        o_x[k * 4 : k * 4 + 4, :] = q0[k * ROWS + 12 : k * ROWS + 16, :]
        send_rows(o_m, k, q2, k, info, 3)


def last_kernel(info_ref, u, p, old_p, u3, p3, *rest):
    forces = rest[:6]
    out_u, out_p, new_u, new_p, m_x, m_m, sems = rest[6:]
    info = Info(info_ref)
    size = 18 * ROWS
    copies = []

    def send(src, dst, mu):
        copies.append(pltpu.make_async_copy(src, dst.at[mu * size : mu * size + size, :], sems.at[len(copies)]))
        copies[-1].start()

    send(u3, out_u, 3)
    send(p3, out_p, 3)
    place_faces(forces[5], m_x, m_m)
    for mu in range(3):
        for h in range(2):
            diag, upper = updated_momenta(
                lambda n: ld(p, mu * 9 + n, h), *both_forces(mu, h, info.edge_block, *forces, m_x, m_m)
            )
            put_full_momenta(new_p, old_p, mu, mu, h, diag, upper)
            put_matrix(new_u, mu, h, link_step(diag, upper, matrix(u, mu, h)))
        send(new_p.at[mu * size : mu * size + size, :], out_p, mu)
        send(new_u.at[mu * size : mu * size + size, :], out_u, mu)
    for copy in copies:
        copy.wait()


VM = pl.BlockSpec(memory_space=pltpu.VMEM)
HBM = pl.BlockSpec(memory_space=pltpu.HBM)
FULL = ROWS * 12
FACE = 4 * 12


def call(kernel, args, outs, scratch, limit=4, from_hbm=False, to_hbm=False):
    return pl.pallas_call(
        kernel,
        out_shape=[jax.ShapeDtypeStruct((s, 128), F32) if isinstance(s, int) else s for s in outs],
        in_specs=[HBM if from_hbm else VM] * len(args),
        out_specs=[HBM if to_hbm else VM] * len(outs),
        scratch_shapes=[s if not isinstance(s, int) else pltpu.VMEM((s, 128), F32) for s in scratch],
        compiler_params=pltpu.CompilerParams(vmem_limit_bytes=limit << 20),
    )(*args)


def swap(value, axis, far):
    n = lax.axis_size(axis)
    if far:
        pairs = [(i, (i + 1) % n if i % 2 else (i - 1) % n) for i in range(n)]
    else:
        pairs = [(i, i ^ 1) for i in range(n)]
    return lax.ppermute(value, axis, pairs)


def shift(value, axis, by):
    n = lax.axis_size(axis)
    return lax.ppermute(value, axis, [(i, (i + by) % n) for i in range(n)])


def mirror_swap(value):
    n = lax.axis_size("xd")
    return lax.ppermute(value, "xd", [(i, i ^ (n // 2)) for i in range(n)])


def moved(name, value):
    if name == "far_t":
        return swap(value, "ta", True)
    if name == "near_t":
        return swap(value, "ta", False)
    if name == "far_x":
        return swap(value, "xd", True)
    if name == "near_x":
        return swap(value, "xd", False)
    if name == "back_t":
        return shift(value, "ta", -1)
    if name == "back_x":
        return shift(value, "xd", -1)
    if name == "on_t":
        return shift(value, "ta", 1)
    if name == "on_x":
        return shift(value, "xd", 1)
    return mirror_swap(value)


SWAP_ORDER = ("far_t", "mirror", "far_x", "near_x", "near_t")
BACK_ORDER = ("mirror", "back_t", "back_x", "early")
ON_ORDER = ("on_t", "mirror", "on_x")


def exchange(order, **values):
    return {name: moved(name, values[name]) for name in order}


def swap_exchange(t_a, t_b, x_a, x_b, m):
    got = exchange(SWAP_ORDER, near_t=t_a, far_t=t_b, near_x=x_a, far_x=x_b, mirror=m)
    return [got[name] for name in ("near_t", "far_t", "near_x", "far_x", "mirror")]


def all_forces(masks, phi, u, y, w, o_t, o_x, o_m):
    early, sent = call(early_force_kernel, (masks, phi, u, y, *w), [24 * ROWS, 24 * ROWS], [12 * HALO])
    got = exchange(BACK_ORDER, back_t=o_t, back_x=o_x, mirror=o_m, early=sent)
    f_t, f_x, f_m, sent = call(
        late_force_kernel,
        (masks, phi, u, y, *w, got["back_t"], got["back_x"], got["mirror"]),
        [8 * ROWS, 8 * ROWS, 8 * ROWS, 12 * ROWS],
        [],
    )
    late = exchange(("mirror",), mirror=sent)["mirror"]
    return early, got["early"], f_t, f_x, f_m, late


def on_exchange(t, x, m):
    got = exchange(ON_ORDER, on_t=t, on_x=x, mirror=m)
    return [got[name] for name in ("on_t", "on_x", "mirror")]


def per_device(gauge_links, momenta, noise_table, noise_index, partner):
    u = gauge_links.reshape(72 * ROWS, 128)
    p = momenta.reshape(72 * ROWS, 128)
    table = jnp.transpose(noise_table, (0, 2, 1, 3))
    index = noise_index.reshape(ROWS, 128)
    messages = [FULL, FULL, FACE, FACE, 2 * FACE]
    local = [FULL, FULL, FULL]
    halo = [12 * HALO, 12 * HALO]
    spin = 24 * ROWS

    psi, *rest, masks, u = call(
        noise_kernel,
        [pltpu.with_memory_space_constraint(v, pltpu.HBM) for v in (partner, index, table, u)],
        [spin] + messages + local + [jax.ShapeDtypeStruct((INFO_ROWS, 128), jnp.int32), 72 * ROWS],
        [
            pltpu.VMEM((24, 4096), F32),
            pltpu.VMEM((384, 768), jnp.bfloat16),
            FULL,
            FULL,
            pltpu.VMEM((2, 3, 4, 4096), F32),
            pltpu.VMEM((ROWS, 128), jnp.int32),
            pltpu.SMEM((4,), jnp.int32),
            pltpu.SemaphoreType.DMA((4,)),
        ],
        12,
        from_hbm=True,
    )
    t_a, t_b, x_a, x_b, m = swap_exchange(*rest[:5])
    q0, q2, q3 = rest[5:]
    (acc,) = call(rest_kernel, (masks, psi, u, q2, q3, t_a, t_b, m), [spin], [FULL, FULL])
    phi, *rest = call(phi_kernel, (masks, psi, u, acc, q0, x_a, x_b), [spin] + messages + local, halo + [FULL, FULL])
    t_a, t_b, x_a, x_b, m = swap_exchange(*rest[:5])
    q0, q2, q3 = rest[5:]
    acc, w1 = call(rest_w_kernel, (masks, phi, u, q2, q3, t_a, t_b, m), [spin, 3 * FULL], [FULL, FULL])
    y, w0, o_t, o_x, o_m = call(
        response_kernel, (masks, phi, u, acc, q0, x_a, x_b), [spin, FULL, FULL, FACE, FACE], halo + [FULL]
    )
    w = (w0, w1)
    forces = all_forces(masks, phi, u, y, w, o_t, o_x, o_m)
    u3, p3, q3 = call(early_update_kernel, (phi, u, p, *forces[:2]), [18 * ROWS, 9 * ROWS, FULL], [])
    u, p1, o_t, o_x, o_m, q0, q2 = call(
        update_kernel,
        (masks, phi, u, p, u3, p3, *forces),
        [72 * ROWS, 36 * ROWS, FULL, FACE, FACE, FULL, FULL],
        [8 * ROWS, 8 * ROWS],
    )
    b_t, b_x, b_m = on_exchange(o_t, o_x, o_m)
    acc, w1 = call(rest2_kernel, (masks, phi, u, q2, q3, t_a, t_b, m, b_t, b_m), [spin, 3 * FULL], [FULL, FULL])
    y, w0, o_t, o_x, o_m = call(
        response2_kernel, (masks, phi, u, acc, q0, x_a, x_b, b_x), [spin, FULL, FULL, FACE, FACE], halo + [FULL]
    )
    w = (w0, w1)
    forces = all_forces(masks, phi, u, y, w, o_t, o_x, o_m)
    u3, p3 = call(early_last_kernel, (u, p1, p, *forces[:2]), [18 * ROWS, 18 * ROWS], [])
    new_u, new_p = call(
        last_kernel,
        (masks, u, p1, p, u3, p3, *forces),
        [72 * ROWS, 72 * ROWS],
        [54 * ROWS, 54 * ROWS, 8 * ROWS, 8 * ROWS, pltpu.SemaphoreType.DMA((8,))],
        to_hbm=True,
    )
    return new_u.reshape(gauge_links.shape), new_p.reshape(momenta.shape)


def solution(mesh):
    sites = P(None, None, None, None, "xd", "ta", None, None)
    return jax.shard_map(
        per_device,
        mesh=mesh,
        in_specs=(sites, sites, P(), P("xd", "ta", None, None), P("xd")),
        out_specs=(sites, sites),
        check_vma=False,
    )
```
